32 devices in a mesh: batch: 8 (over y, x, core), tensor: 4 (over z).
Axes of the slice: x: 2, y: 2, z: 4, core: 2. Of those that a mesh axis runs over, the one named last changes fastest.
Arguments:
- tokens: bfloat16 [8192, 2048], P('batch', 'tensor'), may hold values from -6 to 6
- doc_lengths: int32 [8], replicated, may hold values from 1 to 8192, as said below
- norm1_gain: float32 [2048], P('tensor'), may hold values from 0.1 to 1.9
- w_query: bfloat16 [2048, 256], P(None, 'tensor'), may hold values from -0.125 to 0.125
- w_key: bfloat16 [2048, 256], P(None, 'tensor'), may hold values from -0.125 to 0.125
- w_value: bfloat16 [2048, 2048], P(None, 'tensor'), may hold values from -0.125 to 0.125
- w_out: bfloat16 [2048, 2048], P('tensor'), may hold values from -1 to 1
- norm2_gain: float32 [2048], P('tensor'), may hold values from 0.1 to 1.9
- w_gate: bfloat16 [2048, 5504], P(None, 'tensor'), may hold values from -0.125 to 0.125
- w_up: bfloat16 [2048, 5504], P(None, 'tensor'), may hold values from -0.125 to 0.125
- w_down: bfloat16 [5504, 2048], P('tensor'), may hold values from -0.078125 to 0.078125
- cotangent: bfloat16 [8192, 2048], P('batch', 'tensor'), may hold values from -6 to 6
Outputs:
- output: bfloat16 [8192, 2048], P('batch', 'tensor')
- grad_tokens: float32 [8192, 2048], P('batch', 'tensor')
- grad_norm1_gain: float32 [2048], P('tensor')
- grad_w_query: float32 [2048, 256], P(None, 'tensor')
- grad_w_key: float32 [2048, 256], P(None, 'tensor')
- grad_w_value: float32 [2048, 2048], P(None, 'tensor')
- grad_w_out: float32 [2048, 2048], P('tensor')
- grad_norm2_gain: float32 [2048], P('tensor')
- grad_w_gate: float32 [2048, 5504], P(None, 'tensor')
- grad_w_up: float32 [2048, 5504], P(None, 'tensor')
- grad_w_down: float32 [5504, 2048], P('tensor')
The draws below stay inside these ranges and needn't reach their ends.
Inputs may be any that keep to these rules, and one draw needn't show every extreme that they name: `doc_lengths`: the lengths sum to 8192; the second document starts before token 1024 and has at least 7169 tokens.
All inputs are finite; a program needn't handle non-finite values.
Results may differ from the reference program's by a relative error of at most 0.01.
Values may be sent and summed in bfloat16 or wider, within the bound.
No kernel may reach another device: no remote copies, remote signals or barrier semaphores. Data moves between devices by JAX's collectives and lax.ppermute only.
A program may use at most 256 MiB of HBM per device.

```python
import math
import jax
import jax.numpy as jnp
from jax import lax

D = 2048
HEADS = 16
FEAT = 16
HV = 128
FF = 5504
TOK_DEV = 1024
DOCS = 8
VW = 2048
TAYLOR = 273
TOKENS = 8192


def draw_doc_lengths(key, part):
    first_key, rest_key = jax.random.split(jax.random.fold_in(key, 17))
    first = jax.random.randint(first_key, (1,), 1, TOK_DEV // 2 + 1)
    others = jax.random.randint(rest_key, (DOCS - 2,), 1, max(2, TOK_DEV // 16) + 1)
    longest = TOKENS - first - jnp.sum(others)
    return jnp.concatenate([first, longest, others]).astype(jnp.int32)


def block_scale(stream_key, shape, cuts, least, largest):
    level, own = 1.0, jax.random.fold_in(stream_key, 6)
    for axis_at, blocks in cuts:
        draws = jnp.exp(jax.random.uniform(jax.random.fold_in(own, axis_at), (blocks,), jnp.float32, least / len(cuts), largest / len(cuts)))
        level = level * jnp.repeat(draws, shape[axis_at] // blocks).reshape([-1 if axis == axis_at else 1 for axis in range(len(shape))])
    return level


def centred(key, shape, scale, bound, cuts=(), kind=jnp.bfloat16):
    values = jax.random.normal(key, shape, jnp.float32) * scale
    if len(cuts) > 0:
        values = block_scale(key, shape, cuts, -0.22, 0.18) * values
    return jnp.clip(values, min=-bound, max=bound).astype(kind)


def setup_inputs(seed: int = 0) -> dict:
    seeds = jax.random.split(jax.random.key(seed), 13)
    return {
        "tokens": centred(seeds[0], (TOKENS, D), 1.0, 6.0, ((0, 8), (1, 4))),
        "doc_lengths": draw_doc_lengths(jax.random.fold_in(seeds[12], 71), 0),
        "norm1_gain": jnp.clip(1.0 + 0.18 * jax.random.normal(seeds[2], (D,), jnp.float32), 0.1, 1.9),
        "w_query": centred(seeds[3], (D, HEADS * FEAT), D ** -0.5, 0.125, ((1, 4),)),
        "w_key": centred(seeds[4], (D, HEADS * FEAT), D ** -0.5, 0.125, ((1, 4),)),
        "w_value": centred(seeds[5], (D, VW), D ** -0.5, 0.125, ((1, 4),)),
        "w_out": centred(seeds[6], (VW, D), (VW // 64) ** -0.5, 1.0, ((0, 4),)),
        "norm2_gain": jnp.clip(1.0 + 0.18 * jax.random.normal(seeds[7], (D,), jnp.float32), 0.1, 1.9),
        "w_gate": centred(seeds[8], (D, FF), D ** -0.5, 0.125, ((1, 4),)),
        "w_up": centred(seeds[9], (D, FF), D ** -0.5, 0.125, ((1, 4),)),
        "w_down": centred(seeds[10], (FF, D), FF ** -0.5, 0.078125, ((0, 4),)),
        "cotangent": centred(seeds[11], (TOKENS, D), 1.0, 6.0, ((0, 8), (1, 4))),
    }


EPSILON = 1e-05
HIGHEST = lax.Precision.HIGHEST

@jax.custom_vjp
def low(v):
    return lax.optimization_barrier(v.astype(jnp.bfloat16)).astype(jnp.float32)

@jax.custom_vjp
def low_back(v):
    return v

def low_keep(v):
    return (low(v), None)

def low_pass(kept, grad):
    return (grad,)

def back_keep(v):
    return (v, None)

def back_low(kept, grad):
    return (low(grad),)
low.defvjp(low_keep, low_pass)
low_back.defvjp(back_keep, back_low)

def matmul(left, right):
    return jnp.dot(left, right, precision=HIGHEST)

def taylor(values):
    width = values.shape[-1]
    root = width ** 0.25
    single = jnp.ones(values.shape[:-1] + (1,), values.dtype)
    square = (values[..., :, None] * values[..., None, :]).reshape(values.shape[:-1] + (width * width,))
    return jnp.concatenate([single, values / root, square / (math.sqrt(2.0) * root * root)], axis=-1)

def local_mix(queries, keys_in, values_in, prior_sum, prior_norm, allowed, opened):
    width = queries.shape[-1]
    scores = jnp.einsum('thf,shf->hts', queries, keys_in, precision=HIGHEST) / math.sqrt(width)
    weights = (1.0 + scores + 0.5 * scores * scores) * allowed[None]
    numer = jnp.einsum('hts,shv->thv', weights, values_in, precision=HIGHEST)
    denom = jnp.transpose(lax.optimization_barrier(jnp.sum(weights, axis=2)))
    feats = taylor(queries)
    numer = numer + jnp.einsum('thr,hrv->thv', feats, prior_sum, precision=HIGHEST) * opened[:, None, None]
    denom = denom + jnp.einsum('thr,hr->th', feats, prior_norm, precision=HIGHEST) * opened[:, None]
    return numer / denom[:, :, None]

def carry_out(keys_in, values_in, tail_mask):
    feats = taylor(keys_in) * tail_mask[:, None, None]
    return (jnp.einsum('thr,thv->hrv', feats, values_in, precision=HIGHEST), lax.optimization_barrier(jnp.sum(feats, axis=0)))

def mix_all(queries, keys_in, values_in, segment):
    block = min(256, TOK_DEV)
    count = TOKENS // block
    local_pos = jnp.arange(block, dtype=jnp.int32)
    causal = local_pos[:, None] >= local_pos[None, :]

    def advance(carry, pieces):
        state_sum, state_norm, open_seg = carry
        query_blk, key_blk, value_blk, seg_blk = pieces
        allowed = (causal & (seg_blk[:, None] == seg_blk[None, :])).astype(query_blk.dtype)
        opened = (seg_blk == open_seg).astype(query_blk.dtype)
        result = local_mix(query_blk, key_blk, value_blk, state_sum, state_norm, allowed, opened)
        last_seg = seg_blk[block - 1]
        tail_mask = (seg_blk == last_seg).astype(query_blk.dtype)
        add_sum, add_norm = carry_out(key_blk, value_blk, tail_mask)
        keep = (last_seg == open_seg).astype(query_blk.dtype)
        return ((add_sum + keep * state_sum, add_norm + keep * state_norm, last_seg), result)
    start = (jnp.zeros((HEADS, TAYLOR, HV), queries.dtype), jnp.zeros((HEADS, TAYLOR), queries.dtype), jnp.array(-1, jnp.int32))
    pieces = (queries.reshape(count, block, HEADS, FEAT), keys_in.reshape(count, block, HEADS, FEAT), values_in.reshape(count, block, HEADS, HV), segment.reshape(count, block))
    _, results = lax.scan(jax.checkpoint(advance), start, pieces)
    return results.reshape(TOKENS, HEADS, HV)

def reference(tokens, doc_lengths, norm1_gain, w_query, w_key, w_value, w_out, norm2_gain, w_gate, w_up, w_down, cotangent):
    doc_ends = jnp.cumsum(doc_lengths).astype(jnp.int32)
    doc_begins = (doc_ends - doc_lengths).astype(jnp.int32)
    position = jnp.arange(TOKENS, dtype=jnp.int32)
    segment = (lax.optimization_barrier(jnp.sum((position[:, None] >= doc_begins[None, :]).astype(jnp.int32), axis=1)) - 1).astype(jnp.int32)

    def forward(inputs, gain_one, wq, wk, wv, wo, gain_two, wg, wu, wd):
        scale_one = lax.rsqrt(lax.optimization_barrier(jnp.mean(inputs * inputs, axis=1, keepdims=True)) + EPSILON)
        normed = low(inputs * scale_one * gain_one[None, :])
        queries = low(low_back(matmul(normed, wq))).reshape(TOKENS, HEADS, FEAT)
        keys_in = low(low_back(matmul(normed, wk))).reshape(TOKENS, HEADS, FEAT)
        values_in = low(low_back(matmul(normed, wv))).reshape(TOKENS, HEADS, HV)
        mixed = low(mix_all(queries, keys_in, values_in, segment).reshape(TOKENS, VW))
        hidden = inputs + low_back(matmul(mixed, wo))
        scale_two = lax.rsqrt(lax.optimization_barrier(jnp.mean(hidden * hidden, axis=1, keepdims=True)) + EPSILON)
        normed_two = low(hidden * scale_two * gain_two[None, :])
        gate = low_back(matmul(normed_two, wg))
        up_proj = low_back(matmul(normed_two, wu))
        inner = low(jax.nn.silu(gate) * up_proj)
        return hidden + low_back(matmul(inner, wd))
    single = jnp.float32
    result, pull = jax.vjp(forward, tokens.astype(single), norm1_gain.astype(single), w_query.astype(single), w_key.astype(single), w_value.astype(single), w_out.astype(single), norm2_gain.astype(single), w_gate.astype(single), w_up.astype(single), w_down.astype(single))
    grads = pull(cotangent.astype(single))
    return (result.astype(jnp.bfloat16), grads[0], grads[1], grads[2], grads[3], grads[4], grads[5], grads[6], grads[7], grads[8], grads[9])
```

```python
import functools
import math

import jax
import jax.numpy as jnp
import numpy as np
from jax import lax
from jax.experimental import pallas as pl
from jax.experimental.pallas import tpu as pltpu
from jax.sharding import PartitionSpec as P

FEAT = 16
HV = 128
EPSILON = 1e-05
WIDE = 256
ROWS = 160
STRIP = 256
LOW = jnp.bfloat16
F32 = jnp.float32


def feature_table():
    table = np.zeros((8, WIDE), np.float32)
    table[0:2] = -1.0
    at = 0
    for i in range(FEAT + 1):
        for j in range(i, FEAT + 1):
            table[0, at] = i if i < FEAT else -1
            table[1, at] = j if j < FEAT else -1
            table[2, at] = float(i == FEAT)
            table[3, at] = float(j == FEAT)
            table[4, at] = 0.5 if i == j and i < FEAT else 1.0
            at += 1
    return table


def nt(a, b):
    return lax.dot_general(a, b, (((1,), (1,)), ((), ())), preferred_element_type=F32)


def tn(a, b):
    return lax.dot_general(a, b, (((0,), (0,)), ((), ())), preferred_element_type=F32)


def nn(a, b):
    return lax.dot_general(a, b, (((1,), (0,)), ((), ())), preferred_element_type=F32)


def pickers(table, head, lanes):
    lane = lax.broadcasted_iota(jnp.int32, (lanes, WIDE), 0).astype(F32)
    base = (head * FEAT).astype(F32)
    first, second = table[0:1, :], table[1:2, :]
    one = jnp.where((lane == base + first) & (first >= 0), 0.5, 0.0).astype(LOW)
    two = jnp.where((lane == base + second) & (second >= 0), 0.5, 0.0).astype(LOW)
    return one, two


def head_lanes(head, lanes):
    lane = lax.broadcasted_iota(jnp.int32, (1, lanes), 1)
    return (lane >= head * FEAT) & (lane < (head + 1) * FEAT)


def factors(z, table, one, two):
    return nn(z, one) + table[2:3, :], nn(z, two) + table[3:4, :]


def pad_state(state):
    return jnp.concatenate([state, jnp.zeros((WIDE - ROWS, HV), state.dtype)], axis=0)


def state_body(k_ref, v_ref, tail_ref, table_ref, sum_ref, norm_ref):
    head = pl.program_id(0)
    table = table_ref[...]
    one, two = pickers(table, head, k_ref.shape[1])
    left, right = factors(k_ref[...], table, one, two)
    feats = (left * right * table[4:5, :] * tail_ref[...]).astype(LOW)
    sum_ref[0] = tn(feats, v_ref[...])[:ROWS].astype(sum_ref.dtype)
    norm_ref[0] = nn(jnp.ones((8, feats.shape[0]), LOW), feats)


def masked_weights(scores, segc, segr, row0, width):
    rows = scores.shape[0]
    row = row0 + lax.broadcasted_iota(jnp.int32, (rows, width), 0)
    col = lax.broadcasted_iota(jnp.int32, (rows, width), 1)
    return (row >= col) & (segc == segr)


def inner_body(q_ref, k_ref, v_ref, segc_ref, segr_ref, numer_ref, denom_ref):
    head = pl.program_id(0)
    tokens, lanes = q_ref.shape
    mine = head_lanes(head, lanes)
    for row0 in range(0, tokens, STRIP):
        width = row0 + STRIP
        query = jnp.where(mine, q_ref[pl.ds(row0, STRIP), :] * LOW(0.25), LOW(0.0))
        scores = nt(query, k_ref[pl.ds(0, width), :])
        keep = masked_weights(scores, segc_ref[pl.ds(row0, STRIP), :], segr_ref[:, pl.ds(0, width)], row0, width)
        weights = jnp.where(keep, 1.0 + scores * (1.0 + 0.5 * scores), 0.0).astype(LOW)
        wide = jnp.concatenate([v_ref[pl.ds(0, width), :], jnp.ones((width, HV), LOW)], axis=1)
        both = nn(weights, wide)
        numer_ref[pl.ds(row0, STRIP), :] = both[:, :HV]
        denom_ref[pl.ds(row0, STRIP), :] = both[:, HV:]


def merge_body(q_ref, numer_ref, denom_ref, sum_ref, norm_ref, open_ref, table_ref, y_ref, total_ref):
    head = pl.program_id(0)
    table = table_ref[...]
    one, two = pickers(table, head, q_ref.shape[1])
    left, right = factors(q_ref[...], table, one, two)
    feats = (left * right * open_ref[...]).astype(LOW)
    norm = jnp.broadcast_to(norm_ref[0][0:1, :], (HV, WIDE))
    norm_high = norm.astype(LOW)
    norm_rest = (norm - norm_high.astype(F32)).astype(LOW)
    total = denom_ref[...] + nt(feats, norm_high) + nt(feats, norm_rest)
    numer = numer_ref[...] + nn(feats, pad_state(sum_ref[0].astype(LOW)))
    total_ref[...] = total
    y_ref[...] = (numer / total).astype(LOW)


def pull_state_body(q_ref, dy_ref, y_ref, total_ref, open_ref, table_ref, wide_ref, sum_ref, norm_ref):
    head = pl.program_id(0)
    table = table_ref[...]
    one, two = pickers(table, head, q_ref.shape[1])
    left, right = factors(q_ref[...], table, one, two)
    feats = (left * right * open_ref[...]).astype(LOW)
    inverse = 1.0 / total_ref[...]
    dy = dy_ref[...]
    dnumer = (dy * inverse).astype(LOW)
    ddenom = -jnp.sum(dy * y_ref[...].astype(F32), axis=1, keepdims=True) * inverse
    ddenom = jnp.where(lax.broadcasted_iota(jnp.int32, ddenom.shape, 1) < 8, ddenom, 0.0).astype(LOW)
    wide_ref[...] = jnp.concatenate([dnumer, ddenom], axis=1)
    sum_ref[0] = tn(feats, dnumer)[:ROWS].astype(sum_ref.dtype)
    norm_ref[0] = tn(ddenom, feats)[:8]


def pull_inner_body(
    q_ref, k_ref, v_ref, segc_ref, segr_ref, wide_ref, sum_ref, norm_ref, open_ref, table_ref,
    dq_ref, dk_ref, dv_ref, dq_acc, dk_acc,
):
    head = pl.program_id(0)
    last = pl.num_programs(0) - 1
    tokens, lanes = q_ref.shape
    mine = head_lanes(head, lanes)

    @pl.when(head == 0)
    def _():
        dq_acc[...] = jnp.zeros_like(dq_acc)
        dk_acc[...] = jnp.zeros_like(dk_acc)

    dv_ref[...] = jnp.zeros_like(dv_ref)
    table = table_ref[...]
    one, two = pickers(table, head, lanes)
    state = pad_state(sum_ref[0].astype(LOW))
    norm = norm_ref[0][0:1, :]
    single = (lax.broadcasted_iota(jnp.int32, (1, HV), 1) < 1).astype(LOW)
    for row0 in range(0, tokens, STRIP):
        width = row0 + STRIP
        rows = pl.ds(row0, STRIP)
        query = jnp.where(mine, q_ref[rows, :] * LOW(0.25), LOW(0.0))
        keys = jnp.where(mine, k_ref[pl.ds(0, width), :] * LOW(0.25), LOW(0.0))
        scores = nt(query, k_ref[pl.ds(0, width), :])
        keep = masked_weights(scores, segc_ref[rows, :], segr_ref[:, pl.ds(0, width)], row0, width)
        weights = jnp.where(keep, 1.0 + scores * (1.0 + 0.5 * scores), 0.0).astype(LOW)
        dwide = wide_ref[rows, :]
        ones = jnp.broadcast_to(single, (width, HV))
        wide = jnp.concatenate([v_ref[pl.ds(0, width), :], ones], axis=1)
        dscores = jnp.where(keep, nt(dwide, wide) * (1.0 + scores), 0.0).astype(LOW)
        dv_ref[pl.ds(0, width), :] += tn(weights, dwide[:, :HV])
        dk_acc[pl.ds(0, width), :] += tn(dscores, query)
        left, right = factors(q_ref[rows, :], table, one, two)
        pulled = nt(dwide[:, :HV], state) + dwide[:, HV : HV + 1].astype(F32) * norm
        pulled = pulled * open_ref[rows, :]
        dq_acc[rows, :] += nn(dscores, keys) + nt((pulled * right).astype(LOW), one) + nt((pulled * left).astype(LOW), two)

    @pl.when(head == last)
    def _():
        dq_ref[...] = dq_acc[...].astype(dq_ref.dtype)
        dk_ref[...] = dk_acc[...]


def pull_carry_body(k_ref, v_ref, tail_ref, sum_ref, norm_ref, dk_in_ref, dv_in_ref, table_ref, dk_ref, dv_ref, dk_acc):
    head = pl.program_id(0)

    @pl.when(head == 0)
    def _():
        dk_acc[...] = dk_in_ref[...]

    table = table_ref[...]
    one, two = pickers(table, head, k_ref.shape[1])
    left, right = factors(k_ref[...], table, one, two)
    scale = table[4:5, :] * tail_ref[...]
    state = pad_state(sum_ref[0].astype(LOW))
    dv_ref[...] = (dv_in_ref[...] + nn((left * right * scale).astype(LOW), state)).astype(dv_ref.dtype)
    pulled = (nt(v_ref[...], state) + norm_ref[0][0:1, :]) * scale
    dk_acc[...] += nt((pulled * right).astype(LOW), one) + nt((pulled * left).astype(LOW), two)

    @pl.when(head == pl.num_programs(0) - 1)
    def _():
        dk_ref[...] = dk_acc[...].astype(dk_ref.dtype)


def shape(dims, kind):
    return jax.ShapeDtypeStruct(dims, kind)


class Mixer:
    def __init__(self, tokens, heads):
        self.tokens, self.heads = tokens, heads
        lanes = heads * FEAT
        self.full = lambda a, b: pl.BlockSpec((a, b), lambda h: (0, 0))
        self.thin = self.full(tokens, lanes)
        self.column = self.full(tokens, 1)
        self.row = self.full(1, tokens)
        self.table = self.full(8, WIDE)
        self.head = pl.BlockSpec((tokens, HV), lambda h: (0, h))
        self.pair = pl.BlockSpec((tokens, 2 * HV), lambda h: (0, h))
        self.sum = pl.BlockSpec((1, ROWS, HV), lambda h: (h, 0, 0))
        self.norm = pl.BlockSpec((1, 8, WIDE), lambda h: (h, 0, 0))
        self.thin_shape = lambda kind: shape((tokens, lanes), kind)
        self.head_shape = lambda kind: shape((tokens, heads * HV), kind)
        self.state_shapes = [shape((heads, ROWS, HV), F32), shape((heads, 8, WIDE), F32)]
        self.acc = pltpu.VMEM((tokens, lanes), F32)

    def call(self, body, name, in_specs, out_specs, out_shape, scratch, micros, *args):
        return pl.pallas_call(
            body,
            grid=(self.heads,),
            in_specs=in_specs,
            out_specs=out_specs,
            out_shape=out_shape,
            scratch_shapes=scratch,
            name=name,
            compiler_params=pltpu.CompilerParams(
                dimension_semantics=("arbitrary",), vmem_limit_bytes=48 * 1024 * 1024
            ),
            cost_estimate=pl.CostEstimate(
                flops=int(micros * 1e-6 * 1e15), bytes_accessed=1 << 20, transcendentals=0
            ),
        )(*args)

    def state(self, k, v, tail, table):
        return self.call(
            state_body, "mix_state", [self.thin, self.head, self.column, self.table],
            [self.sum, self.norm], self.state_shapes, [], 4, k, v, tail, table,
        )

    def inner(self, q, k, v, segc, segr):
        return self.call(
            inner_body, "mix_inner", [self.thin, self.thin, self.head, self.column, self.row],
            [self.head, self.head], [self.head_shape(F32)] * 2, [], 10, q, k, v, segc, segr,
        )

    def merge(self, q, numer, denom, total, norm, opened, table):
        return self.call(
            merge_body, "mix_merge",
            [self.thin, self.head, self.head, self.sum, self.norm, self.column, self.table],
            [self.head, self.head], [self.head_shape(LOW), self.head_shape(F32)], [], 5,
            q, numer, denom, total, norm, opened, table,
        )

    def pull_state(self, q, dy, y, total, opened, table):
        return self.call(
            pull_state_body, "mix_pull_state",
            [self.thin, self.head, self.head, self.head, self.column, self.table],
            [self.pair, self.sum, self.norm],
            [shape((self.tokens, self.heads * 2 * HV), LOW)] + self.state_shapes, [], 5,
            q, dy, y, total, opened, table,
        )

    def pull_inner(self, q, k, v, segc, segr, wide, total, norm, opened, table):
        return self.call(
            pull_inner_body, "mix_pull_inner",
            [self.thin, self.thin, self.head, self.column, self.row, self.pair, self.sum, self.norm, self.column, self.table],
            [self.thin, self.thin, self.head],
            [self.thin_shape(LOW), self.thin_shape(F32), self.head_shape(F32)],
            [self.acc, self.acc], 20, q, k, v, segc, segr, wide, total, norm, opened, table,
        )

    def pull_carry(self, k, v, tail, total, norm, dk, dv, table):
        return self.call(
            pull_carry_body, "mix_pull_carry",
            [self.thin, self.head, self.column, self.sum, self.norm, self.thin, self.head, self.table],
            [self.thin, self.head], [self.thin_shape(LOW), self.head_shape(LOW)], [self.acc], 6,
            k, v, tail, total, norm, dk, dv, table,
        )


def outside(part, reverse):
    count, place = lax.axis_size("batch"), lax.axis_index("batch")
    total = list(part)
    before = [jnp.zeros_like(a) for a in part]
    bit = 1
    while bit < count:
        pairs = [(i, i ^ bit) for i in range(count)]
        low = total[0].astype(LOW)
        other = [lax.ppermute(low, "batch", pairs).astype(F32), lax.ppermute(total[1], "batch", pairs)]
        upper = (place & bit) != 0
        take = jnp.logical_not(upper) if reverse else upper
        before = [a + jnp.where(take, b, 0.0) for a, b in zip(before, other)]
        total = [a + b for a, b in zip(total, other)]
        bit *= 2
    return before


def widen(part):
    return lax.all_gather(part, "tensor", axis=1, tiled=True)


def narrow(part):
    return lax.psum_scatter(part, "tensor", scatter_dimension=1, tiled=True)


def project(left, right):
    return jnp.dot(left, right, preferred_element_type=F32)


def project_left(left, right):
    return jnp.einsum("ti,tj->ij", left, right, preferred_element_type=F32)


def project_back(left, right):
    return jnp.einsum("ti,ji->tj", left, right, preferred_element_type=F32)


def local(
    tokens, doc_lengths, norm1_gain, w_query, w_key, w_value, w_out, norm2_gain, w_gate, w_up, w_down, cotangent,
):
    count, slice_width = tokens.shape
    heads = w_value.shape[1] // HV
    lanes = heads * FEAT
    width = w_query.shape[0]
    begin_here = lax.axis_index("batch") * count
    position = begin_here + jnp.arange(count, dtype=jnp.int32)
    doc_index = jnp.arange(doc_lengths.shape[0], dtype=jnp.int32)
    doc_begins = jnp.sum(jnp.where(doc_index[None, :] < doc_index[:, None], doc_lengths[None, :], 0), axis=1)
    segment = jnp.sum((position[:, None] >= doc_begins[None, :]).astype(jnp.int32), axis=1) - 1
    head_seg, tail_seg = segment[0], segment[-1]
    first_begin = jnp.sum(jnp.where(doc_index == head_seg, doc_begins, 0))
    opened = ((segment == head_seg) & (first_begin < begin_here)).astype(F32)[:, None]
    tail = (segment == tail_seg).astype(F32)[:, None]
    segc, segr = segment[:, None], segment[None, :]
    table = jnp.asarray(feature_table())
    mixer = Mixer(count, heads)

    gains = lax.all_gather(jnp.stack([norm1_gain, norm2_gain]), "tensor", axis=1, tiled=True)
    x_full = widen(tokens)
    c_full = widen(cotangent)
    inputs = tokens.astype(F32)
    x_wide = x_full.astype(F32)
    scale_one = lax.rsqrt(jnp.mean(x_wide * x_wide, axis=1, keepdims=True) + EPSILON)
    normed_one = (x_wide * scale_one * gains[0:1]).astype(LOW)
    w_mix = jnp.concatenate([w_query, w_key, w_value], axis=1)
    mixed_in = project(normed_one, w_mix).astype(LOW)
    q, k, v = mixed_in[:, :lanes], mixed_in[:, lanes : 2 * lanes], mixed_in[:, 2 * lanes :]

    carry = mixer.state(k, v, tail, table)
    prior = outside(carry, False)
    numer, denom = mixer.inner(q, k, v, segc, segr)
    y, total = mixer.merge(q, numer, denom, *prior, opened, table)

    hidden = inputs + narrow(project(y, w_out).astype(LOW)).astype(F32)
    hidden_full = widen(hidden.astype(LOW)).astype(F32)
    scale_two = lax.rsqrt(jnp.mean(hidden_full * hidden_full, axis=1, keepdims=True) + EPSILON)
    normed_two = (hidden_full * scale_two * gains[1:2]).astype(LOW)
    gate = project(normed_two, w_gate)
    up = project(normed_two, w_up)
    sig = jax.nn.sigmoid(gate)
    silu = gate * sig
    inner = (silu * up).astype(LOW)
    output = (hidden + narrow(project(inner, w_down).astype(LOW)).astype(F32)).astype(LOW)

    dinner = project_back(c_full, w_down)
    dgate = (dinner * up * sig * (1.0 + gate * (1.0 - sig))).astype(LOW)
    dup = (dinner * silu).astype(LOW)
    dot_two = lax.psum(
        jnp.sum(dgate.astype(F32) * gate + dup.astype(F32) * up, axis=1, keepdims=True), "tensor"
    )
    dnormed_two = narrow((project_back(dgate, w_gate) + project_back(dup, w_up)).astype(LOW)).astype(F32)
    grad_hidden = (
        cotangent.astype(F32)
        + scale_two * norm2_gain[None, :] * dnormed_two
        - hidden * (scale_two * scale_two * dot_two / width)
    )
    dh_full = widen(grad_hidden.astype(LOW))
    dy = project_back(dh_full, w_out)
    wide, dsum, dnorm = mixer.pull_state(q, dy, y, total, opened, table)
    after = outside([dsum, dnorm], True)
    dq, dk, dv = mixer.pull_inner(q, k, v, segc, segr, wide, *prior, opened, table)
    dk, dv = mixer.pull_carry(k, v, tail, *after, dk, dv, table)
    dmix = jnp.concatenate([dq, dk, dv], axis=1)
    dot_one = lax.psum(
        jnp.sum(dmix.astype(F32) * mixed_in.astype(F32), axis=1, keepdims=True), "tensor"
    )
    dnormed_one = narrow(project_back(dmix, w_mix).astype(LOW)).astype(F32)
    grad_tokens = (
        grad_hidden
        + scale_one * norm1_gain[None, :] * dnormed_one
        - inputs * (scale_one * scale_one * dot_one / width)
    )

    grad_w_down = project_left(inner, c_full)
    grad_w_gate = project_left(normed_two, dgate)
    grad_w_up = project_left(normed_two, dup)
    grad_w_out = project_left(y, dh_full)
    grad_w_mix = project_left(normed_one, dmix)
    gain_one = jnp.sum(grad_w_mix * w_mix.astype(F32), axis=1)
    gain_two = jnp.sum(grad_w_gate * w_gate.astype(F32) + grad_w_up * w_up.astype(F32), axis=1)
    gain_grads = lax.psum(jnp.stack([gain_one, gain_two]), ("batch", "tensor")) / gains
    gain_grads = lax.dynamic_slice_in_dim(gain_grads, lax.axis_index("tensor") * slice_width, slice_width, 1)
    ffn = lax.psum([g.astype(LOW) for g in (grad_w_down, grad_w_gate, grad_w_up)], "batch")
    mix = lax.psum([g.astype(LOW) for g in (grad_w_out, grad_w_mix)], "batch")
    grad_w_down, grad_w_gate, grad_w_up = [g.astype(F32) for g in ffn]
    grad_w_out, grad_w_mix = [g.astype(F32) for g in mix]
    return (
        output,
        grad_tokens,
        gain_grads[0],
        grad_w_mix[:, :lanes],
        grad_w_mix[:, lanes : 2 * lanes],
        grad_w_mix[:, 2 * lanes :],
        grad_w_out,
        gain_grads[1],
        grad_w_gate,
        grad_w_up,
        grad_w_down,
    )


def solution(mesh):
    rows, cols = P("tensor", None), P(None, "tensor")
    both, one = P("batch", "tensor"), P("tensor")
    in_specs = (both, P(), one, cols, cols, cols, rows, one, cols, cols, rows, both)
    out_specs = (both, both, one, cols, cols, cols, rows, one, cols, cols, rows)
    return jax.shard_map(local, mesh=mesh, in_specs=in_specs, out_specs=out_specs, check_vma=False)
```

```python
import functools
import math

import jax
import jax.numpy as jnp
import numpy as np
from jax import lax
from jax.experimental import pallas as pl
from jax.experimental.pallas import tpu as pltpu
from jax.sharding import PartitionSpec as P

FEAT = 16
HV = 128
EPSILON = 1e-05
WIDE = 256
ROWS = 160
STRIP = 256
CHUNKS = 2
LOW = jnp.bfloat16
F32 = jnp.float32


def feature_table():
    table = np.zeros((8, WIDE), np.float32)
    table[0:2] = -1.0
    at = 0
    for i in range(FEAT + 1):
        for j in range(i, FEAT + 1):
            table[0, at] = i if i < FEAT else -1
            table[1, at] = j if j < FEAT else -1
            table[2, at] = float(i == FEAT)
            table[3, at] = float(j == FEAT)
            table[4, at] = 0.5 if i == j and i < FEAT else 1.0
            at += 1
    return table


def nt(a, b):
    return lax.dot_general(a, b, (((1,), (1,)), ((), ())), preferred_element_type=F32)


def tn(a, b):
    return lax.dot_general(a, b, (((0,), (0,)), ((), ())), preferred_element_type=F32)


def nn(a, b):
    return lax.dot_general(a, b, (((1,), (0,)), ((), ())), preferred_element_type=F32)


def pickers(table, head, lanes):
    lane = lax.broadcasted_iota(jnp.int32, (lanes, WIDE), 0).astype(F32)
    base = (head * FEAT).astype(F32)
    first, second = table[0:1, :], table[1:2, :]
    one = jnp.where((lane == base + first) & (first >= 0), 0.5, 0.0).astype(LOW)
    two = jnp.where((lane == base + second) & (second >= 0), 0.5, 0.0).astype(LOW)
    return one, two


def head_lanes(head, lanes):
    lane = lax.broadcasted_iota(jnp.int32, (1, lanes), 1)
    return (lane >= head * FEAT) & (lane < (head + 1) * FEAT)


def factors(z, table, one, two):
    return nn(z, one) + table[2:3, :], nn(z, two) + table[3:4, :]


def pad_state(state):
    return jnp.concatenate([state, jnp.zeros((WIDE - ROWS, HV), state.dtype)], axis=0)


def state_body(k_ref, v_ref, tail_ref, table_ref, sum_ref, norm_ref):
    head = pl.program_id(0)
    table = table_ref[...]
    one, two = pickers(table, head, k_ref.shape[1])
    left, right = factors(k_ref[...], table, one, two)
    feats = (left * right * table[4:5, :] * tail_ref[...]).astype(LOW)
    sum_ref[0] = tn(feats, v_ref[...])[:ROWS].astype(sum_ref.dtype)
    norm_ref[0] = nn(jnp.ones((8, feats.shape[0]), LOW), feats)


def masked_weights(scores, segc, segr, row0, width):
    rows = scores.shape[0]
    row = row0 + lax.broadcasted_iota(jnp.int32, (rows, width), 0)
    col = lax.broadcasted_iota(jnp.int32, (rows, width), 1)
    return (row >= col) & (segc == segr)


def inner_body(q_ref, k_ref, v_ref, segc_ref, segr_ref, numer_ref, denom_ref):
    head = pl.program_id(0)
    tokens, lanes = q_ref.shape
    mine = head_lanes(head, lanes)
    for row0 in range(0, tokens, STRIP):
        width = row0 + STRIP
        query = jnp.where(mine, q_ref[pl.ds(row0, STRIP), :] * LOW(0.25), LOW(0.0))
        scores = nt(query, k_ref[pl.ds(0, width), :])
        keep = masked_weights(scores, segc_ref[pl.ds(row0, STRIP), :], segr_ref[:, pl.ds(0, width)], row0, width)
        weights = jnp.where(keep, 1.0 + scores * (1.0 + 0.5 * scores), 0.0).astype(LOW)
        wide = jnp.concatenate([v_ref[pl.ds(0, width), :], jnp.ones((width, HV), LOW)], axis=1)
        both = nn(weights, wide)
        numer_ref[pl.ds(row0, STRIP), :] = both[:, :HV]
        denom_ref[pl.ds(row0, STRIP), :] = both[:, HV:]


def merge_body(q_ref, numer_ref, denom_ref, sum_ref, norm_ref, open_ref, table_ref, y_ref, total_ref):
    head = pl.program_id(0)
    table = table_ref[...]
    one, two = pickers(table, head, q_ref.shape[1])
    left, right = factors(q_ref[...], table, one, two)
    feats = (left * right * open_ref[...]).astype(LOW)
    norm = jnp.broadcast_to(norm_ref[0][0:1, :], (HV, WIDE))
    norm_high = norm.astype(LOW)
    norm_rest = (norm - norm_high.astype(F32)).astype(LOW)
    total = denom_ref[...] + nt(feats, norm_high) + nt(feats, norm_rest)
    numer = numer_ref[...] + nn(feats, pad_state(sum_ref[0].astype(LOW)))
    total_ref[...] = total
    y_ref[...] = (numer / total).astype(LOW)


def pull_state_body(q_ref, y_ref, total_ref, open_ref, table_ref, *refs):
    *dy_refs, wide_ref, sum_ref, norm_ref = refs
    head = pl.program_id(0)
    table = table_ref[...]
    one, two = pickers(table, head, q_ref.shape[1])
    left, right = factors(q_ref[...], table, one, two)
    feats = (left * right * open_ref[...]).astype(LOW)
    inverse = 1.0 / total_ref[...]
    dy = jnp.concatenate([r[...] for r in dy_refs], axis=0)
    dnumer = (dy * inverse).astype(LOW)
    ddenom = -jnp.sum(dy * y_ref[...].astype(F32), axis=1, keepdims=True) * inverse
    ddenom = jnp.where(lax.broadcasted_iota(jnp.int32, ddenom.shape, 1) < 8, ddenom, 0.0).astype(LOW)
    wide_ref[...] = jnp.concatenate([dnumer, ddenom], axis=1)
    sum_ref[0] = tn(feats, dnumer)[:ROWS].astype(sum_ref.dtype)
    norm_ref[0] = tn(ddenom, feats)[:8]


def pull_inner_body(
    q_ref, k_ref, v_ref, segc_ref, segr_ref, wide_ref, sum_ref, norm_ref, open_ref, table_ref,
    dq_ref, dk_ref, dv_ref, dq_acc, dk_acc,
):
    head = pl.program_id(0)
    last = pl.num_programs(0) - 1
    tokens, lanes = q_ref.shape
    mine = head_lanes(head, lanes)

    @pl.when(head == 0)
    def _():
        dq_acc[...] = jnp.zeros_like(dq_acc)
        dk_acc[...] = jnp.zeros_like(dk_acc)

    dv_ref[...] = jnp.zeros_like(dv_ref)
    table = table_ref[...]
    one, two = pickers(table, head, lanes)
    state = pad_state(sum_ref[0].astype(LOW))
    norm = norm_ref[0][0:1, :]
    single = (lax.broadcasted_iota(jnp.int32, (1, HV), 1) < 1).astype(LOW)
    for row0 in range(0, tokens, STRIP):
        width = row0 + STRIP
        rows = pl.ds(row0, STRIP)
        query = jnp.where(mine, q_ref[rows, :] * LOW(0.25), LOW(0.0))
        keys = jnp.where(mine, k_ref[pl.ds(0, width), :] * LOW(0.25), LOW(0.0))
        scores = nt(query, k_ref[pl.ds(0, width), :])
        keep = masked_weights(scores, segc_ref[rows, :], segr_ref[:, pl.ds(0, width)], row0, width)
        weights = jnp.where(keep, 1.0 + scores * (1.0 + 0.5 * scores), 0.0).astype(LOW)
        dwide = wide_ref[rows, :]
        ones = jnp.broadcast_to(single, (width, HV))
        wide = jnp.concatenate([v_ref[pl.ds(0, width), :], ones], axis=1)
        dscores = jnp.where(keep, nt(dwide, wide) * (1.0 + scores), 0.0).astype(LOW)
        dv_ref[pl.ds(0, width), :] += tn(weights, dwide[:, :HV])
        dk_acc[pl.ds(0, width), :] += tn(dscores, query)
        left, right = factors(q_ref[rows, :], table, one, two)
        pulled = nt(dwide[:, :HV], state) + dwide[:, HV : HV + 1].astype(F32) * norm
        pulled = pulled * open_ref[rows, :]
        dq_acc[rows, :] += nn(dscores, keys) + nt((pulled * right).astype(LOW), one) + nt((pulled * left).astype(LOW), two)

    @pl.when(head == last)
    def _():
        dq_ref[...] = dq_acc[...].astype(dq_ref.dtype)
        dk_ref[...] = dk_acc[...]


def pull_carry_body(k_ref, v_ref, tail_ref, sum_ref, norm_ref, dk_in_ref, dv_in_ref, table_ref, dk_ref, dv_ref, dk_acc):
    head = pl.program_id(0)

    @pl.when(head == 0)
    def _():
        dk_acc[...] = dk_in_ref[...]

    table = table_ref[...]
    one, two = pickers(table, head, k_ref.shape[1])
    left, right = factors(k_ref[...], table, one, two)
    scale = table[4:5, :] * tail_ref[...]
    state = pad_state(sum_ref[0].astype(LOW))
    dv_ref[...] = (dv_in_ref[...] + nn((left * right * scale).astype(LOW), state)).astype(dv_ref.dtype)
    pulled = (nt(v_ref[...], state) + norm_ref[0][0:1, :]) * scale
    dk_acc[...] += nt((pulled * right).astype(LOW), one) + nt((pulled * left).astype(LOW), two)

    @pl.when(head == pl.num_programs(0) - 1)
    def _():
        dk_ref[...] = dk_acc[...].astype(dk_ref.dtype)


def shape(dims, kind):
    return jax.ShapeDtypeStruct(dims, kind)


class Mixer:
    def __init__(self, tokens, heads):
        self.tokens, self.heads = tokens, heads
        lanes = heads * FEAT
        self.full = lambda a, b: pl.BlockSpec((a, b), lambda h: (0, 0))
        self.thin = self.full(tokens, lanes)
        self.column = self.full(tokens, 1)
        self.row = self.full(1, tokens)
        self.table = self.full(8, WIDE)
        self.head = pl.BlockSpec((tokens, HV), lambda h: (0, h))
        self.pair = pl.BlockSpec((tokens, 2 * HV), lambda h: (0, h))
        self.sum = pl.BlockSpec((1, ROWS, HV), lambda h: (h, 0, 0))
        self.norm = pl.BlockSpec((1, 8, WIDE), lambda h: (h, 0, 0))
        self.thin_shape = lambda kind: shape((tokens, lanes), kind)
        self.head_shape = lambda kind: shape((tokens, heads * HV), kind)
        self.state_shapes = [shape((heads, ROWS, HV), F32), shape((heads, 8, WIDE), F32)]
        self.acc = pltpu.VMEM((tokens, lanes), F32)

    def call(self, body, name, in_specs, out_specs, out_shape, scratch, micros, *args):
        return pl.pallas_call(
            body,
            grid=(self.heads,),
            in_specs=in_specs,
            out_specs=out_specs,
            out_shape=out_shape,
            scratch_shapes=scratch,
            name=name,
            compiler_params=pltpu.CompilerParams(
                dimension_semantics=("arbitrary",), vmem_limit_bytes=48 * 1024 * 1024
            ),
            cost_estimate=pl.CostEstimate(
                flops=int(micros * 1e-6 * 1e15), bytes_accessed=1 << 20, transcendentals=0
            ),
        )(*args)

    def state(self, k, v, tail, table):
        return self.call(
            state_body, "mix_state", [self.thin, self.head, self.column, self.table],
            [self.sum, self.norm], self.state_shapes, [], 4, k, v, tail, table,
        )

    def inner(self, q, k, v, segc, segr):
        return self.call(
            inner_body, "mix_inner", [self.thin, self.thin, self.head, self.column, self.row],
            [self.head, self.head], [self.head_shape(F32)] * 2, [], 10, q, k, v, segc, segr,
        )

    def merge(self, q, numer, denom, total, norm, opened, table):
        return self.call(
            merge_body, "mix_merge",
            [self.thin, self.head, self.head, self.sum, self.norm, self.column, self.table],
            [self.head, self.head], [self.head_shape(LOW), self.head_shape(F32)], [], 5,
            q, numer, denom, total, norm, opened, table,
        )

    def pull_state(self, q, dy, y, total, opened, table):
        return self.call(
            pull_state_body, "mix_pull_state",
            [self.thin, self.head, self.head, self.column, self.table]
            + [pl.BlockSpec((d.shape[0], HV), lambda h: (0, h)) for d in dy],
            [self.pair, self.sum, self.norm],
            [shape((self.tokens, self.heads * 2 * HV), LOW)] + self.state_shapes, [], 5,
            q, y, total, opened, table, *dy,
        )

    def pull_inner(self, q, k, v, segc, segr, wide, total, norm, opened, table):
        return self.call(
            pull_inner_body, "mix_pull_inner",
            [self.thin, self.thin, self.head, self.column, self.row, self.pair, self.sum, self.norm, self.column, self.table],
            [self.thin, self.thin, self.head],
            [self.thin_shape(LOW), self.thin_shape(F32), self.head_shape(F32)],
            [self.acc, self.acc], 20, q, k, v, segc, segr, wide, total, norm, opened, table,
        )

    def pull_carry(self, k, v, tail, total, norm, dk, dv, table):
        return self.call(
            pull_carry_body, "mix_pull_carry",
            [self.thin, self.head, self.column, self.sum, self.norm, self.thin, self.head, self.table],
            [self.thin, self.head], [self.thin_shape(LOW), self.head_shape(LOW)], [self.acc], 6,
            k, v, tail, total, norm, dk, dv, table,
        )


def outside(part, reverse):
    count, place = lax.axis_size("batch"), lax.axis_index("batch")
    total = list(part)
    before = [jnp.zeros_like(a) for a in part]
    bit = 1
    while bit < count:
        pairs = [(i, i ^ bit) for i in range(count)]
        low = total[0].astype(LOW)
        other = [lax.ppermute(low, "batch", pairs).astype(F32), lax.ppermute(total[1], "batch", pairs)]
        upper = (place & bit) != 0
        take = jnp.logical_not(upper) if reverse else upper
        before = [a + jnp.where(take, b, 0.0) for a, b in zip(before, other)]
        total = [a + b for a, b in zip(total, other)]
        bit *= 2
    return before


def padded(width):
    return -(-width // 16) * 16


def batch_orders():
    count = lax.axis_size("batch")
    bits = [1 << b for b in range(count.bit_length() - 1)]
    return bits[:1] + bits[1:], bits[:1] + bits[:0:-1]


def block_order():
    count = lax.axis_size("batch")
    first, second = batch_orders()
    relative, places = [], []
    for step in range(count):
        at = sum(bit for n, bit in enumerate(first) if step >> (len(first) - 1 - n) & 1)
        relative.append(at)
        places.append(sum(1 << (len(second) - 1 - n) for n, bit in enumerate(second) if at & bit))
    blocks = jnp.asarray(np.array(relative, np.int32)) ^ lax.axis_index("batch").astype(jnp.int32)
    return blocks, places


def cost(micros):
    return pl.CostEstimate(flops=int(micros * 1e9), bytes_accessed=1 << 20, transcendentals=0)


BIG = pltpu.CompilerParams(dimension_semantics=("arbitrary",), vmem_limit_bytes=56 * 1024 * 1024)


def grad_blocks_body(blocks, swap, *refs, groups):
    out_a, out_b = refs[-2:]
    refs = list(refs[:-2])
    at = 0
    for rows, parts in groups:
        value = None
        for _ in range(parts):
            term = nn(refs[1][...], refs[0][...])
            refs = refs[2:]
            value = term if value is None else value + term
        for n, out in enumerate((out_a, out_b)):
            half = value[n * rows // 2 : (n + 1) * rows // 2].astype(LOW)
            gap = padded(rows // 2) - rows // 2
            if gap:
                half = jnp.concatenate([half, jnp.zeros((gap, half.shape[1]), LOW)], axis=0)
            out[0, at : at + padded(rows // 2), :] = half
        at += padded(rows // 2)


def grad_blocks(name, groups, far, micros):
    count = lax.axis_size("batch")
    split = count // 2
    width = groups[0][0][0].shape[1]
    columns = width // count
    blocks, places = block_order()
    base = split if far else 0
    in_specs, operands, kinds, rows = [], [], [], 0
    for parts in groups:
        for left, right in parts:
            in_specs.append(pl.BlockSpec((left.shape[0], columns), lambda s, b, w: (0, b[s])))
            in_specs.append(pl.BlockSpec(right.shape, lambda s, b, w: (0, 0)))
            operands += [left, right]
        kinds.append((parts[0][1].shape[0], len(parts)))
        rows += padded(parts[0][1].shape[0] // 2)
    size = (1, rows, columns)
    return pl.pallas_call(
        functools.partial(grad_blocks_body, groups=tuple(kinds)),
        grid_spec=pltpu.PrefetchScalarGridSpec(
            num_scalar_prefetch=2,
            grid=(split,),
            in_specs=in_specs,
            out_specs=[
                pl.BlockSpec(size, lambda s, b, w: (s, 0, 0)),
                pl.BlockSpec(size, lambda s, b, w: (w[s], 0, 0)),
            ],
        ),
        out_shape=[shape((split, rows, columns), LOW)] * 2,
        name=name,
        compiler_params=BIG,
        cost_estimate=cost(micros),
    )(
        blocks[base : base + split],
        jnp.asarray(np.array(places[base : base + split], np.int32) - base),
        *operands,
    )


def flip(value, bit):
    return lax.ppermute(value, "batch", [(i, i ^ bit) for i in range(lax.axis_size("batch"))])


def added(one, other):
    return (one.astype(F32) + other.astype(F32)).astype(LOW)


class Exchange:
    def __init__(self, far):
        self.orders = batch_orders()
        self.steps = len(self.orders[0])
        self.away, self.near, self.came = [[f] for f in far], None, [[], []]
        self.step = 0

    def get(self):
        return [self.away, self.near, self.came]

    def put(self, values):
        self.away, self.near, self.came = values

    def send(self, limit=None):
        n = self.step
        if n == 2 * self.steps:
            return
        for half, order in enumerate(self.orders):
            bit = order[n if n < self.steps else 2 * self.steps - 1 - n]
            first = len(self.came[half])
            last = len(self.away[half]) if limit is None else first + limit
            self.came[half] += [flip(a, bit) for a in self.away[half][first:last]]

    def take(self):
        n = self.step
        if n == 2 * self.steps:
            return
        self.step += 1
        if n < self.steps:
            half = self.near[0].shape[0] // 2
            pairs = [(k, c[0]) for k, c in zip(self.near, self.came)]
            if half:
                self.away = [[added(k[half:], c[half:])] for k, c in pairs]
                self.near = [added(k[:half], c[:half]) for k, c in pairs]
            else:
                self.near = [added(k, c) for k, c in pairs]
                self.away = [[k] for k in self.near]
        else:
            self.away = [a + c for a, c in zip(self.away, self.came)]
        self.came = [[], []]

    def run(self):
        while self.step < 2 * self.steps:
            self.send()
            self.take()
        return self.away


def place_body(blocks, table, *refs, outs, count):
    step = pl.program_id(0)
    pieces = count
    chosen = []
    for n in range(2):
        which = table[n, step]
        group = refs[n * pieces : (n + 1) * pieces]
        value = group[0][0]
        for m in range(1, pieces):
            value = jnp.where(which == m, group[m][0], value)
        chosen.append(value)
    results = refs[2 * pieces :]
    for start, rows, targets in outs:
        both = jnp.concatenate([c[start : start + rows // 2].astype(F32) for c in chosen], axis=0)
        for index, first, size, turned in targets:
            part = both[first : first + size]
            results[index][...] = part.T if turned else part


def place_blocks(name, pieces, outs, width, micros):
    count = lax.axis_size("batch")
    columns = width // count
    blocks, places = block_order()
    table = np.array([list(range(count)), places], np.int32)
    size = pieces[0][0].shape[1:]
    piece = pl.BlockSpec((1,) + size, lambda s, b, t: (0, 0, 0), pipeline_mode=pl.Buffered(1))
    out_specs, out_shape, layout, start = [], [], [], 0
    for rows, targets in outs:
        listed = []
        for first, used, turned in targets:
            listed.append((len(out_shape), first, used, turned))
            if turned:
                out_specs.append(pl.BlockSpec((columns, used), lambda s, b, t: (b[s], 0)))
                out_shape.append(shape((width, used), F32))
            else:
                out_specs.append(pl.BlockSpec((used, columns), lambda s, b, t: (0, b[s])))
                out_shape.append(shape((used, width), F32))
        layout.append((start, rows, tuple(listed)))
        start += padded(rows // 2)
    return pl.pallas_call(
        functools.partial(place_body, outs=tuple(layout), count=count),
        grid_spec=pltpu.PrefetchScalarGridSpec(
            num_scalar_prefetch=2,
            grid=(count,),
            in_specs=[piece] * (2 * count),
            out_specs=out_specs,
        ),
        out_shape=out_shape,
        name=name,
        compiler_params=BIG,
        cost_estimate=cost(micros),
    )(blocks, jnp.asarray(table), *pieces[0], *pieces[1])


def batch_sum(value):
    bit = 1
    while bit < lax.axis_size("batch"):
        value = value + flip(value, bit)
        bit *= 2
    return value


def after(values, *others):
    return lax.optimization_barrier((values, others))[0]


def lock(*items):
    values = lax.optimization_barrier([i.get() if hasattr(i, "get") else i for i in items])
    for item, value in zip(items, values):
        if hasattr(item, "put"):
            item.put(value)
    return [v for i, v in zip(items, values) if not hasattr(i, "get")]


class Gather:
    def __init__(self, *parts):
        self.right, self.left = [list(parts)], [list(parts)]
        self.hops = 0
        self.least = lax.axis_size("tensor") - 1

    def get(self):
        return [self.right, self.left]

    def put(self, values):
        self.right, self.left = values

    def hop(self):
        count = lax.axis_size("tensor")
        self.hops += 1
        to_right = [(k, k + 1) for k in range(self.hops - 1, count - 1)]
        to_left = [(k, k - 1) for k in range(1, count - self.hops + 1)]
        self.right.append([lax.ppermute(a, "tensor", to_right) for a in self.right[-1]])
        self.left.append([lax.ppermute(a, "tensor", to_left) for a in self.left[-1]])

    def run(self):
        while self.hops < self.least:
            self.hop()
        return self

    def pieces(self, n=0):
        count, place = lax.axis_size("tensor"), lax.axis_index("tensor")
        return [self.right[0][n]] + [
            jnp.where(place + r < count, self.left[r][n], self.right[count - r][n]) for r in range(1, count)
        ]

    def total(self, n=0):
        return sum(a[n] for a in self.right) + sum(a[n] for a in self.left[1:])


class Scatter:
    def __init__(self, make):
        self.make, self.came, self.made = make, [], {}
        self.left = lax.axis_size("tensor") - 1
        self.prepare()

    def prepare(self):
        count = lax.axis_size("tensor")
        for r in (self.left, (count - self.left) % count):
            if r not in self.made:
                self.made[r] = self.make(r)

    def get(self):
        return [self.came, self.made]

    def put(self, values):
        self.came, self.made = values

    def hop(self):
        count = lax.axis_size("tensor")
        sends = [self.made[self.left], self.made[count - self.left]]
        if self.came:
            sends = [s + c.astype(F32) for s, c in zip(sends, self.came)]
        sends = [s.astype(LOW) for s in sends]
        self.came = [
            lax.ppermute(sends[0], "tensor", [(k, k + 1) for k in range(0, count - self.left)]),
            lax.ppermute(sends[1], "tensor", [(k, k - 1) for k in range(self.left, count)]),
        ]
        self.left -= 1
        self.prepare()

    def result(self):
        return self.made[0] + self.came[0].astype(F32) + self.came[1].astype(F32)


def copy_body(turn, in_ref, out_ref):
    out_ref[...] = in_ref[...]


def straighten(array):
    count = lax.axis_size("tensor")
    turn = (jnp.arange(count, dtype=jnp.int32) - lax.axis_index("tensor")) % count
    size = (array.shape[0], array.shape[1] // count)
    return pl.pallas_call(
        copy_body,
        grid_spec=pltpu.PrefetchScalarGridSpec(
            num_scalar_prefetch=1,
            grid=(count,),
            in_specs=[pl.BlockSpec(size, lambda n, t: (0, t[n]))],
            out_specs=pl.BlockSpec(size, lambda n, t: (0, n)),
        ),
        out_shape=shape(array.shape, array.dtype),
        name="straighten",
        compiler_params=BIG,
        cost_estimate=cost(4),
    )(turn, array)


def widen(part):
    return lax.all_gather(part, "tensor", axis=1, tiled=True)


def narrow(part):
    return lax.psum_scatter(part, "tensor", scatter_dimension=1, tiled=True).astype(F32)


def project(left, right):
    return jnp.dot(left, right, preferred_element_type=F32)


def project_back(left, right):
    return jnp.einsum("ti,ji->tj", left, right, preferred_element_type=F32)


def across(left, right):
    return jnp.einsum("it,ij->tj", left, right, preferred_element_type=F32)


def row_sum(values):
    return jnp.sum(values, axis=1, keepdims=True)


def local(
    tokens, doc_lengths, norm1_gain, w_query, w_key, w_value, w_out, norm2_gain, w_gate, w_up, w_down, cotangent,
):
    count, slice_width = tokens.shape
    heads = w_value.shape[1] // HV
    lanes = heads * FEAT
    width = w_query.shape[0]
    begin_here = lax.axis_index("batch") * count
    position = begin_here + jnp.arange(count, dtype=jnp.int32)
    doc_index = jnp.arange(doc_lengths.shape[0], dtype=jnp.int32)
    doc_begins = jnp.sum(jnp.where(doc_index[None, :] < doc_index[:, None], doc_lengths[None, :], 0), axis=1)
    segment = jnp.sum((position[:, None] >= doc_begins[None, :]).astype(jnp.int32), axis=1) - 1
    head_seg, tail_seg = segment[0], segment[-1]
    first_begin = jnp.sum(jnp.where(doc_index == head_seg, doc_begins, 0))
    opened = ((segment == head_seg) & (first_begin < begin_here)).astype(F32)[:, None]
    tail = (segment == tail_seg).astype(F32)[:, None]
    segc, segr = segment[:, None], segment[None, :]
    table = jnp.asarray(feature_table())
    mixer = Mixer(count, heads)

    size, place = lax.axis_size("tensor"), lax.axis_index("tensor")
    half = count // 2
    cut = lambda a: (a[:half], a[half:])
    join = lambda *parts: jnp.concatenate(parts, axis=0)
    c_a, c_b = cut(cotangent)
    w_gate, w_up = w_gate.T, w_up.T
    units = w_gate.shape[0]

    x_full = widen(tokens)
    gains = lax.all_gather(jnp.stack([norm1_gain, norm2_gain]), "tensor", axis=1, tiled=True)
    w_mix = jnp.concatenate([w_query, w_key, w_value], axis=1)
    gather_c = Gather(cotangent)
    x_full, gains, w_mix = lock(x_full, gains, w_mix, gather_c)

    gather_c.hop()
    x_wide = x_full.astype(F32)
    scale_one = lax.rsqrt(row_sum(x_wide * x_wide) / width + EPSILON)
    normed_one = (x_wide * scale_one * gains[0:1]).astype(LOW)
    mixed_in = project(normed_one, w_mix).astype(LOW)
    q, k, v = mixed_in[:, :lanes], mixed_in[:, lanes : 2 * lanes], mixed_in[:, 2 * lanes :]
    carry = mixer.state(k, v, tail, table)
    prior = outside(carry, False)
    numer, denom = mixer.inner(q, k, v, segc, segr)
    y, total = mixer.merge(q, numer, denom, *prior, opened, table)
    columns = lambda w, r: lax.dynamic_slice_in_dim(w, ((place + r) % size) * slice_width, slice_width, 1)
    scatter = Scatter(lambda r: project(y, columns(w_out, r)))
    y, total = lock(y, total, gather_c, scatter)
    while scatter.left:
        scatter.hop()
        if gather_c.hops < gather_c.least:
            gather_c.hop()
        lock(scatter, gather_c)
    hidden = tokens.astype(F32) + scatter.result()
    hidden_a, hidden_b = cut(hidden)
    low_a, low_b = cut(hidden.astype(LOW))
    hidden_a, hidden_b, low_a, low_b = lock(hidden_a, hidden_b, low_a, low_b)

    wide_a = widen(low_a)
    c_full = straighten(jnp.concatenate(gather_c.pieces(), axis=1))
    ca_full, cb_full = cut(c_full)
    dinner_a = project_back(w_down, ca_full)
    dinner_b = project_back(w_down, cb_full)
    wide_a, c_full, dinner_a, dinner_b = lock(wide_a, c_full, dinner_a, dinner_b)
    ca_full, cb_full = cut(c_full)

    def feed(wide, dinner):
        wide32 = wide.astype(F32)
        scale = lax.rsqrt(row_sum(wide32 * wide32) / width + EPSILON)
        normed = (wide32 * scale * gains[1:2]).astype(LOW)
        gate = project_back(w_gate, normed)
        up = project_back(w_up, normed)
        sig = jax.nn.sigmoid(gate)
        silu = gate * sig
        inner = (silu * up).astype(LOW)
        dgate = (dinner * up * sig * (1.0 + gate * (1.0 - sig))).astype(LOW)
        dup = (dinner * silu).astype(LOW)
        pulled = (across(dgate, w_gate) + across(dup, w_up)).astype(LOW)
        return scale, normed, inner, dgate, dup, pulled

    wide_b = widen(low_b)
    wide_b, (scale_a, normed_a, inner_a, dgate_a, dup_a, part) = lock(wide_b, feed(wide_a, dinner_a))

    back_a = narrow(part)
    scale_b, normed_b, inner_b, dgate_b, dup_b, part = feed(wide_b, dinner_b)
    groups = [
        [(normed_a, dgate_a), (normed_b, dgate_b)],
        [(normed_a, dup_a), (normed_b, dup_b)],
        [(ca_full, inner_a), (cb_full, inner_b)],
    ]
    ffn = Exchange(grad_blocks("grad_ffn_far", groups, True, 16))
    back_a, scale_b, normed_b, inner_b, dgate_b, dup_b, part = lock(
        back_a, scale_b, normed_b, inner_b, dgate_b, dup_b, part, ffn
    )

    def turned(c, scale, back, hidden):
        scaled = scale * back
        return c.astype(F32) + norm2_gain[None, :] * scaled, jnp.sum(scaled * hidden, axis=0)

    def spread(u, c, wide, scale, local_u, hidden):
        u, wide = u.astype(F32), wide.astype(F32)
        dot = row_sum((u - c.astype(F32)) * wide) * scale * scale / width
        dh = (u - wide * dot).astype(LOW)
        return dh, local_u - hidden * dot, project_back(dh, w_out)

    back_b = narrow(part)
    u_a, gain_a = turned(c_a, scale_a, back_a, hidden_a)
    low_a = u_a.astype(LOW)
    groups = [
        [(normed_a, dgate_a), (normed_b, dgate_b)],
        [(normed_a, dup_a), (normed_b, dup_b)],
        [(ca_full, inner_a), (cb_full, inner_b)],
    ]
    ffn.send()
    ffn.near = grad_blocks("grad_ffn_near", groups, False, 16)
    ffn.take()
    ffn.send()
    back_b, u_a, gain_a, low_a, ffn.away, ffn.near = lock(back_b, u_a, gain_a, low_a, ffn.away, ffn.near)

    wide_u = widen(low_a)
    u_b, gain_b = turned(c_b, scale_b, back_b, hidden_b)
    low_b = u_b.astype(LOW)
    parts = [across(m, w_down).astype(LOW) for m in (inner_a, inner_b)]
    wide_u, u_b, gain_b, low_b, parts = lock(wide_u, u_b, gain_b, low_b, parts, ffn)

    wide_v = widen(low_b)
    ffn.take()
    ffn.send()
    dh_a, grad_hidden_a, dy_a = spread(wide_u, ca_full, wide_a, scale_a, u_a, hidden_a)
    ffn.take()
    ffn.send()
    wide_v, dh_a, grad_hidden_a, dy_a = lock(wide_v, dh_a, grad_hidden_a, dy_a, ffn)

    down = narrow(join(*parts))
    ffn.take()
    ffn.send(1)
    dh_b, grad_hidden_b, dy_b = spread(wide_v, cb_full, wide_b, scale_b, u_b, hidden_b)
    wide, dsum, dnorm = mixer.pull_state(q, [dy_a, dy_b], y, total, opened, table)
    wide, dsum, dnorm = lock(wide, dsum, dnorm, ffn)
    following = outside([dsum, dnorm], True)
    dq, dk, dv = mixer.pull_inner(q, k, v, segc, segr, wide, *prior, opened, table)
    following, dq, dk, dv = lock(following, dq, dk, dv, ffn)
    ffn.send()
    dk, dv = mixer.pull_carry(k, v, tail, *following, dk, dv, table)
    dmix = jnp.concatenate([dq, dk, dv], axis=1)
    part = project_back(dmix, w_mix).astype(LOW)
    down, part, dmix, dh_b, grad_hidden_b = lock(down, part, dmix, dh_b, grad_hidden_b)

    back = narrow(part)
    y_a, y_b = cut(y)
    groups = [[(normed_one, dmix.T)], [(dh_a, y_a.T), (dh_b, y_b.T)]]
    mix = Exchange(grad_blocks("grad_mix_far", groups, True, 5))
    mix.send()
    mix.near = grad_blocks("grad_mix_near", groups, False, 5)
    dots = Gather(row_sum(dmix.astype(F32) * mixed_in.astype(F32)).reshape(count // 128, 128)).run()
    lock(mix, ffn)
    mix.take()
    mix.send()
    ffn.take()
    ffn.send()
    output = (join(hidden_a, hidden_b) + down).astype(LOW)
    output = lock(mix, ffn, output, dots)[0]
    mix.take()
    mix.send()
    ffn.take()
    grad_w_gate, grad_w_up, grad_w_down = place_blocks(
        "place_ffn", ffn.run(), [(units, [(0, units, False)])] * 3, width, 20
    )
    mix.take()
    mix.send()
    mix.take()
    mix.send()
    back, grad_w_gate, grad_w_up, grad_w_down, output = lock(
        back, grad_w_gate, grad_w_up, grad_w_down, output, mix
    )
    inputs = tokens.astype(F32)
    gain_one = jnp.sum(back * inputs * scale_one, axis=0)
    gain_grads = batch_sum(jnp.stack([gain_one, gain_a + gain_b]))
    grad_tokens = (
        join(grad_hidden_a, grad_hidden_b)
        + scale_one * norm1_gain[None, :] * back
        - inputs * (scale_one * scale_one * dots.total().reshape(count, 1) / width)
    )
    values = heads * HV
    grad_w_query, grad_w_key, grad_w_value, grad_w_out = place_blocks(
        "place_mix",
        mix.run(),
        [
            (2 * lanes + values, [(0, lanes, False), (lanes, lanes, False), (2 * lanes, values, True)]),
            (values, [(0, values, False)]),
        ],
        width,
        5,
    )
    return (
        output,
        grad_tokens,
        gain_grads[0],
        grad_w_query.T,
        grad_w_key.T,
        grad_w_value,
        grad_w_out,
        gain_grads[1],
        grad_w_gate.T,
        grad_w_up.T,
        grad_w_down,
    )


def solution(mesh):
    rows, cols = P("tensor", None), P(None, "tensor")
    both, one = P("batch", "tensor"), P("tensor")
    in_specs = (both, P(), one, cols, cols, cols, rows, one, cols, cols, rows, both)
    out_specs = (both, both, one, cols, cols, cols, rows, one, cols, cols, rows)
    return jax.shard_map(local, mesh=mesh, in_specs=in_specs, out_specs=out_specs, check_vma=False)
```

```python
import functools
import math

import jax
import jax.numpy as jnp
import numpy as np
from jax import lax
from jax.experimental import pallas as pl
from jax.experimental.pallas import tpu as pltpu
from jax.sharding import PartitionSpec as P

FEAT = 16
HV = 128
EPSILON = 1e-05
WIDE = 256
ROWS = 160
STRIP = 256
CHUNKS = 2
LOW = jnp.bfloat16
F32 = jnp.float32


def feature_table():
    table = np.zeros((8, WIDE), np.float32)
    table[0:2] = -1.0
    at = 0
    for i in range(FEAT + 1):
        for j in range(i, FEAT + 1):
            table[0, at] = i if i < FEAT else -1
            table[1, at] = j if j < FEAT else -1
            table[2, at] = float(i == FEAT)
            table[3, at] = float(j == FEAT)
            table[4, at] = 0.5 if i == j and i < FEAT else 1.0
            at += 1
    return table


def nt(a, b):
    return lax.dot_general(a, b, (((1,), (1,)), ((), ())), preferred_element_type=F32)


def tn(a, b):
    return lax.dot_general(a, b, (((0,), (0,)), ((), ())), preferred_element_type=F32)


def nn(a, b):
    return lax.dot_general(a, b, (((1,), (0,)), ((), ())), preferred_element_type=F32)


def pickers(table, head, lanes):
    lane = lax.broadcasted_iota(jnp.int32, (lanes, WIDE), 0).astype(F32)
    base = (head * FEAT).astype(F32)
    first, second = table[0:1, :], table[1:2, :]
    one = jnp.where((lane == base + first) & (first >= 0), 0.5, 0.0).astype(LOW)
    two = jnp.where((lane == base + second) & (second >= 0), 0.5, 0.0).astype(LOW)
    return one, two


def head_lanes(head, lanes):
    lane = lax.broadcasted_iota(jnp.int32, (1, lanes), 1)
    return (lane >= head * FEAT) & (lane < (head + 1) * FEAT)


def factors(z, table, one, two):
    return nn(z, one) + table[2:3, :], nn(z, two) + table[3:4, :]


def pad_state(state):
    return jnp.concatenate([state, jnp.zeros((WIDE - ROWS, HV), state.dtype)], axis=0)


def state_body(k_ref, v_ref, tail_ref, table_ref, sum_ref, norm_ref):
    head = pl.program_id(0)
    table = table_ref[...]
    one, two = pickers(table, head, k_ref.shape[1])
    left, right = factors(k_ref[...], table, one, two)
    feats = (left * right * table[4:5, :] * tail_ref[...]).astype(LOW)
    sum_ref[0] = tn(feats, v_ref[...])[:ROWS].astype(sum_ref.dtype)
    norm_ref[0] = nn(jnp.ones((8, feats.shape[0]), LOW), feats)


def masked_weights(scores, segc, segr, row0, width):
    rows = scores.shape[0]
    row = row0 + lax.broadcasted_iota(jnp.int32, (rows, width), 0)
    col = lax.broadcasted_iota(jnp.int32, (rows, width), 1)
    return (row >= col) & (segc == segr)


def inner_body(q_ref, k_ref, v_ref, segc_ref, segr_ref, numer_ref, denom_ref):
    head = pl.program_id(0)
    tokens, lanes = q_ref.shape
    mine = head_lanes(head, lanes)
    for row0 in range(0, tokens, STRIP):
        width = row0 + STRIP
        query = jnp.where(mine, q_ref[pl.ds(row0, STRIP), :] * LOW(0.25), LOW(0.0))
        scores = nt(query, k_ref[pl.ds(0, width), :])
        keep = masked_weights(scores, segc_ref[pl.ds(row0, STRIP), :], segr_ref[:, pl.ds(0, width)], row0, width)
        weights = jnp.where(keep, 1.0 + scores * (1.0 + 0.5 * scores), 0.0).astype(LOW)
        wide = jnp.concatenate([v_ref[pl.ds(0, width), :], jnp.ones((width, HV), LOW)], axis=1)
        both = nn(weights, wide)
        numer_ref[pl.ds(row0, STRIP), :] = both[:, :HV]
        denom_ref[pl.ds(row0, STRIP), :] = both[:, HV:]


def merge_body(q_ref, numer_ref, denom_ref, sum_ref, norm_ref, open_ref, table_ref, y_ref, total_ref):
    head = pl.program_id(0)
    table = table_ref[...]
    one, two = pickers(table, head, q_ref.shape[1])
    left, right = factors(q_ref[...], table, one, two)
    feats = (left * right * open_ref[...]).astype(LOW)
    norm = jnp.broadcast_to(norm_ref[0][0:1, :], (HV, WIDE))
    norm_high = norm.astype(LOW)
    norm_rest = (norm - norm_high.astype(F32)).astype(LOW)
    total = denom_ref[...] + nt(feats, norm_high) + nt(feats, norm_rest)
    numer = numer_ref[...] + nn(feats, pad_state(sum_ref[0].astype(LOW)))
    total_ref[...] = total
    y_ref[...] = (numer / total).astype(LOW)


def pull_state_body(q_ref, y_ref, total_ref, open_ref, table_ref, *refs):
    *dy_refs, wide_ref, sum_ref, norm_ref = refs
    head = pl.program_id(0)
    table = table_ref[...]
    one, two = pickers(table, head, q_ref.shape[1])
    left, right = factors(q_ref[...], table, one, two)
    feats = (left * right * open_ref[...]).astype(LOW)
    inverse = 1.0 / total_ref[...]
    dy = jnp.concatenate([r[...] for r in dy_refs], axis=0)
    dnumer = (dy * inverse).astype(LOW)
    ddenom = -jnp.sum(dy * y_ref[...].astype(F32), axis=1, keepdims=True) * inverse
    ddenom = jnp.where(lax.broadcasted_iota(jnp.int32, ddenom.shape, 1) < 8, ddenom, 0.0).astype(LOW)
    wide_ref[...] = jnp.concatenate([dnumer, ddenom], axis=1)
    sum_ref[0] = tn(feats, dnumer)[:ROWS].astype(sum_ref.dtype)
    norm_ref[0] = tn(ddenom, feats)[:8]


def pull_inner_body(
    q_ref, k_ref, v_ref, segc_ref, segr_ref, wide_ref, sum_ref, norm_ref, open_ref, table_ref,
    dq_ref, dk_ref, dv_ref, dq_acc, dk_acc,
):
    head = pl.program_id(0)
    last = pl.num_programs(0) - 1
    tokens, lanes = q_ref.shape
    mine = head_lanes(head, lanes)

    @pl.when(head == 0)
    def _():
        dq_acc[...] = jnp.zeros_like(dq_acc)
        dk_acc[...] = jnp.zeros_like(dk_acc)

    dv_ref[...] = jnp.zeros_like(dv_ref)
    table = table_ref[...]
    one, two = pickers(table, head, lanes)
    state = pad_state(sum_ref[0].astype(LOW))
    norm = norm_ref[0][0:1, :]
    single = (lax.broadcasted_iota(jnp.int32, (1, HV), 1) < 1).astype(LOW)
    for row0 in range(0, tokens, STRIP):
        width = row0 + STRIP
        rows = pl.ds(row0, STRIP)
        query = jnp.where(mine, q_ref[rows, :] * LOW(0.25), LOW(0.0))
        keys = jnp.where(mine, k_ref[pl.ds(0, width), :] * LOW(0.25), LOW(0.0))
        scores = nt(query, k_ref[pl.ds(0, width), :])
        keep = masked_weights(scores, segc_ref[rows, :], segr_ref[:, pl.ds(0, width)], row0, width)
        weights = jnp.where(keep, 1.0 + scores * (1.0 + 0.5 * scores), 0.0).astype(LOW)
        dwide = wide_ref[rows, :]
        ones = jnp.broadcast_to(single, (width, HV))
        wide = jnp.concatenate([v_ref[pl.ds(0, width), :], ones], axis=1)
        dscores = jnp.where(keep, nt(dwide, wide) * (1.0 + scores), 0.0).astype(LOW)
        dv_ref[pl.ds(0, width), :] += tn(weights, dwide[:, :HV])
        dk_acc[pl.ds(0, width), :] += tn(dscores, query)
        left, right = factors(q_ref[rows, :], table, one, two)
        pulled = nt(dwide[:, :HV], state) + dwide[:, HV : HV + 1].astype(F32) * norm
        pulled = pulled * open_ref[rows, :]
        dq_acc[rows, :] += nn(dscores, keys) + nt((pulled * right).astype(LOW), one) + nt((pulled * left).astype(LOW), two)

    @pl.when(head == last)
    def _():
        dq_ref[...] = dq_acc[...].astype(dq_ref.dtype)
        dk_ref[...] = dk_acc[...]


def thin_width(heads):
    return -(-2 * heads * FEAT // HV) * HV


def pull_carry_body(k_ref, v_ref, tail_ref, sum_ref, norm_ref, dq_ref, dk_ref, dv_ref, table_ref, out_ref, dk_acc):
    head = pl.program_id(0)
    tokens, lanes = k_ref.shape
    start = 2 * lanes + -2 * lanes % HV

    @pl.when(head == 0)
    def _():
        dk_acc[...] = dk_ref[...]

    table = table_ref[...]
    one, two = pickers(table, head, lanes)
    left, right = factors(k_ref[...], table, one, two)
    scale = table[4:5, :] * tail_ref[...]
    state = pad_state(sum_ref[0].astype(LOW))
    dv = dv_ref[...] + nn((left * right * scale).astype(LOW), state)
    out_ref[:, pl.ds(pl.multiple_of(start + head * HV, HV), HV)] = dv.astype(out_ref.dtype)
    pulled = (nt(v_ref[...], state) + norm_ref[0][0:1, :]) * scale
    dk_acc[...] += nt((pulled * right).astype(LOW), one) + nt((pulled * left).astype(LOW), two)

    @pl.when(head == pl.num_programs(0) - 1)
    def _():
        thin = [dq_ref[...], dk_acc[...].astype(out_ref.dtype)]
        if start > 2 * lanes:
            thin.append(jnp.zeros((tokens, start - 2 * lanes), out_ref.dtype))
        out_ref[:, :start] = jnp.concatenate(thin, axis=1)


def shape(dims, kind):
    return jax.ShapeDtypeStruct(dims, kind)


class Mixer:
    def __init__(self, tokens, heads):
        self.tokens, self.heads = tokens, heads
        lanes = heads * FEAT
        self.full = lambda a, b: pl.BlockSpec((a, b), lambda h: (0, 0))
        self.thin = self.full(tokens, lanes)
        self.column = self.full(tokens, 1)
        self.row = self.full(1, tokens)
        self.table = self.full(8, WIDE)
        self.head = pl.BlockSpec((tokens, HV), lambda h: (0, h))
        self.pair = pl.BlockSpec((tokens, 2 * HV), lambda h: (0, h))
        self.sum = pl.BlockSpec((1, ROWS, HV), lambda h: (h, 0, 0))
        self.norm = pl.BlockSpec((1, 8, WIDE), lambda h: (h, 0, 0))
        self.thin_shape = lambda kind: shape((tokens, lanes), kind)
        self.head_shape = lambda kind: shape((tokens, heads * HV), kind)
        self.state_shapes = [shape((heads, ROWS, HV), F32), shape((heads, 8, WIDE), F32)]
        self.acc = pltpu.VMEM((tokens, lanes), F32)

    def call(self, body, name, in_specs, out_specs, out_shape, scratch, micros, *args):
        return pl.pallas_call(
            body,
            grid=(self.heads,),
            in_specs=in_specs,
            out_specs=out_specs,
            out_shape=out_shape,
            scratch_shapes=scratch,
            name=name,
            compiler_params=pltpu.CompilerParams(
                dimension_semantics=("arbitrary",), vmem_limit_bytes=48 * 1024 * 1024
            ),
            cost_estimate=pl.CostEstimate(
                flops=int(micros * 1e-6 * 1e15), bytes_accessed=1 << 20, transcendentals=0
            ),
        )(*args)

    def state(self, k, v, tail, table):
        return self.call(
            state_body, "mix_state", [self.thin, self.head, self.column, self.table],
            [self.sum, self.norm], self.state_shapes, [], 4, k, v, tail, table,
        )

    def inner(self, q, k, v, segc, segr):
        return self.call(
            inner_body, "mix_inner", [self.thin, self.thin, self.head, self.column, self.row],
            [self.head, self.head], [self.head_shape(F32)] * 2, [], 10, q, k, v, segc, segr,
        )

    def merge(self, q, numer, denom, total, norm, opened, table):
        return self.call(
            merge_body, "mix_merge",
            [self.thin, self.head, self.head, self.sum, self.norm, self.column, self.table],
            [self.head, self.head], [self.head_shape(LOW), self.head_shape(F32)], [], 5,
            q, numer, denom, total, norm, opened, table,
        )

    def pull_state(self, q, dy, y, total, opened, table):
        return self.call(
            pull_state_body, "mix_pull_state",
            [self.thin, self.head, self.head, self.column, self.table]
            + [pl.BlockSpec((d.shape[0], HV), lambda h: (0, h)) for d in dy],
            [self.pair, self.sum, self.norm],
            [shape((self.tokens, self.heads * 2 * HV), LOW)] + self.state_shapes, [], 5,
            q, y, total, opened, table, *dy,
        )

    def pull_inner(self, q, k, v, segc, segr, wide, total, norm, opened, table):
        return self.call(
            pull_inner_body, "mix_pull_inner",
            [self.thin, self.thin, self.head, self.column, self.row, self.pair, self.sum, self.norm, self.column, self.table],
            [self.thin, self.thin, self.head],
            [self.thin_shape(LOW), self.thin_shape(F32), self.head_shape(F32)],
            [self.acc, self.acc], 20, q, k, v, segc, segr, wide, total, norm, opened, table,
        )

    def pull_carry(self, k, v, tail, total, norm, dq, dk, dv, table):
        width = thin_width(self.heads) + self.heads * HV
        return self.call(
            pull_carry_body, "mix_pull_carry",
            [self.thin, self.head, self.column, self.sum, self.norm, self.thin, self.thin, self.head, self.table],
            self.full(self.tokens, width), shape((self.tokens, width), LOW), [self.acc], 6,
            k, v, tail, total, norm, dq, dk, dv, table,
        )


def outside(part, reverse):
    count, place = lax.axis_size("batch"), lax.axis_index("batch")
    total = list(part)
    before = [jnp.zeros_like(a) for a in part]
    bit = 1
    while bit < count:
        pairs = [(i, i ^ bit) for i in range(count)]
        low = total[0].astype(LOW)
        other = [lax.ppermute(low, "batch", pairs).astype(F32), lax.ppermute(total[1], "batch", pairs)]
        upper = (place & bit) != 0
        take = jnp.logical_not(upper) if reverse else upper
        before = [a + jnp.where(take, b, 0.0) for a, b in zip(before, other)]
        total = [a + b for a, b in zip(total, other)]
        bit *= 2
    return before


def padded(width):
    return -(-width // 16) * 16


def batch_orders():
    count = lax.axis_size("batch")
    bits = [1 << b for b in range(count.bit_length() - 1)]
    return bits[:1] + bits[1:], bits[:1] + bits[:0:-1]


def block_order():
    count = lax.axis_size("batch")
    first, second = batch_orders()
    relative, places = [], []
    for step in range(count):
        at = sum(bit for n, bit in enumerate(first) if step >> (len(first) - 1 - n) & 1)
        relative.append(at)
        places.append(sum(1 << (len(second) - 1 - n) for n, bit in enumerate(second) if at & bit))
    blocks = jnp.asarray(np.array(relative, np.int32)) ^ lax.axis_index("batch").astype(jnp.int32)
    return blocks, places


def cost(micros):
    return pl.CostEstimate(flops=int(micros * 1e9), bytes_accessed=1 << 20, transcendentals=0)


BIG = pltpu.CompilerParams(dimension_semantics=("arbitrary",), vmem_limit_bytes=56 * 1024 * 1024)


def grad_values(refs, groups):
    values = []
    for rows, parts in groups:
        value = None
        for _ in range(parts):
            term = nn(refs[1][...], refs[0][...])
            refs = refs[2:]
            value = term if value is None else value + term
        values.append(value)
    return values


def grad_body(blocks, swap, *refs, groups, summed):
    step = pl.program_id(0)
    places = (step, swap[0, step])
    middle = pl.num_programs(0) // 2
    sources = 2 * sum(parts for _, parts in groups)
    values = grad_values(list(refs[:sources]), groups)
    outs = refs[-4:]
    came = refs[sources:-4]
    at = 0
    for (rows, _), value in zip(groups, values):
        size = padded(rows // 2)
        for n in range(2):
            half = value[n * rows // 2 : (n + 1) * rows // 2]
            if size > rows // 2:
                half = jnp.concatenate([half, jnp.zeros((size - rows // 2, half.shape[1]), F32)], axis=0)
            span = slice(at, at + size)
            if summed:
                other = jnp.where(places[n] < middle, came[n][0, span, :], came[2 + n][0, span, :])
                half = half + other.astype(F32)
            half = half.astype(LOW)

            @pl.when(places[n] < middle)
            def _():
                outs[n][0, span, :] = half

            @pl.when(places[n] >= middle)
            def _():
                outs[2 + n][0, span, :] = half

        at += size


def grad_blocks(name, groups, far, came, micros):
    count = lax.axis_size("batch")
    split = count // 2
    width = groups[0][0][0].shape[1]
    columns = width // count
    blocks, places = block_order()
    base = split if far else 0
    in_specs, operands, kinds, rows = [], [], [], 0
    for parts in groups:
        for left, right in parts:
            in_specs.append(pl.BlockSpec((left.shape[0], columns), lambda s, b, w: (0, b[s])))
            in_specs.append(pl.BlockSpec(right.shape, lambda s, b, w: (0, 0)))
            operands += [left, right]
        kinds.append((parts[0][1].shape[0], len(parts)))
        rows += padded(parts[0][1].shape[0] // 2)
    size = (1, rows, columns)
    places = [p - base for p in places[base : base + split]]
    table, specs = [places], []
    for low in (0, split // 2):
        for order in (list(range(split)), places):
            uses = [(s, p - low) for s, p in enumerate(order) if low <= p < low + split // 2]
            table.append([([at for when, at in uses if when <= s] or [uses[0][1]])[-1] for s in range(split)])
            specs.append(pl.BlockSpec(size, lambda s, b, w, n=len(table) - 1: (w[n, s], 0, 0)))
    if came:
        in_specs += specs
        operands += came
    outs = pl.pallas_call(
        functools.partial(grad_body, groups=tuple(kinds), summed=bool(came)),
        grid_spec=pltpu.PrefetchScalarGridSpec(
            num_scalar_prefetch=2, grid=(split,), in_specs=in_specs, out_specs=specs
        ),
        out_shape=[shape((split // 2, rows, columns), LOW)] * 4,
        name=name,
        compiler_params=BIG,
        cost_estimate=cost(micros),
    )(blocks[base : base + split], jnp.asarray(np.array(table, np.int32)), *operands)
    return outs[:2], outs[2:]


def flip(value, bit):
    return lax.ppermute(value, "batch", [(i, i ^ bit) for i in range(lax.axis_size("batch"))])


def added(one, other):
    return (one.astype(F32) + other.astype(F32)).astype(LOW)


class Exchange:
    def __init__(self, far):
        self.orders = batch_orders()
        self.steps = len(self.orders[0])
        self.away, self.near, self.came = [list(f) for f in zip(*far)], None, [[], []]
        self.step = 0

    def get(self):
        return [self.away, self.near, self.came]

    def put(self, values):
        self.away, self.near, self.came = values

    def send(self, limit=None):
        n = self.step
        if n == 2 * self.steps:
            return
        for half, order in enumerate(self.orders):
            bit = order[n if n < self.steps else 2 * self.steps - 1 - n]
            first = len(self.came[half])
            last = len(self.away[half]) if limit is None else first + limit
            self.came[half] += [flip(a, bit) for a in self.away[half][first:last]]

    def begin(self, name, groups, micros):
        self.near, away = grad_blocks(name, groups, False, [c[n] for n in range(2) for c in self.came], micros)
        self.away, self.came, self.step = [[a] for a in away], [[], []], 1

    def take(self):
        n = self.step
        if n == 2 * self.steps:
            return
        self.step += 1
        if n == 0:
            self.near, away = [[added(b, c[m]) for b, c in zip(half, self.came)] for m, half in enumerate(self.near)]
            self.away = [[a] for a in away]
        elif n < self.steps:
            half = self.near[0].shape[0] // 2
            pairs = [(k, c[0]) for k, c in zip(self.near, self.came)]
            if half:
                self.away = [[added(k[half:], c[half:])] for k, c in pairs]
                self.near = [added(k[:half], c[:half]) for k, c in pairs]
            else:
                self.near = [added(k, c) for k, c in pairs]
                self.away = [[k] for k in self.near]
        else:
            self.away = [a + c for a, c in zip(self.away, self.came)]
        self.came = [[], []]

    def run(self):
        while self.step < 2 * self.steps:
            self.send()
            self.take()
        return self.away


def place_body(blocks, table, *refs, outs, count):
    step = pl.program_id(0)
    pieces = count
    chosen = []
    for n in range(2):
        which = table[n, step]
        group = refs[n * pieces : (n + 1) * pieces]
        value = group[0][0]
        for m in range(1, pieces):
            value = jnp.where(which == m, group[m][0], value)
        chosen.append(value)
    results = refs[2 * pieces :]
    for start, rows, targets in outs:
        both = jnp.concatenate([c[start : start + rows // 2].astype(F32) for c in chosen], axis=0)
        for index, first, size, turned in targets:
            part = both[first : first + size]
            results[index][...] = part.T if turned else part


def place_blocks(name, pieces, outs, width, micros, part=None):
    count = lax.axis_size("batch")
    columns = width // count
    blocks, places = block_order()
    table = np.array([list(range(count)), places], np.int32)
    size = pieces[0][0].shape[1:]
    if part is not None:
        size = (padded(outs[0][0] // 2), size[1])
    piece = pl.BlockSpec((1,) + size, lambda s, b, t: (0, part or 0, 0), pipeline_mode=pl.Buffered(1))
    out_specs, out_shape, layout, start = [], [], [], 0
    for rows, targets in outs:
        listed = []
        for first, used, turned in targets:
            listed.append((len(out_shape), first, used, turned))
            if turned:
                out_specs.append(pl.BlockSpec((columns, used), lambda s, b, t: (b[s], 0)))
                out_shape.append(shape((width, used), F32))
            else:
                out_specs.append(pl.BlockSpec((used, columns), lambda s, b, t: (0, b[s])))
                out_shape.append(shape((used, width), F32))
        layout.append((start, rows, tuple(listed)))
        start += padded(rows // 2)
    return pl.pallas_call(
        functools.partial(place_body, outs=tuple(layout), count=count),
        grid_spec=pltpu.PrefetchScalarGridSpec(
            num_scalar_prefetch=2,
            grid=(count,),
            in_specs=[piece] * (2 * count),
            out_specs=out_specs,
        ),
        out_shape=out_shape,
        name=name,
        compiler_params=BIG,
        cost_estimate=cost(micros),
    )(blocks, jnp.asarray(table), *pieces[0], *pieces[1])


def batch_sum(value):
    bit = 1
    while bit < lax.axis_size("batch"):
        value = value + flip(value, bit)
        bit *= 2
    return value


def after(values, *others):
    return lax.optimization_barrier((values, others))[0]


def lock(*items):
    values = lax.optimization_barrier([i.get() if hasattr(i, "get") else i for i in items])
    for item, value in zip(items, values):
        if hasattr(item, "put"):
            item.put(value)
    return [v for i, v in zip(items, values) if not hasattr(i, "get")]


class Gather:
    def __init__(self, *parts):
        self.right, self.left = [list(parts)], [list(parts)]
        self.hops = 0
        self.least = lax.axis_size("tensor") - 1

    def get(self):
        return [self.right, self.left]

    def put(self, values):
        self.right, self.left = values

    def hop(self):
        count = lax.axis_size("tensor")
        self.hops += 1
        to_right = [(k, k + 1) for k in range(self.hops - 1, count - 1)]
        to_left = [(k, k - 1) for k in range(1, count - self.hops + 1)]
        self.right.append([lax.ppermute(a, "tensor", to_right) for a in self.right[-1]])
        self.left.append([lax.ppermute(a, "tensor", to_left) for a in self.left[-1]])

    def run(self):
        while self.hops < self.least:
            self.hop()
        return self

    def pieces(self, n=0):
        count, place = lax.axis_size("tensor"), lax.axis_index("tensor")
        return [self.right[0][n]] + [
            jnp.where(place + r < count, self.left[r][n], self.right[count - r][n]) for r in range(1, count)
        ]

    def total(self, n=0):
        return sum(a[n] for a in self.right) + sum(a[n] for a in self.left[1:])


class Scatter:
    def __init__(self, make):
        self.make, self.came, self.made = make, [], {}
        self.left = lax.axis_size("tensor") - 1
        self.prepare()

    def prepare(self):
        count = lax.axis_size("tensor")
        for r in (self.left, (count - self.left) % count):
            if r not in self.made:
                self.made[r] = self.make(r)

    def get(self):
        return [self.came, self.made]

    def put(self, values):
        self.came, self.made = values

    def hop(self):
        count = lax.axis_size("tensor")
        sends = [self.made[self.left], self.made[count - self.left]]
        if self.came:
            sends = [s + c.astype(F32) for s, c in zip(sends, self.came)]
        sends = [s.astype(LOW) for s in sends]
        self.came = [
            lax.ppermute(sends[0], "tensor", [(k, k + 1) for k in range(0, count - self.left)]),
            lax.ppermute(sends[1], "tensor", [(k, k - 1) for k in range(self.left, count)]),
        ]
        self.left -= 1
        self.prepare()

    def result(self):
        return self.made[0] + self.came[0].astype(F32) + self.came[1].astype(F32)


def copy_body(turn, in_ref, out_ref):
    out_ref[...] = in_ref[...]


def straighten(array):
    count = lax.axis_size("tensor")
    turn = (jnp.arange(count, dtype=jnp.int32) - lax.axis_index("tensor")) % count
    size = (array.shape[0], array.shape[1] // count)
    return pl.pallas_call(
        copy_body,
        grid_spec=pltpu.PrefetchScalarGridSpec(
            num_scalar_prefetch=1,
            grid=(count,),
            in_specs=[pl.BlockSpec(size, lambda n, t: (0, t[n]))],
            out_specs=pl.BlockSpec(size, lambda n, t: (0, n)),
        ),
        out_shape=shape(array.shape, array.dtype),
        name="straighten",
        compiler_params=BIG,
        cost_estimate=cost(4),
    )(turn, array)


def widen(part):
    return lax.all_gather(part, "tensor", axis=1, tiled=True)


def narrow(part):
    return lax.psum_scatter(part, "tensor", scatter_dimension=1, tiled=True)


def project(left, right):
    return jnp.dot(left, right, preferred_element_type=F32)


def project_back(left, right):
    return jnp.einsum("ti,ji->tj", left, right, preferred_element_type=F32)


def across(left, right):
    return jnp.einsum("it,ij->tj", left, right, preferred_element_type=F32)


def row_sum(values):
    return jnp.sum(values, axis=1, keepdims=True)


def local(
    tokens, doc_lengths, norm1_gain, w_query, w_key, w_value, w_out, norm2_gain, w_gate, w_up, w_down, cotangent,
):
    count, slice_width = tokens.shape
    heads = w_value.shape[1] // HV
    lanes = heads * FEAT
    width = w_query.shape[0]
    begin_here = lax.axis_index("batch") * count
    position = begin_here + jnp.arange(count, dtype=jnp.int32)
    doc_index = jnp.arange(doc_lengths.shape[0], dtype=jnp.int32)
    doc_begins = jnp.sum(jnp.where(doc_index[None, :] < doc_index[:, None], doc_lengths[None, :], 0), axis=1)
    segment = jnp.sum((position[:, None] >= doc_begins[None, :]).astype(jnp.int32), axis=1) - 1
    head_seg, tail_seg = segment[0], segment[-1]
    first_begin = jnp.sum(jnp.where(doc_index == head_seg, doc_begins, 0))
    opened = ((segment == head_seg) & (first_begin < begin_here)).astype(F32)[:, None]
    tail = (segment == tail_seg).astype(F32)[:, None]
    segc, segr = segment[:, None], segment[None, :]
    table = jnp.asarray(feature_table())
    mixer = Mixer(count, heads)

    size, place = lax.axis_size("tensor"), lax.axis_index("tensor")
    half = count // 2
    cut = lambda a: (a[:half], a[half:])
    join = lambda *parts: jnp.concatenate(parts, axis=0)
    c_a, c_b = cut(cotangent)
    w_gate, w_up = w_gate.T, w_up.T
    units = w_gate.shape[0]

    x_full = widen(tokens)
    gains = lax.all_gather(jnp.stack([norm1_gain, norm2_gain]), "tensor", axis=1, tiled=True)
    thin = thin_width(heads)
    w_mix = [w_query, w_key, jnp.zeros((width, thin - 2 * lanes), LOW), w_value]
    w_mix = jnp.concatenate([w for w in w_mix if w.shape[1]], axis=1)
    gather_c = Gather(cotangent)
    x_full, gains, w_mix = lock(x_full, gains, w_mix, gather_c)

    gather_c.hop()
    x_wide = x_full.astype(F32)
    scale_one = lax.rsqrt(row_sum(x_wide * x_wide) / width + EPSILON)
    normed_one = (x_wide * scale_one * gains[0:1]).astype(LOW)
    pair = project(normed_one, w_mix[:, :thin]).astype(LOW)
    q, k, v = pair[:, :lanes], pair[:, lanes : 2 * lanes], project(normed_one, w_value).astype(LOW)
    carry = mixer.state(k, v, tail, table)
    prior = outside(carry, False)
    numer, denom = mixer.inner(q, k, v, segc, segr)
    y, total = mixer.merge(q, numer, denom, *prior, opened, table)
    columns = lambda w, r: lax.dynamic_slice_in_dim(w, ((place + r) % size) * slice_width, slice_width, 1)
    scatter = Scatter(lambda r: project(y, columns(w_out, r)))
    y, total = lock(y, total, gather_c, scatter)
    while scatter.left:
        scatter.hop()
        if gather_c.hops < gather_c.least:
            gather_c.hop()
        lock(scatter, gather_c)
    hidden = tokens.astype(F32) + scatter.result()
    hidden_a, hidden_b = cut(hidden)
    low_a, low_b = cut(hidden.astype(LOW))
    hidden_a, hidden_b, low_a, low_b = lock(hidden_a, hidden_b, low_a, low_b)

    wide_a = widen(low_a)
    c_full = straighten(jnp.concatenate(gather_c.pieces(), axis=1))
    ca_full, cb_full = cut(c_full)
    dinner_a = project_back(w_down, ca_full)
    dinner_b = project_back(w_down, cb_full)
    wide_a, c_full, dinner_a, dinner_b = lock(wide_a, c_full, dinner_a, dinner_b)
    ca_full, cb_full = cut(c_full)

    def feed(wide, dinner):
        wide32 = wide.astype(F32)
        scale = lax.rsqrt(row_sum(wide32 * wide32) / width + EPSILON)
        normed = (wide32 * scale * gains[1:2]).astype(LOW)
        gate = project_back(w_gate, normed)
        up = project_back(w_up, normed)
        sig = jax.nn.sigmoid(gate)
        silu = gate * sig
        inner = (silu * up).astype(LOW)
        dgate = (dinner * up * sig * (1.0 + gate * (1.0 - sig))).astype(LOW)
        dup = (dinner * silu).astype(LOW)
        pulled = (across(dgate, w_gate) + across(dup, w_up)).astype(LOW)
        return scale, normed, inner, dgate, dup, pulled

    wide_b = widen(low_b)
    wide_b, (scale_a, normed_a, inner_a, dgate_a, dup_a, part) = lock(wide_b, feed(wide_a, dinner_a))

    back_a = narrow(part)
    scale_b, normed_b, inner_b, dgate_b, dup_b, part = feed(wide_b, dinner_b)
    groups = [
        [(normed_a, dgate_a), (normed_b, dgate_b)],
        [(normed_a, dup_a), (normed_b, dup_b)],
        [(ca_full, inner_a), (cb_full, inner_b)],
    ]
    ffn = Exchange(grad_blocks("grad_ffn_far", groups, True, None, 16))
    back_a, scale_b, normed_b, inner_b, dgate_b, dup_b, part = lock(
        back_a, scale_b, normed_b, inner_b, dgate_b, dup_b, part, ffn
    )

    def turned(c, scale, back, hidden):
        scaled = scale * back.astype(F32)
        return c.astype(F32) + norm2_gain[None, :] * scaled, jnp.sum(scaled * hidden, axis=0)

    def spread(u, c, wide, scale, local_u, hidden):
        u, wide = u.astype(F32), wide.astype(F32)
        dot = row_sum((u - c.astype(F32)) * wide) * scale * scale / width
        dh = (u - wide * dot).astype(LOW)
        return dh, local_u - hidden * dot, project_back(dh, w_out)

    back_b = narrow(part)
    u_a, gain_a = turned(c_a, scale_a, back_a, hidden_a)
    low_a = u_a.astype(LOW)
    groups = [
        [(normed_a, dgate_a), (normed_b, dgate_b)],
        [(normed_a, dup_a), (normed_b, dup_b)],
        [(ca_full, inner_a), (cb_full, inner_b)],
    ]
    ffn.send()
    ffn.near = grad_blocks("grad_ffn_near", groups, False, None, 16)
    ffn.take()
    ffn.send()
    back_b, u_a, gain_a, low_a, ffn.away, ffn.near = lock(back_b, u_a, gain_a, low_a, ffn.away, ffn.near)

    wide_u = widen(low_a)
    u_b, gain_b = turned(c_b, scale_b, back_b, hidden_b)
    low_b = u_b.astype(LOW)
    parts = [across(m, w_down).astype(LOW) for m in (inner_a, inner_b)]
    wide_u, u_b, gain_b, low_b, parts = lock(wide_u, u_b, gain_b, low_b, parts, ffn)

    wide_v = widen(low_b)
    ffn.take()
    ffn.send()
    dh_a, grad_hidden_a, dy_a = spread(wide_u, ca_full, wide_a, scale_a, u_a, hidden_a)
    ffn.take()
    ffn.send()
    wide_v, dh_a, grad_hidden_a, dy_a, ffn.away, ffn.near = lock(
        wide_v, dh_a, grad_hidden_a, dy_a, ffn.away, ffn.near
    )

    down = narrow(join(*parts))
    dh_b, grad_hidden_b, dy_b = spread(wide_v, cb_full, wide_b, scale_b, u_b, hidden_b)
    wide, dsum, dnorm = mixer.pull_state(q, [dy_a, dy_b], y, total, opened, table)
    ffn.take()
    ffn.send(1)
    wide, dsum, dnorm = lock(wide, dsum, dnorm, ffn)
    following = outside([dsum, dnorm], True)
    dq, dk, dv = mixer.pull_inner(q, k, v, segc, segr, wide, *prior, opened, table)
    following, dq, dk, dv = lock(following, dq, dk, dv, ffn)
    ffn.send()
    dmix = mixer.pull_carry(k, v, tail, *following, dq, dk, dv, table)
    part = project_back(dmix, w_mix).astype(LOW)
    down, part, dmix, dh_b, grad_hidden_b = lock(down, part, dmix, dh_b, grad_hidden_b, ffn)

    back = narrow(part)
    y_a, y_b = cut(y)
    groups = [[(normed_one, dmix.T)], [(dh_a, y_a.T), (dh_b, y_b.T)]]
    ffn.take()
    ffn.send()
    mix = Exchange(grad_blocks("grad_mix_far", groups, True, None, 5))
    mix.send()
    mix.begin("grad_mix_near", groups, 5)
    dot = row_sum(dmix[:, :thin].astype(F32) * pair.astype(F32))
    dot = dot + row_sum(dmix[:, thin:].astype(F32) * v.astype(F32))
    dots = Gather(dot.reshape(count // 128, 128))
    lock(mix, dots, ffn)
    mix.send()
    dots.hop()
    ffn.take()
    final = ffn.run()

    def ffn_weight(n):
        return place_blocks(f"place_ffn_{n}", final, [(units, [(0, units, False)])], width, 7, n)[0]

    grad_w_gate = lock(mix, dots, ffn_weight(0))[0]
    mix.take()
    mix.send()
    dots.hop()
    grad_w_up = lock(mix, dots, ffn_weight(1))[0]
    mix.take()
    mix.send()
    dots.run()
    output = (join(hidden_a, hidden_b) + down.astype(F32)).astype(LOW)
    output = lock(mix, dots, output)[0]
    mix.take()
    mix.send()
    grad_w_down = lock(mix, ffn_weight(2))[0]
    mix.take()
    mix.send()
    back = lock(back, mix)[0]
    inputs, back = tokens.astype(F32), back.astype(F32)
    gain_one = jnp.sum(back * inputs * scale_one, axis=0)
    gain_grads = batch_sum(jnp.stack([gain_one, gain_a + gain_b]))
    grad_tokens = (
        join(grad_hidden_a, grad_hidden_b)
        + scale_one * norm1_gain[None, :] * back
        - inputs * (scale_one * scale_one * dots.total().reshape(count, 1) / width)
    )
    values = heads * HV
    grad_w_query, grad_w_key, grad_w_value, grad_w_out = place_blocks(
        "place_mix",
        mix.run(),
        [
            (thin + values, [(0, lanes, False), (lanes, lanes, False), (thin, values, True)]),
            (values, [(0, values, False)]),
        ],
        width,
        5,
    )
    return (
        output,
        grad_tokens,
        gain_grads[0],
        grad_w_query.T,
        grad_w_key.T,
        grad_w_value,
        grad_w_out,
        gain_grads[1],
        grad_w_gate.T,
        grad_w_up.T,
        grad_w_down,
    )


def solution(mesh):
    rows, cols = P("tensor", None), P(None, "tensor")
    both, one = P("batch", "tensor"), P("tensor")
    in_specs = (both, P(), one, cols, cols, cols, rows, one, cols, cols, rows, both)
    out_specs = (both, both, one, cols, cols, cols, rows, one, cols, cols, rows)
    return jax.shard_map(local, mesh=mesh, in_specs=in_specs, out_specs=out_specs, check_vma=False)
```

```python
import functools
import math

import jax
import jax.numpy as jnp
import numpy as np
from jax import lax
from jax.experimental import pallas as pl
from jax.experimental.pallas import tpu as pltpu
from jax.sharding import PartitionSpec as P

FEAT = 16
HV = 128
EPSILON = 1e-05
WIDE = 256
ROWS = 160
STRIP = 256
CHUNKS = 2
LOW = jnp.bfloat16
F32 = jnp.float32


def feature_table():
    table = np.zeros((8, WIDE), np.float32)
    table[0:2] = -1.0
    at = 0
    for i in range(FEAT + 1):
        for j in range(i, FEAT + 1):
            table[0, at] = i if i < FEAT else -1
            table[1, at] = j if j < FEAT else -1
            table[2, at] = float(i == FEAT)
            table[3, at] = float(j == FEAT)
            table[4, at] = 0.5 if i == j and i < FEAT else 1.0
            at += 1
    return table


def nt(a, b):
    return lax.dot_general(a, b, (((1,), (1,)), ((), ())), preferred_element_type=F32)


def tn(a, b):
    return lax.dot_general(a, b, (((0,), (0,)), ((), ())), preferred_element_type=F32)


def nn(a, b):
    return lax.dot_general(a, b, (((1,), (0,)), ((), ())), preferred_element_type=F32)


def pickers(table, head, lanes):
    lane = lax.broadcasted_iota(jnp.int32, (lanes, WIDE), 0).astype(F32)
    base = (head * FEAT).astype(F32)
    first, second = table[0:1, :], table[1:2, :]
    one = jnp.where((lane == base + first) & (first >= 0), 0.5, 0.0).astype(LOW)
    two = jnp.where((lane == base + second) & (second >= 0), 0.5, 0.0).astype(LOW)
    return one, two


def head_lanes(head, lanes):
    lane = lax.broadcasted_iota(jnp.int32, (1, lanes), 1)
    return (lane >= head * FEAT) & (lane < (head + 1) * FEAT)


def factors(z, table, one, two):
    return nn(z, one) + table[2:3, :], nn(z, two) + table[3:4, :]


def pad_state(state):
    return jnp.concatenate([state, jnp.zeros((WIDE - ROWS, HV), state.dtype)], axis=0)


def state_body(k_ref, v_ref, tail_ref, table_ref, sum_ref, norm_ref):
    head = pl.program_id(0)
    table = table_ref[...]
    one, two = pickers(table, head, k_ref.shape[1])
    left, right = factors(k_ref[...], table, one, two)
    feats = (left * right * table[4:5, :] * tail_ref[...]).astype(LOW)
    sum_ref[0] = tn(feats, v_ref[...])[:ROWS].astype(sum_ref.dtype)
    norm_ref[0] = nn(jnp.ones((8, feats.shape[0]), LOW), feats)


def masked_weights(scores, segc, segr, row0, width):
    rows = scores.shape[0]
    row = row0 + lax.broadcasted_iota(jnp.int32, (rows, width), 0)
    col = lax.broadcasted_iota(jnp.int32, (rows, width), 1)
    return (row >= col) & (segc == segr)


def inner_body(q_ref, k_ref, v_ref, segc_ref, segr_ref, numer_ref, denom_ref):
    head = pl.program_id(0)
    tokens, lanes = q_ref.shape
    mine = head_lanes(head, lanes)
    for row0 in range(0, tokens, STRIP):
        width = row0 + STRIP
        query = jnp.where(mine, q_ref[pl.ds(row0, STRIP), :] * LOW(0.25), LOW(0.0))
        scores = nt(query, k_ref[pl.ds(0, width), :])
        keep = masked_weights(scores, segc_ref[pl.ds(row0, STRIP), :], segr_ref[:, pl.ds(0, width)], row0, width)
        weights = jnp.where(keep, 1.0 + scores * (1.0 + 0.5 * scores), 0.0).astype(LOW)
        wide = jnp.concatenate([v_ref[pl.ds(0, width), :], jnp.ones((width, HV), LOW)], axis=1)
        both = nn(weights, wide)
        numer_ref[pl.ds(row0, STRIP), :] = both[:, :HV]
        denom_ref[pl.ds(row0, STRIP), :] = both[:, HV:]


def merge_body(q_ref, numer_ref, denom_ref, sum_ref, norm_ref, open_ref, table_ref, y_ref, total_ref):
    head = pl.program_id(0)
    table = table_ref[...]
    one, two = pickers(table, head, q_ref.shape[1])
    left, right = factors(q_ref[...], table, one, two)
    feats = (left * right * open_ref[...]).astype(LOW)
    norm = jnp.broadcast_to(norm_ref[0][0:1, :], (HV, WIDE))
    norm_high = norm.astype(LOW)
    norm_rest = (norm - norm_high.astype(F32)).astype(LOW)
    total = denom_ref[...] + nt(feats, norm_high) + nt(feats, norm_rest)
    numer = numer_ref[...] + nn(feats, pad_state(sum_ref[0].astype(LOW)))
    total_ref[...] = total
    y_ref[...] = (numer / total).astype(LOW)


def pull_state_body(q_ref, y_ref, total_ref, open_ref, table_ref, *refs):
    *dy_refs, wide_ref, sum_ref, norm_ref = refs
    head = pl.program_id(0)
    table = table_ref[...]
    one, two = pickers(table, head, q_ref.shape[1])
    left, right = factors(q_ref[...], table, one, two)
    feats = (left * right * open_ref[...]).astype(LOW)
    inverse = 1.0 / total_ref[...]
    dy = jnp.concatenate([r[...] for r in dy_refs], axis=0)
    dnumer = (dy * inverse).astype(LOW)
    ddenom = -jnp.sum(dy * y_ref[...].astype(F32), axis=1, keepdims=True) * inverse
    ddenom = jnp.where(lax.broadcasted_iota(jnp.int32, ddenom.shape, 1) < 8, ddenom, 0.0).astype(LOW)
    wide_ref[...] = jnp.concatenate([dnumer, ddenom], axis=1)
    sum_ref[0] = tn(feats, dnumer)[:ROWS].astype(sum_ref.dtype)
    norm_ref[0] = tn(ddenom, feats)[:8]


def pull_inner_body(
    q_ref, k_ref, v_ref, segc_ref, segr_ref, wide_ref, sum_ref, norm_ref, open_ref, table_ref,
    dq_ref, dk_ref, dv_ref, dq_acc, dk_acc,
):
    head = pl.program_id(0)
    last = pl.num_programs(0) - 1
    tokens, lanes = q_ref.shape
    mine = head_lanes(head, lanes)

    @pl.when(head == 0)
    def _():
        dq_acc[...] = jnp.zeros_like(dq_acc)
        dk_acc[...] = jnp.zeros_like(dk_acc)

    dv_ref[...] = jnp.zeros_like(dv_ref)
    table = table_ref[...]
    one, two = pickers(table, head, lanes)
    state = pad_state(sum_ref[0].astype(LOW))
    norm = norm_ref[0][0:1, :]
    single = (lax.broadcasted_iota(jnp.int32, (1, HV), 1) < 1).astype(LOW)
    for row0 in range(0, tokens, STRIP):
        width = row0 + STRIP
        rows = pl.ds(row0, STRIP)
        query = jnp.where(mine, q_ref[rows, :] * LOW(0.25), LOW(0.0))
        keys = jnp.where(mine, k_ref[pl.ds(0, width), :] * LOW(0.25), LOW(0.0))
        scores = nt(query, k_ref[pl.ds(0, width), :])
        keep = masked_weights(scores, segc_ref[rows, :], segr_ref[:, pl.ds(0, width)], row0, width)
        weights = jnp.where(keep, 1.0 + scores * (1.0 + 0.5 * scores), 0.0).astype(LOW)
        dwide = wide_ref[rows, :]
        ones = jnp.broadcast_to(single, (width, HV))
        wide = jnp.concatenate([v_ref[pl.ds(0, width), :], ones], axis=1)
        dscores = jnp.where(keep, nt(dwide, wide) * (1.0 + scores), 0.0).astype(LOW)
        dv_ref[pl.ds(0, width), :] += tn(weights, dwide[:, :HV])
        dk_acc[pl.ds(0, width), :] += tn(dscores, query)
        left, right = factors(q_ref[rows, :], table, one, two)
        pulled = nt(dwide[:, :HV], state) + dwide[:, HV : HV + 1].astype(F32) * norm
        pulled = pulled * open_ref[rows, :]
        dq_acc[rows, :] += nn(dscores, keys) + nt((pulled * right).astype(LOW), one) + nt((pulled * left).astype(LOW), two)

    @pl.when(head == last)
    def _():
        dq_ref[...] = dq_acc[...].astype(dq_ref.dtype)
        dk_ref[...] = dk_acc[...]


def thin_width(heads):
    return -(-2 * heads * FEAT // HV) * HV


def pull_carry_body(k_ref, v_ref, tail_ref, sum_ref, norm_ref, dq_ref, dk_ref, dv_ref, table_ref, out_ref, dk_acc):
    head = pl.program_id(0)
    tokens, lanes = k_ref.shape
    start = 2 * lanes + -2 * lanes % HV

    @pl.when(head == 0)
    def _():
        dk_acc[...] = dk_ref[...]

    table = table_ref[...]
    one, two = pickers(table, head, lanes)
    left, right = factors(k_ref[...], table, one, two)
    scale = table[4:5, :] * tail_ref[...]
    state = pad_state(sum_ref[0].astype(LOW))
    dv = dv_ref[...] + nn((left * right * scale).astype(LOW), state)
    out_ref[:, pl.ds(pl.multiple_of(start + head * HV, HV), HV)] = dv.astype(out_ref.dtype)
    pulled = (nt(v_ref[...], state) + norm_ref[0][0:1, :]) * scale
    dk_acc[...] += nt((pulled * right).astype(LOW), one) + nt((pulled * left).astype(LOW), two)

    @pl.when(head == pl.num_programs(0) - 1)
    def _():
        thin = [dq_ref[...], dk_acc[...].astype(out_ref.dtype)]
        if start > 2 * lanes:
            thin.append(jnp.zeros((tokens, start - 2 * lanes), out_ref.dtype))
        out_ref[:, :start] = jnp.concatenate(thin, axis=1)


def shape(dims, kind):
    return jax.ShapeDtypeStruct(dims, kind)


class Mixer:
    def __init__(self, tokens, heads):
        self.tokens, self.heads = tokens, heads
        lanes = heads * FEAT
        self.full = lambda a, b: pl.BlockSpec((a, b), lambda h: (0, 0))
        self.thin = self.full(tokens, lanes)
        self.column = self.full(tokens, 1)
        self.row = self.full(1, tokens)
        self.table = self.full(8, WIDE)
        self.head = pl.BlockSpec((tokens, HV), lambda h: (0, h))
        self.pair = pl.BlockSpec((tokens, 2 * HV), lambda h: (0, h))
        self.sum = pl.BlockSpec((1, ROWS, HV), lambda h: (h, 0, 0))
        self.norm = pl.BlockSpec((1, 8, WIDE), lambda h: (h, 0, 0))
        self.thin_shape = lambda kind: shape((tokens, lanes), kind)
        self.head_shape = lambda kind: shape((tokens, heads * HV), kind)
        self.state_shapes = [shape((heads, ROWS, HV), F32), shape((heads, 8, WIDE), F32)]
        self.acc = pltpu.VMEM((tokens, lanes), F32)

    def call(self, body, name, in_specs, out_specs, out_shape, scratch, micros, *args):
        return pl.pallas_call(
            body,
            grid=(self.heads,),
            in_specs=in_specs,
            out_specs=out_specs,
            out_shape=out_shape,
            scratch_shapes=scratch,
            name=name,
            compiler_params=pltpu.CompilerParams(
                dimension_semantics=("arbitrary",), vmem_limit_bytes=48 * 1024 * 1024
            ),
            cost_estimate=pl.CostEstimate(
                flops=int(micros * 1e-6 * 1e15), bytes_accessed=1 << 20, transcendentals=0
            ),
        )(*args)

    def state(self, k, v, tail, table):
        return self.call(
            state_body, "mix_state", [self.thin, self.head, self.column, self.table],
            [self.sum, self.norm], self.state_shapes, [], 4, k, v, tail, table,
        )

    def inner(self, q, k, v, segc, segr):
        return self.call(
            inner_body, "mix_inner", [self.thin, self.thin, self.head, self.column, self.row],
            [self.head, self.head], [self.head_shape(F32)] * 2, [], 10, q, k, v, segc, segr,
        )

    def merge(self, q, numer, denom, total, norm, opened, table):
        return self.call(
            merge_body, "mix_merge",
            [self.thin, self.head, self.head, self.sum, self.norm, self.column, self.table],
            [self.head, self.head], [self.head_shape(LOW), self.head_shape(F32)], [], 5,
            q, numer, denom, total, norm, opened, table,
        )

    def pull_state(self, q, dy, y, total, opened, table):
        return self.call(
            pull_state_body, "mix_pull_state",
            [self.thin, self.head, self.head, self.column, self.table]
            + [pl.BlockSpec((d.shape[0], HV), lambda h: (0, h)) for d in dy],
            [self.pair, self.sum, self.norm],
            [shape((self.tokens, self.heads * 2 * HV), LOW)] + self.state_shapes, [], 5,
            q, y, total, opened, table, *dy,
        )

    def pull_inner(self, q, k, v, segc, segr, wide, total, norm, opened, table):
        return self.call(
            pull_inner_body, "mix_pull_inner",
            [self.thin, self.thin, self.head, self.column, self.row, self.pair, self.sum, self.norm, self.column, self.table],
            [self.thin, self.thin, self.head],
            [self.thin_shape(LOW), self.thin_shape(F32), self.head_shape(F32)],
            [self.acc, self.acc], 20, q, k, v, segc, segr, wide, total, norm, opened, table,
        )

    def pull_carry(self, k, v, tail, total, norm, dq, dk, dv, table):
        width = thin_width(self.heads) + self.heads * HV
        return self.call(
            pull_carry_body, "mix_pull_carry",
            [self.thin, self.head, self.column, self.sum, self.norm, self.thin, self.thin, self.head, self.table],
            self.full(self.tokens, width), shape((self.tokens, width), LOW), [self.acc], 6,
            k, v, tail, total, norm, dq, dk, dv, table,
        )


def outside(part, reverse):
    count, place = lax.axis_size("batch"), lax.axis_index("batch")
    total = list(part)
    before = [jnp.zeros_like(a) for a in part]
    bit = 1
    while bit < count:
        pairs = [(i, i ^ bit) for i in range(count)]
        low = total[0].astype(LOW)
        other = [lax.ppermute(low, "batch", pairs).astype(F32), lax.ppermute(total[1], "batch", pairs)]
        upper = (place & bit) != 0
        take = jnp.logical_not(upper) if reverse else upper
        before = [a + jnp.where(take, b, 0.0) for a, b in zip(before, other)]
        total = [a + b for a, b in zip(total, other)]
        bit *= 2
    return before


def padded(width):
    return -(-width // 16) * 16


def batch_orders():
    count = lax.axis_size("batch")
    bits = [1 << b for b in range(count.bit_length() - 1)]
    return bits[:1] + bits[1:], bits[:1] + bits[:0:-1]


def block_order():
    count = lax.axis_size("batch")
    first, second = batch_orders()
    relative, places = [], []
    for step in range(count):
        at = sum(bit for n, bit in enumerate(first) if step >> (len(first) - 1 - n) & 1)
        relative.append(at)
        places.append(sum(1 << (len(second) - 1 - n) for n, bit in enumerate(second) if at & bit))
    blocks = jnp.asarray(np.array(relative, np.int32)) ^ lax.axis_index("batch").astype(jnp.int32)
    return blocks, places


def cost(micros):
    return pl.CostEstimate(flops=int(micros * 1e9), bytes_accessed=1 << 20, transcendentals=0)


BIG = pltpu.CompilerParams(dimension_semantics=("arbitrary",), vmem_limit_bytes=56 * 1024 * 1024)


def grad_values(refs, groups):
    values = []
    for rows, parts in groups:
        value = None
        for _ in range(parts):
            term = nn(refs[1][...], refs[0][...])
            refs = refs[2:]
            value = term if value is None else value + term
        values.append(value)
    return values


def grad_body(blocks, swap, *refs, groups, summed):
    step = pl.program_id(0)
    places = (step, swap[0, step])
    middle = pl.num_programs(0) // 2
    sources = 2 * sum(parts for _, parts in groups)
    values = grad_values(list(refs[:sources]), groups)
    outs = refs[-4:]
    came = refs[sources:-4]
    at = 0
    for (rows, _), value in zip(groups, values):
        size = padded(rows // 2)
        for n in range(2):
            half = value[n * rows // 2 : (n + 1) * rows // 2]
            if size > rows // 2:
                half = jnp.concatenate([half, jnp.zeros((size - rows // 2, half.shape[1]), F32)], axis=0)
            span = slice(at, at + size)
            if summed:
                other = jnp.where(places[n] < middle, came[n][0, span, :], came[2 + n][0, span, :])
                half = half + other.astype(F32)
            half = half.astype(LOW)

            @pl.when(places[n] < middle)
            def _():
                outs[n][0, span, :] = half

            @pl.when(places[n] >= middle)
            def _():
                outs[2 + n][0, span, :] = half

        at += size


def grad_blocks(name, groups, far, came, micros):
    count = lax.axis_size("batch")
    split = count // 2
    width = groups[0][0][0].shape[1]
    columns = width // count
    blocks, places = block_order()
    base = split if far else 0
    in_specs, operands, kinds, rows = [], [], [], 0
    for parts in groups:
        for left, right in parts:
            in_specs.append(pl.BlockSpec((left.shape[0], columns), lambda s, b, w: (0, b[s])))
            in_specs.append(pl.BlockSpec(right.shape, lambda s, b, w: (0, 0)))
            operands += [left, right]
        kinds.append((parts[0][1].shape[0], len(parts)))
        rows += padded(parts[0][1].shape[0] // 2)
    size = (1, rows, columns)
    places = [p - base for p in places[base : base + split]]
    table, specs = [places], []
    for low in (0, split // 2):
        for order in (list(range(split)), places):
            uses = [(s, p - low) for s, p in enumerate(order) if low <= p < low + split // 2]
            table.append([([at for when, at in uses if when <= s] or [uses[0][1]])[-1] for s in range(split)])
            specs.append(pl.BlockSpec(size, lambda s, b, w, n=len(table) - 1: (w[n, s], 0, 0)))
    if came:
        in_specs += specs
        operands += came
    outs = pl.pallas_call(
        functools.partial(grad_body, groups=tuple(kinds), summed=bool(came)),
        grid_spec=pltpu.PrefetchScalarGridSpec(
            num_scalar_prefetch=2, grid=(split,), in_specs=in_specs, out_specs=specs
        ),
        out_shape=[shape((split // 2, rows, columns), LOW)] * 4,
        name=name,
        compiler_params=BIG,
        cost_estimate=cost(micros),
    )(blocks[base : base + split], jnp.asarray(np.array(table, np.int32)), *operands)
    return outs[:2], outs[2:]


def flip(value, bit):
    return lax.ppermute(value, "batch", [(i, i ^ bit) for i in range(lax.axis_size("batch"))])


def added(one, other):
    return (one.astype(F32) + other.astype(F32)).astype(LOW)


class Exchange:
    def __init__(self, far):
        self.orders = batch_orders()
        self.steps = len(self.orders[0])
        self.away, self.near, self.came = [list(f) for f in zip(*far)], None, [[], []]
        self.step = 0

    def get(self):
        return [self.away, self.near, self.came]

    def put(self, values):
        self.away, self.near, self.came = values

    def send(self, limit=None):
        n = self.step
        if n == 2 * self.steps:
            return
        for half, order in enumerate(self.orders):
            bit = order[n if n < self.steps else 2 * self.steps - 1 - n]
            first = len(self.came[half])
            last = len(self.away[half]) if limit is None else first + limit
            self.came[half] += [flip(a, bit) for a in self.away[half][first:last]]

    def begin(self, name, groups, micros):
        self.near, away = grad_blocks(name, groups, False, [c[n] for n in range(2) for c in self.came], micros)
        self.away, self.came, self.step = [[a] for a in away], [[], []], 1

    def take(self):
        n = self.step
        if n == 2 * self.steps:
            return
        self.step += 1
        if n == 0:
            self.near, away = [[added(b, c[m]) for b, c in zip(half, self.came)] for m, half in enumerate(self.near)]
            self.away = [[a] for a in away]
        elif n < self.steps:
            half = self.near[0].shape[0] // 2
            pairs = [(k, c[0]) for k, c in zip(self.near, self.came)]
            if half:
                self.away = [[added(k[half:], c[half:])] for k, c in pairs]
                self.near = [added(k[:half], c[:half]) for k, c in pairs]
            else:
                self.near = [added(k, c) for k, c in pairs]
                self.away = [[k] for k in self.near]
        else:
            self.away = [a + c for a, c in zip(self.away, self.came)]
        self.came = [[], []]

    def run(self):
        while self.step < 2 * self.steps:
            self.send()
            self.take()
        return self.away


def place_body(blocks, table, *refs, outs, count):
    step = pl.program_id(0)
    pieces = count
    chosen = []
    for n in range(2):
        which = table[n, step]
        group = refs[n * pieces : (n + 1) * pieces]
        value = group[0][0]
        for m in range(1, pieces):
            value = jnp.where(which == m, group[m][0], value)
        chosen.append(value)
    results = refs[2 * pieces :]
    for start, rows, targets in outs:
        both = jnp.concatenate([c[start : start + rows // 2].astype(F32) for c in chosen], axis=0)
        for index, first, size, turned in targets:
            part = both[first : first + size]
            results[index][...] = part.T if turned else part


def place_blocks(name, pieces, outs, width, micros, part=None):
    count = lax.axis_size("batch")
    columns = width // count
    blocks, places = block_order()
    table = np.array([list(range(count)), places], np.int32)
    size = pieces[0][0].shape[1:]
    if part is not None:
        size = (padded(outs[0][0] // 2), size[1])
    piece = pl.BlockSpec((1,) + size, lambda s, b, t: (0, part or 0, 0), pipeline_mode=pl.Buffered(1))
    out_specs, out_shape, layout, start = [], [], [], 0
    for rows, targets in outs:
        listed = []
        for first, used, turned in targets:
            listed.append((len(out_shape), first, used, turned))
            if turned:
                out_specs.append(pl.BlockSpec((columns, used), lambda s, b, t: (b[s], 0)))
                out_shape.append(shape((width, used), F32))
            else:
                out_specs.append(pl.BlockSpec((used, columns), lambda s, b, t: (0, b[s])))
                out_shape.append(shape((used, width), F32))
        layout.append((start, rows, tuple(listed)))
        start += padded(rows // 2)
    return pl.pallas_call(
        functools.partial(place_body, outs=tuple(layout), count=count),
        grid_spec=pltpu.PrefetchScalarGridSpec(
            num_scalar_prefetch=2,
            grid=(count,),
            in_specs=[piece] * (2 * count),
            out_specs=out_specs,
        ),
        out_shape=out_shape,
        name=name,
        compiler_params=BIG,
        cost_estimate=cost(micros),
    )(blocks, jnp.asarray(table), *pieces[0], *pieces[1])


def line_sum(value):
    count = lax.axis_size("tensor")
    turned = [lax.ppermute(value, "tensor", [(i, (i + n) % count) for i in range(count)]) for n in range(1, count)]
    return [value] + turned


def batch_sum(value):
    value = value + flip(value, 1)
    return value + sum(flip(value, mask) for mask in range(2, lax.axis_size("batch"), 2))


def after(values, *others):
    return lax.optimization_barrier((values, others))[0]


def lock(*items):
    values = lax.optimization_barrier([i.get() if hasattr(i, "get") else i for i in items])
    for item, value in zip(items, values):
        if hasattr(item, "put"):
            item.put(value)
    return [v for i, v in zip(items, values) if not hasattr(i, "get")]


class Gather:
    def __init__(self, *parts):
        self.right, self.left = [list(parts)], [list(parts)]
        self.hops = 0
        self.least = lax.axis_size("tensor") - 1

    def get(self):
        return [self.right, self.left]

    def put(self, values):
        self.right, self.left = values

    def hop(self):
        count = lax.axis_size("tensor")
        self.hops += 1
        to_right = [(k, k + 1) for k in range(self.hops - 1, count - 1)]
        to_left = [(k, k - 1) for k in range(1, count - self.hops + 1)]
        self.right.append([lax.ppermute(a, "tensor", to_right) for a in self.right[-1]])
        self.left.append([lax.ppermute(a, "tensor", to_left) for a in self.left[-1]])

    def run(self):
        while self.hops < self.least:
            self.hop()
        return self

    def pieces(self, n=0):
        count, place = lax.axis_size("tensor"), lax.axis_index("tensor")
        return [self.right[0][n]] + [
            jnp.where(place + r < count, self.left[r][n], self.right[count - r][n]) for r in range(1, count)
        ]

    def total(self, n=0):
        return sum(a[n] for a in self.right) + sum(a[n] for a in self.left[1:])


class Scatter:
    def __init__(self, make):
        self.make, self.came, self.made = make, [], {}
        self.left = lax.axis_size("tensor") - 1
        self.prepare()

    def prepare(self):
        count = lax.axis_size("tensor")
        for r in (self.left, (count - self.left) % count):
            if r not in self.made:
                self.made[r] = self.make(r)

    def get(self):
        return [self.came, self.made]

    def put(self, values):
        self.came, self.made = values

    def hop(self):
        count = lax.axis_size("tensor")
        sends = [self.made[self.left], self.made[count - self.left]]
        if self.came:
            sends = [s + c.astype(F32) for s, c in zip(sends, self.came)]
        sends = [s.astype(LOW) for s in sends]
        self.came = [
            lax.ppermute(sends[0], "tensor", [(k, k + 1) for k in range(0, count - self.left)]),
            lax.ppermute(sends[1], "tensor", [(k, k - 1) for k in range(self.left, count)]),
        ]
        self.left -= 1
        self.prepare()

    def result(self):
        return self.made[0] + self.came[0].astype(F32) + self.came[1].astype(F32)


def copy_body(turn, in_ref, out_ref):
    out_ref[...] = in_ref[...]


def straighten(array):
    count = lax.axis_size("tensor")
    turn = (jnp.arange(count, dtype=jnp.int32) - lax.axis_index("tensor")) % count
    size = (array.shape[0], array.shape[1] // count)
    return pl.pallas_call(
        copy_body,
        grid_spec=pltpu.PrefetchScalarGridSpec(
            num_scalar_prefetch=1,
            grid=(count,),
            in_specs=[pl.BlockSpec(size, lambda n, t: (0, t[n]))],
            out_specs=pl.BlockSpec(size, lambda n, t: (0, n)),
        ),
        out_shape=shape(array.shape, array.dtype),
        name="straighten",
        compiler_params=BIG,
        cost_estimate=cost(4),
    )(turn, array)


def widen(part):
    return lax.all_gather(part, "tensor", axis=1, tiled=True)


def narrow(part):
    return lax.psum_scatter(part, "tensor", scatter_dimension=1, tiled=True)


def project(left, right):
    return jnp.dot(left, right, preferred_element_type=F32)


def project_back(left, right):
    return jnp.einsum("ti,ji->tj", left, right, preferred_element_type=F32)


def across(left, right):
    return jnp.einsum("it,ij->tj", left, right, preferred_element_type=F32)


def row_sum(values):
    return jnp.sum(values, axis=1, keepdims=True)


def local(
    tokens, doc_lengths, norm1_gain, w_query, w_key, w_value, w_out, norm2_gain, w_gate, w_up, w_down, cotangent,
):
    count, slice_width = tokens.shape
    heads = w_value.shape[1] // HV
    lanes = heads * FEAT
    width = w_query.shape[0]
    begin_here = lax.axis_index("batch") * count
    position = begin_here + jnp.arange(count, dtype=jnp.int32)
    doc_index = jnp.arange(doc_lengths.shape[0], dtype=jnp.int32)
    doc_begins = jnp.sum(jnp.where(doc_index[None, :] < doc_index[:, None], doc_lengths[None, :], 0), axis=1)
    segment = jnp.sum((position[:, None] >= doc_begins[None, :]).astype(jnp.int32), axis=1) - 1
    head_seg, tail_seg = segment[0], segment[-1]
    first_begin = jnp.sum(jnp.where(doc_index == head_seg, doc_begins, 0))
    opened = ((segment == head_seg) & (first_begin < begin_here)).astype(F32)[:, None]
    tail = (segment == tail_seg).astype(F32)[:, None]
    segc, segr = segment[:, None], segment[None, :]
    table = jnp.asarray(feature_table())
    mixer = Mixer(count, heads)

    size, place = lax.axis_size("tensor"), lax.axis_index("tensor")
    half = count // 2
    cut = lambda a: (a[:half], a[half:])
    join = lambda *parts: jnp.concatenate(parts, axis=0)
    c_a, c_b = cut(cotangent)
    w_gate, w_up = w_gate.T, w_up.T
    units = w_gate.shape[0]

    x_full = widen(tokens)
    gains = lax.all_gather(jnp.stack([norm1_gain, norm2_gain]), "tensor", axis=1, tiled=True)
    thin = thin_width(heads)
    w_mix = [w_query, w_key, jnp.zeros((width, thin - 2 * lanes), LOW), w_value]
    w_mix = jnp.concatenate([w for w in w_mix if w.shape[1]], axis=1)
    gather_c = Gather(cotangent)
    x_full, gains, w_mix = lock(x_full, gains, w_mix, gather_c)

    gather_c.hop()
    x_wide = x_full.astype(F32)
    scale_one = lax.rsqrt(row_sum(x_wide * x_wide) / width + EPSILON)
    normed_one = (x_wide * scale_one * gains[0:1]).astype(LOW)
    pair = project(normed_one, w_mix[:, :thin]).astype(LOW)
    q, k, v = pair[:, :lanes], pair[:, lanes : 2 * lanes], project(normed_one, w_value).astype(LOW)
    carry = mixer.state(k, v, tail, table)
    prior = outside(carry, False)
    numer, denom = mixer.inner(q, k, v, segc, segr)
    y, total = mixer.merge(q, numer, denom, *prior, opened, table)
    columns = lambda w, r: lax.dynamic_slice_in_dim(w, ((place + r) % size) * slice_width, slice_width, 1)
    scatter = Scatter(lambda r: project(y, columns(w_out, r)))
    y, total = lock(y, total, gather_c, scatter)
    while scatter.left:
        scatter.hop()
        if gather_c.hops < gather_c.least:
            gather_c.hop()
        lock(scatter, gather_c)
    hidden = tokens.astype(F32) + scatter.result()
    hidden_a, hidden_b = cut(hidden)
    low_a, low_b = cut(hidden.astype(LOW))
    hidden_a, hidden_b, low_a, low_b = lock(hidden_a, hidden_b, low_a, low_b)

    wide_a = widen(low_a)
    c_full = straighten(jnp.concatenate(gather_c.pieces(), axis=1))
    ca_full, cb_full = cut(c_full)
    dinner_a = project_back(w_down, ca_full)
    dinner_b = project_back(w_down, cb_full)
    wide_a, c_full, dinner_a, dinner_b = lock(wide_a, c_full, dinner_a, dinner_b)
    ca_full, cb_full = cut(c_full)

    def feed(wide, dinner):
        wide32 = wide.astype(F32)
        scale = lax.rsqrt(row_sum(wide32 * wide32) / width + EPSILON)
        normed = (wide32 * scale * gains[1:2]).astype(LOW)
        gate = project_back(w_gate, normed)
        up = project_back(w_up, normed)
        sig = jax.nn.sigmoid(gate)
        silu = gate * sig
        inner = (silu * up).astype(LOW)
        dgate = (dinner * up * sig * (1.0 + gate * (1.0 - sig))).astype(LOW)
        dup = (dinner * silu).astype(LOW)
        pulled = (across(dgate, w_gate) + across(dup, w_up)).astype(LOW)
        return scale, normed, inner, dgate, dup, pulled

    wide_b = widen(low_b)
    wide_b, (scale_a, normed_a, inner_a, dgate_a, dup_a, part) = lock(wide_b, feed(wide_a, dinner_a))

    back_a = narrow(part)
    scale_b, normed_b, inner_b, dgate_b, dup_b, part = feed(wide_b, dinner_b)
    groups = [
        [(normed_a, dgate_a), (normed_b, dgate_b)],
        [(normed_a, dup_a), (normed_b, dup_b)],
        [(ca_full, inner_a), (cb_full, inner_b)],
    ]
    ffn = Exchange(grad_blocks("grad_ffn_far", groups, True, None, 16))
    back_a, scale_b, normed_b, inner_b, dgate_b, dup_b, part = lock(
        back_a, scale_b, normed_b, inner_b, dgate_b, dup_b, part, ffn
    )

    def turned(c, scale, back, hidden):
        scaled = scale * back.astype(F32)
        return c.astype(F32) + norm2_gain[None, :] * scaled, jnp.sum(scaled * hidden, axis=0)

    def spread(u, c, wide, scale, local_u, hidden):
        u, wide = u.astype(F32), wide.astype(F32)
        dot = row_sum((u - c.astype(F32)) * wide) * scale * scale / width
        dh = (u - wide * dot).astype(LOW)
        return dh, local_u - hidden * dot, project_back(dh, w_out)

    back_b = narrow(part)
    u_a, gain_a = turned(c_a, scale_a, back_a, hidden_a)
    low_a = u_a.astype(LOW)
    groups = [
        [(normed_a, dgate_a), (normed_b, dgate_b)],
        [(normed_a, dup_a), (normed_b, dup_b)],
        [(ca_full, inner_a), (cb_full, inner_b)],
    ]
    ffn.send()
    ffn.near = grad_blocks("grad_ffn_near", groups, False, None, 16)
    ffn.take()
    ffn.send()
    back_b, u_a, gain_a, low_a, ffn.away, ffn.near = lock(back_b, u_a, gain_a, low_a, ffn.away, ffn.near)

    wide_u = widen(low_a)
    u_b, gain_b = turned(c_b, scale_b, back_b, hidden_b)
    low_b = u_b.astype(LOW)
    parts = [across(m, w_down).astype(LOW) for m in (inner_a, inner_b)]
    wide_u, u_b, gain_b, low_b, parts = lock(wide_u, u_b, gain_b, low_b, parts, ffn)

    wide_v = widen(low_b)
    ffn.take()
    ffn.send()
    dh_a, grad_hidden_a, dy_a = spread(wide_u, ca_full, wide_a, scale_a, u_a, hidden_a)
    ffn.take()
    ffn.send()
    wide_v, dh_a, grad_hidden_a, dy_a, ffn.away, ffn.near = lock(
        wide_v, dh_a, grad_hidden_a, dy_a, ffn.away, ffn.near
    )

    down = narrow(join(*parts))
    dh_b, grad_hidden_b, dy_b = spread(wide_v, cb_full, wide_b, scale_b, u_b, hidden_b)
    wide, dsum, dnorm = mixer.pull_state(q, [dy_a, dy_b], y, total, opened, table)
    ffn.take()
    ffn.send(1)
    wide, dsum, dnorm = lock(wide, dsum, dnorm, ffn)
    following = outside([dsum, dnorm], True)
    dq, dk, dv = mixer.pull_inner(q, k, v, segc, segr, wide, *prior, opened, table)
    following, dq, dk, dv = lock(following, dq, dk, dv, ffn)
    ffn.send()
    dmix = mixer.pull_carry(k, v, tail, *following, dq, dk, dv, table)
    part = project_back(dmix, w_mix).astype(LOW)
    dot = row_sum(dmix[:, :thin].astype(F32) * pair.astype(F32))
    dot = dot + row_sum(dmix[:, thin:].astype(F32) * v.astype(F32))
    dots = line_sum(dot.reshape(count // 128, 128))
    down, part, dmix, dh_b, grad_hidden_b, dots = lock(down, part, dmix, dh_b, grad_hidden_b, dots, ffn)

    back = narrow(part)
    y_a, y_b = cut(y)
    groups = [[(normed_one, dmix.T)], [(dh_a, y_a.T), (dh_b, y_b.T)]]
    ffn.take()
    ffn.send()
    mix = Exchange(grad_blocks("grad_mix_far", groups, True, None, 5))
    mix.send()
    mix.begin("grad_mix_near", groups, 5)
    lock(mix, ffn)
    mix.send()
    ffn.take()
    final = ffn.run()

    def ffn_weight(n):
        return place_blocks(f"place_ffn_{n}", final, [(units, [(0, units, False)])], width, 7, n)[0]

    grad_w_gate = lock(mix, ffn_weight(0))[0]
    mix.take()
    mix.send()
    grad_w_up = lock(mix, ffn_weight(1))[0]
    mix.take()
    mix.send()
    output = (join(hidden_a, hidden_b) + down.astype(F32)).astype(LOW)
    output = lock(mix, output)[0]
    mix.take()
    mix.send()
    grad_w_down = lock(mix, ffn_weight(2))[0]
    mix.take()
    mix.send()
    back = lock(back, mix)[0]
    inputs, back = tokens.astype(F32), back.astype(F32)
    gain_one = jnp.sum(back * inputs * scale_one, axis=0)
    gain_grads = batch_sum(jnp.stack([gain_one, gain_a + gain_b]))
    grad_tokens = (
        join(grad_hidden_a, grad_hidden_b)
        + scale_one * norm1_gain[None, :] * back
        - inputs * (scale_one * scale_one * sum(dots).reshape(count, 1) / width)
    )
    values = heads * HV
    grad_w_query, grad_w_key, grad_w_value, grad_w_out = place_blocks(
        "place_mix",
        mix.run(),
        [
            (thin + values, [(0, lanes, False), (lanes, lanes, False), (thin, values, True)]),
            (values, [(0, values, False)]),
        ],
        width,
        5,
    )
    return (
        output,
        grad_tokens,
        gain_grads[0],
        grad_w_query.T,
        grad_w_key.T,
        grad_w_value,
        grad_w_out,
        gain_grads[1],
        grad_w_gate.T,
        grad_w_up.T,
        grad_w_down,
    )


def solution(mesh):
    rows, cols = P("tensor", None), P(None, "tensor")
    both, one = P("batch", "tensor"), P("tensor")
    in_specs = (both, P(), one, cols, cols, cols, rows, one, cols, cols, rows, both)
    out_specs = (both, both, one, cols, cols, cols, rows, one, cols, cols, rows)
    return jax.shard_map(local, mesh=mesh, in_specs=in_specs, out_specs=out_specs, check_vma=False)
```

```python
import functools
import math

import jax
import jax.numpy as jnp
import numpy as np
from jax import lax
from jax.experimental import pallas as pl
from jax.experimental.pallas import tpu as pltpu
from jax.sharding import PartitionSpec as P

FEAT = 16
HV = 128
EPSILON = 1e-05
WIDE = 256
ROWS = 160
STRIP = 256
CHUNKS = 2
LOW = jnp.bfloat16
F32 = jnp.float32


def feature_table():
    table = np.zeros((8, WIDE), np.float32)
    table[0:2] = -1.0
    at = 0
    for i in range(FEAT + 1):
        for j in range(i, FEAT + 1):
            table[0, at] = i if i < FEAT else -1
            table[1, at] = j if j < FEAT else -1
            table[2, at] = float(i == FEAT)
            table[3, at] = float(j == FEAT)
            table[4, at] = 0.5 if i == j and i < FEAT else 1.0
            at += 1
    return table


def nt(a, b):
    return lax.dot_general(a, b, (((1,), (1,)), ((), ())), preferred_element_type=F32)


def tn(a, b):
    return lax.dot_general(a, b, (((0,), (0,)), ((), ())), preferred_element_type=F32)


def nn(a, b):
    return lax.dot_general(a, b, (((1,), (0,)), ((), ())), preferred_element_type=F32)


def pickers(table, head, lanes):
    lane = lax.broadcasted_iota(jnp.int32, (lanes, WIDE), 0).astype(F32)
    base = (head * FEAT).astype(F32)
    first, second = table[0:1, :], table[1:2, :]
    one = jnp.where((lane == base + first) & (first >= 0), 0.5, 0.0).astype(LOW)
    two = jnp.where((lane == base + second) & (second >= 0), 0.5, 0.0).astype(LOW)
    return one, two


def head_lanes(head, lanes):
    lane = lax.broadcasted_iota(jnp.int32, (1, lanes), 1)
    return (lane >= head * FEAT) & (lane < (head + 1) * FEAT)


def factors(z, table, one, two):
    return nn(z, one) + table[2:3, :], nn(z, two) + table[3:4, :]


def pad_state(state):
    return jnp.concatenate([state, jnp.zeros((WIDE - ROWS, HV), state.dtype)], axis=0)


def state_body(k_ref, v_ref, tail_ref, table_ref, sum_ref, norm_ref):
    head = pl.program_id(0)
    table = table_ref[...]
    one, two = pickers(table, head, k_ref.shape[1])
    left, right = factors(k_ref[...], table, one, two)
    feats = (left * right * table[4:5, :] * tail_ref[...]).astype(LOW)
    sum_ref[0] = tn(feats, v_ref[...])[:ROWS].astype(sum_ref.dtype)
    norm_ref[0] = nn(jnp.ones((8, feats.shape[0]), LOW), feats)


def masked_weights(scores, segc, segr, row0, width):
    rows = scores.shape[0]
    row = row0 + lax.broadcasted_iota(jnp.int32, (rows, width), 0)
    col = lax.broadcasted_iota(jnp.int32, (rows, width), 1)
    return (row >= col) & (segc == segr)


def inner_body(q_ref, k_ref, v_ref, segc_ref, segr_ref, numer_ref, denom_ref):
    head = pl.program_id(0)
    tokens, lanes = q_ref.shape
    mine = head_lanes(head, lanes)
    for row0 in range(0, tokens, STRIP):
        width = row0 + STRIP
        query = jnp.where(mine, q_ref[pl.ds(row0, STRIP), :] * LOW(0.25), LOW(0.0))
        scores = nt(query, k_ref[pl.ds(0, width), :])
        keep = masked_weights(scores, segc_ref[pl.ds(row0, STRIP), :], segr_ref[:, pl.ds(0, width)], row0, width)
        weights = jnp.where(keep, 1.0 + scores * (1.0 + 0.5 * scores), 0.0).astype(LOW)
        wide = jnp.concatenate([v_ref[pl.ds(0, width), :], jnp.ones((width, HV), LOW)], axis=1)
        both = nn(weights, wide)
        numer_ref[pl.ds(row0, STRIP), :] = both[:, :HV]
        denom_ref[pl.ds(row0, STRIP), :] = both[:, HV:]


def merge_body(q_ref, numer_ref, denom_ref, sum_ref, norm_ref, open_ref, table_ref, y_ref, total_ref):
    head = pl.program_id(0)
    table = table_ref[...]
    one, two = pickers(table, head, q_ref.shape[1])
    left, right = factors(q_ref[...], table, one, two)
    feats = (left * right * open_ref[...]).astype(LOW)
    norm = jnp.broadcast_to(norm_ref[0][0:1, :], (HV, WIDE))
    norm_high = norm.astype(LOW)
    norm_rest = (norm - norm_high.astype(F32)).astype(LOW)
    total = denom_ref[...] + nt(feats, norm_high) + nt(feats, norm_rest)
    numer = numer_ref[...] + nn(feats, pad_state(sum_ref[0].astype(LOW)))
    total_ref[...] = total
    y_ref[...] = (numer / total).astype(LOW)


def pull_state_body(q_ref, y_ref, total_ref, open_ref, table_ref, *refs):
    *dy_refs, wide_ref, sum_ref, norm_ref = refs
    head = pl.program_id(0)
    table = table_ref[...]
    one, two = pickers(table, head, q_ref.shape[1])
    left, right = factors(q_ref[...], table, one, two)
    feats = (left * right * open_ref[...]).astype(LOW)
    inverse = 1.0 / total_ref[...]
    dy = jnp.concatenate([r[...] for r in dy_refs], axis=0)
    dnumer = (dy * inverse).astype(LOW)
    ddenom = -jnp.sum(dy * y_ref[...].astype(F32), axis=1, keepdims=True) * inverse
    ddenom = jnp.where(lax.broadcasted_iota(jnp.int32, ddenom.shape, 1) < 8, ddenom, 0.0).astype(LOW)
    wide_ref[...] = jnp.concatenate([dnumer, ddenom], axis=1)
    sum_ref[0] = tn(feats, dnumer)[:ROWS].astype(sum_ref.dtype)
    norm_ref[0] = tn(ddenom, feats)[:8]


def pull_inner_body(
    q_ref, k_ref, v_ref, segc_ref, segr_ref, wide_ref, sum_ref, norm_ref, open_ref, table_ref,
    dq_ref, dk_ref, dv_ref, dq_acc, dk_acc,
):
    head = pl.program_id(0)
    last = pl.num_programs(0) - 1
    tokens, lanes = q_ref.shape
    mine = head_lanes(head, lanes)

    @pl.when(head == 0)
    def _():
        dq_acc[...] = jnp.zeros_like(dq_acc)
        dk_acc[...] = jnp.zeros_like(dk_acc)

    dv_ref[...] = jnp.zeros_like(dv_ref)
    table = table_ref[...]
    one, two = pickers(table, head, lanes)
    state = pad_state(sum_ref[0].astype(LOW))
    norm = norm_ref[0][0:1, :]
    single = (lax.broadcasted_iota(jnp.int32, (1, HV), 1) < 1).astype(LOW)
    for row0 in range(0, tokens, STRIP):
        width = row0 + STRIP
        rows = pl.ds(row0, STRIP)
        query = jnp.where(mine, q_ref[rows, :] * LOW(0.25), LOW(0.0))
        keys = jnp.where(mine, k_ref[pl.ds(0, width), :] * LOW(0.25), LOW(0.0))
        scores = nt(query, k_ref[pl.ds(0, width), :])
        keep = masked_weights(scores, segc_ref[rows, :], segr_ref[:, pl.ds(0, width)], row0, width)
        weights = jnp.where(keep, 1.0 + scores * (1.0 + 0.5 * scores), 0.0).astype(LOW)
        dwide = wide_ref[rows, :]
        ones = jnp.broadcast_to(single, (width, HV))
        wide = jnp.concatenate([v_ref[pl.ds(0, width), :], ones], axis=1)
        dscores = jnp.where(keep, nt(dwide, wide) * (1.0 + scores), 0.0).astype(LOW)
        dv_ref[pl.ds(0, width), :] += tn(weights, dwide[:, :HV])
        dk_acc[pl.ds(0, width), :] += tn(dscores, query)
        left, right = factors(q_ref[rows, :], table, one, two)
        pulled = nt(dwide[:, :HV], state) + dwide[:, HV : HV + 1].astype(F32) * norm
        pulled = pulled * open_ref[rows, :]
        dq_acc[rows, :] += nn(dscores, keys) + nt((pulled * right).astype(LOW), one) + nt((pulled * left).astype(LOW), two)

    @pl.when(head == last)
    def _():
        dq_ref[...] = dq_acc[...].astype(dq_ref.dtype)
        dk_ref[...] = dk_acc[...]


def thin_width(heads):
    return -(-2 * heads * FEAT // HV) * HV


def pull_carry_body(k_ref, v_ref, tail_ref, sum_ref, norm_ref, dq_ref, dk_ref, dv_ref, table_ref, out_ref, dk_acc):
    head = pl.program_id(0)
    tokens, lanes = k_ref.shape
    start = 2 * lanes + -2 * lanes % HV

    @pl.when(head == 0)
    def _():
        dk_acc[...] = dk_ref[...]

    table = table_ref[...]
    one, two = pickers(table, head, lanes)
    left, right = factors(k_ref[...], table, one, two)
    scale = table[4:5, :] * tail_ref[...]
    state = pad_state(sum_ref[0].astype(LOW))
    dv = dv_ref[...] + nn((left * right * scale).astype(LOW), state)
    out_ref[:, pl.ds(pl.multiple_of(start + head * HV, HV), HV)] = dv.astype(out_ref.dtype)
    pulled = (nt(v_ref[...], state) + norm_ref[0][0:1, :]) * scale
    dk_acc[...] += nt((pulled * right).astype(LOW), one) + nt((pulled * left).astype(LOW), two)

    @pl.when(head == pl.num_programs(0) - 1)
    def _():
        thin = [dq_ref[...], dk_acc[...].astype(out_ref.dtype)]
        if start > 2 * lanes:
            thin.append(jnp.zeros((tokens, start - 2 * lanes), out_ref.dtype))
        out_ref[:, :start] = jnp.concatenate(thin, axis=1)


def shape(dims, kind):
    return jax.ShapeDtypeStruct(dims, kind)


class Mixer:
    def __init__(self, tokens, heads):
        self.tokens, self.heads = tokens, heads
        lanes = heads * FEAT
        self.full = lambda a, b: pl.BlockSpec((a, b), lambda h: (0, 0))
        self.thin = self.full(tokens, lanes)
        self.column = self.full(tokens, 1)
        self.row = self.full(1, tokens)
        self.table = self.full(8, WIDE)
        self.head = pl.BlockSpec((tokens, HV), lambda h: (0, h))
        self.pair = pl.BlockSpec((tokens, 2 * HV), lambda h: (0, h))
        self.sum = pl.BlockSpec((1, ROWS, HV), lambda h: (h, 0, 0))
        self.norm = pl.BlockSpec((1, 8, WIDE), lambda h: (h, 0, 0))
        self.thin_shape = lambda kind: shape((tokens, lanes), kind)
        self.head_shape = lambda kind: shape((tokens, heads * HV), kind)
        self.state_shapes = [shape((heads, ROWS, HV), F32), shape((heads, 8, WIDE), F32)]
        self.acc = pltpu.VMEM((tokens, lanes), F32)

    def call(self, body, name, in_specs, out_specs, out_shape, scratch, micros, *args):
        return pl.pallas_call(
            body,
            grid=(self.heads,),
            in_specs=in_specs,
            out_specs=out_specs,
            out_shape=out_shape,
            scratch_shapes=scratch,
            name=name,
            compiler_params=pltpu.CompilerParams(
                dimension_semantics=("arbitrary",), vmem_limit_bytes=48 * 1024 * 1024
            ),
            cost_estimate=pl.CostEstimate(
                flops=int(micros * 1e-6 * 1e15), bytes_accessed=1 << 20, transcendentals=0
            ),
        )(*args)

    def state(self, k, v, tail, table):
        return self.call(
            state_body, "mix_state", [self.thin, self.head, self.column, self.table],
            [self.sum, self.norm], self.state_shapes, [], 4, k, v, tail, table,
        )

    def inner(self, q, k, v, segc, segr):
        return self.call(
            inner_body, "mix_inner", [self.thin, self.thin, self.head, self.column, self.row],
            [self.head, self.head], [self.head_shape(F32)] * 2, [], 10, q, k, v, segc, segr,
        )

    def merge(self, q, numer, denom, total, norm, opened, table):
        return self.call(
            merge_body, "mix_merge",
            [self.thin, self.head, self.head, self.sum, self.norm, self.column, self.table],
            [self.head, self.head], [self.head_shape(LOW), self.head_shape(F32)], [], 5,
            q, numer, denom, total, norm, opened, table,
        )

    def pull_state(self, q, dy, y, total, opened, table):
        return self.call(
            pull_state_body, "mix_pull_state",
            [self.thin, self.head, self.head, self.column, self.table]
            + [pl.BlockSpec((d.shape[0], HV), lambda h: (0, h)) for d in dy],
            [self.pair, self.sum, self.norm],
            [shape((self.tokens, self.heads * 2 * HV), LOW)] + self.state_shapes, [], 5,
            q, y, total, opened, table, *dy,
        )

    def pull_inner(self, q, k, v, segc, segr, wide, total, norm, opened, table):
        return self.call(
            pull_inner_body, "mix_pull_inner",
            [self.thin, self.thin, self.head, self.column, self.row, self.pair, self.sum, self.norm, self.column, self.table],
            [self.thin, self.thin, self.head],
            [self.thin_shape(LOW), self.thin_shape(F32), self.head_shape(F32)],
            [self.acc, self.acc], 20, q, k, v, segc, segr, wide, total, norm, opened, table,
        )

    def pull_carry(self, k, v, tail, total, norm, dq, dk, dv, table):
        width = thin_width(self.heads) + self.heads * HV
        return self.call(
            pull_carry_body, "mix_pull_carry",
            [self.thin, self.head, self.column, self.sum, self.norm, self.thin, self.thin, self.head, self.table],
            self.full(self.tokens, width), shape((self.tokens, width), LOW), [self.acc], 6,
            k, v, tail, total, norm, dq, dk, dv, table,
        )


def outside(part, reverse):
    count, place = lax.axis_size("batch"), lax.axis_index("batch")
    total = list(part)
    before = [jnp.zeros_like(a) for a in part]
    bit = 1
    while bit < count:
        pairs = [(i, i ^ bit) for i in range(count)]
        low = total[0].astype(LOW)
        other = [lax.ppermute(low, "batch", pairs).astype(F32), lax.ppermute(total[1], "batch", pairs)]
        upper = (place & bit) != 0
        take = jnp.logical_not(upper) if reverse else upper
        before = [a + jnp.where(take, b, 0.0) for a, b in zip(before, other)]
        total = [a + b for a, b in zip(total, other)]
        bit *= 2
    return before


def padded(width):
    return -(-width // 16) * 16


def batch_orders():
    count = lax.axis_size("batch")
    bits = [1 << b for b in range(count.bit_length() - 1)]
    return bits[:1] + bits[1:], bits[:1] + bits[:0:-1]


def block_order():
    count = lax.axis_size("batch")
    first, second = batch_orders()
    relative, places = [], []
    for step in range(count):
        at = sum(bit for n, bit in enumerate(first) if step >> (len(first) - 1 - n) & 1)
        relative.append(at)
        places.append(sum(1 << (len(second) - 1 - n) for n, bit in enumerate(second) if at & bit))
    blocks = jnp.asarray(np.array(relative, np.int32)) ^ lax.axis_index("batch").astype(jnp.int32)
    return blocks, places


def cost(micros):
    return pl.CostEstimate(flops=int(micros * 1e9), bytes_accessed=1 << 20, transcendentals=0)


BIG = pltpu.CompilerParams(dimension_semantics=("arbitrary",), vmem_limit_bytes=56 * 1024 * 1024)


def grad_values(refs, groups):
    values = []
    for rows, parts in groups:
        value = None
        for _ in range(parts):
            term = nn(refs[1][...], refs[0][...])
            refs = refs[2:]
            value = term if value is None else value + term
        values.append(value)
    return values


def grad_body(blocks, swap, *refs, groups, summed):
    step = pl.program_id(0)
    places = (step, swap[0, step])
    middle = pl.num_programs(0) // 2
    sources = 2 * sum(parts for _, parts in groups)
    values = grad_values(list(refs[:sources]), groups)
    outs = refs[-4:]
    came = refs[sources:-4]
    at = 0
    for (rows, _), value in zip(groups, values):
        size = padded(rows // 2)
        for n in range(2):
            half = value[n * rows // 2 : (n + 1) * rows // 2]
            if size > rows // 2:
                half = jnp.concatenate([half, jnp.zeros((size - rows // 2, half.shape[1]), F32)], axis=0)
            span = slice(at, at + size)
            if summed:
                other = jnp.where(places[n] < middle, came[n][0, span, :], came[2 + n][0, span, :])
                half = half + other.astype(F32)
            half = half.astype(LOW)

            @pl.when(places[n] < middle)
            def _():
                outs[n][0, span, :] = half

            @pl.when(places[n] >= middle)
            def _():
                outs[2 + n][0, span, :] = half

        at += size


def grad_blocks(name, groups, far, came, micros):
    count = lax.axis_size("batch")
    split = count // 2
    width = groups[0][0][0].shape[1]
    columns = width // count
    blocks, places = block_order()
    base = split if far else 0
    in_specs, operands, kinds, rows = [], [], [], 0
    for parts in groups:
        for left, right in parts:
            in_specs.append(pl.BlockSpec((left.shape[0], columns), lambda s, b, w: (0, b[s])))
            in_specs.append(pl.BlockSpec(right.shape, lambda s, b, w: (0, 0)))
            operands += [left, right]
        kinds.append((parts[0][1].shape[0], len(parts)))
        rows += padded(parts[0][1].shape[0] // 2)
    size = (1, rows, columns)
    places = [p - base for p in places[base : base + split]]
    table, specs = [places], []
    for low in (0, split // 2):
        for order in (list(range(split)), places):
            uses = [(s, p - low) for s, p in enumerate(order) if low <= p < low + split // 2]
            table.append([([at for when, at in uses if when <= s] or [uses[0][1]])[-1] for s in range(split)])
            specs.append(pl.BlockSpec(size, lambda s, b, w, n=len(table) - 1: (w[n, s], 0, 0)))
    if came:
        in_specs += specs
        operands += came
    outs = pl.pallas_call(
        functools.partial(grad_body, groups=tuple(kinds), summed=bool(came)),
        grid_spec=pltpu.PrefetchScalarGridSpec(
            num_scalar_prefetch=2, grid=(split,), in_specs=in_specs, out_specs=specs
        ),
        out_shape=[shape((split // 2, rows, columns), LOW)] * 4,
        name=name,
        compiler_params=BIG,
        cost_estimate=cost(micros),
    )(blocks[base : base + split], jnp.asarray(np.array(table, np.int32)), *operands)
    return outs[:2], outs[2:]


def flip(value, bit):
    return lax.ppermute(value, "batch", [(i, i ^ bit) for i in range(lax.axis_size("batch"))])


def added(one, other):
    return (one.astype(F32) + other.astype(F32)).astype(LOW)


class Exchange:
    def __init__(self, far):
        self.orders = batch_orders()
        self.steps = len(self.orders[0])
        self.away, self.near, self.came = [list(f) for f in zip(*far)], None, [[], []]
        self.step = 0

    def get(self):
        return [self.away, self.near, self.came]

    def put(self, values):
        self.away, self.near, self.came = values

    def send(self, limit=None):
        n = self.step
        if n == 2 * self.steps:
            return
        for half, order in enumerate(self.orders):
            bit = order[n if n < self.steps else 2 * self.steps - 1 - n]
            first = len(self.came[half])
            last = len(self.away[half]) if limit is None else first + limit
            self.came[half] += [flip(a, bit) for a in self.away[half][first:last]]

    def begin(self, name, groups, micros):
        self.near, away = grad_blocks(name, groups, False, [c[n] for n in range(2) for c in self.came], micros)
        self.away, self.came, self.step = [[a] for a in away], [[], []], 1

    def take(self):
        n = self.step
        if n == 2 * self.steps:
            return
        self.step += 1
        if n == 0:
            self.near, away = [[added(b, c[m]) for b, c in zip(half, self.came)] for m, half in enumerate(self.near)]
            self.away = [[a] for a in away]
        elif n < self.steps:
            half = self.near[0].shape[0] // 2
            pairs = [(k, c[0]) for k, c in zip(self.near, self.came)]
            if half:
                self.away = [[added(k[half:], c[half:])] for k, c in pairs]
                self.near = [added(k[:half], c[:half]) for k, c in pairs]
            else:
                self.near = [added(k, c) for k, c in pairs]
                self.away = [[k] for k in self.near]
        else:
            self.away = [a + c for a, c in zip(self.away, self.came)]
        self.came = [[], []]

    def run(self):
        while self.step < 2 * self.steps:
            self.send()
            self.take()
        return self.away


def place_body(blocks, table, *refs, outs, count):
    step = pl.program_id(0)
    pieces = count
    chosen = []
    for n in range(2):
        which = table[n, step]
        group = refs[n * pieces : (n + 1) * pieces]
        value = group[0][0]
        for m in range(1, pieces):
            value = jnp.where(which == m, group[m][0], value)
        chosen.append(value)
    results = refs[2 * pieces :]
    for start, rows, targets in outs:
        both = jnp.concatenate([c[start : start + rows // 2].astype(F32) for c in chosen], axis=0)
        for index, first, size, turned in targets:
            part = both[first : first + size]
            results[index][...] = part.T if turned else part


def place_blocks(name, pieces, outs, width, micros, part=None):
    count = lax.axis_size("batch")
    columns = width // count
    blocks, places = block_order()
    table = np.array([list(range(count)), places], np.int32)
    size = pieces[0][0].shape[1:]
    if part is not None:
        size = (padded(outs[0][0] // 2), size[1])
    piece = pl.BlockSpec((1,) + size, lambda s, b, t: (0, part or 0, 0), pipeline_mode=pl.Buffered(1))
    out_specs, out_shape, layout, start = [], [], [], 0
    for rows, targets in outs:
        listed = []
        for first, used, turned in targets:
            listed.append((len(out_shape), first, used, turned))
            if turned:
                out_specs.append(pl.BlockSpec((columns, used), lambda s, b, t: (b[s], 0)))
                out_shape.append(shape((width, used), F32))
            else:
                out_specs.append(pl.BlockSpec((used, columns), lambda s, b, t: (0, b[s])))
                out_shape.append(shape((used, width), F32))
        layout.append((start, rows, tuple(listed)))
        start += padded(rows // 2)
    return pl.pallas_call(
        functools.partial(place_body, outs=tuple(layout), count=count),
        grid_spec=pltpu.PrefetchScalarGridSpec(
            num_scalar_prefetch=2,
            grid=(count,),
            in_specs=[piece] * (2 * count),
            out_specs=out_specs,
        ),
        out_shape=out_shape,
        name=name,
        compiler_params=BIG,
        cost_estimate=cost(micros),
    )(blocks, jnp.asarray(table), *pieces[0], *pieces[1])


def line_sum(value):
    count = lax.axis_size("tensor")
    turned = [lax.ppermute(value, "tensor", [(i, (i + n) % count) for i in range(count)]) for n in range(1, count)]
    return [value] + turned


def batch_sum(value):
    value = value + flip(value, 1)
    return value + sum(flip(value, mask) for mask in range(2, lax.axis_size("batch"), 2))


def after(values, *others):
    return lax.optimization_barrier((values, others))[0]


def lock(*items):
    values = lax.optimization_barrier([i.get() if hasattr(i, "get") else i for i in items])
    for item, value in zip(items, values):
        if hasattr(item, "put"):
            item.put(value)
    return [v for i, v in zip(items, values) if not hasattr(i, "get")]


class Gather:
    def __init__(self, *parts):
        self.right, self.left = [list(parts)], [list(parts)]
        self.hops = 0
        self.least = lax.axis_size("tensor") - 1

    def get(self):
        return [self.right, self.left]

    def put(self, values):
        self.right, self.left = values

    def hop(self):
        count = lax.axis_size("tensor")
        self.hops += 1
        to_right = [(k, k + 1) for k in range(self.hops - 1, count - 1)]
        to_left = [(k, k - 1) for k in range(1, count - self.hops + 1)]
        self.right.append([lax.ppermute(a, "tensor", to_right) for a in self.right[-1]])
        self.left.append([lax.ppermute(a, "tensor", to_left) for a in self.left[-1]])

    def run(self):
        while self.hops < self.least:
            self.hop()
        return self

    def pieces(self, n=0):
        count, place = lax.axis_size("tensor"), lax.axis_index("tensor")
        return [self.right[0][n]] + [
            jnp.where(place + r < count, self.left[r][n], self.right[count - r][n]) for r in range(1, count)
        ]

    def total(self, n=0):
        return sum(a[n] for a in self.right) + sum(a[n] for a in self.left[1:])


class Scatter:
    def __init__(self, make):
        self.make, self.came, self.made = make, [], {}
        self.left = lax.axis_size("tensor") - 1
        self.prepare()

    def prepare(self):
        count = lax.axis_size("tensor")
        for r in (self.left, (count - self.left) % count):
            if r not in self.made:
                self.made[r] = self.make(r)

    def get(self):
        return [self.came, self.made]

    def put(self, values):
        self.came, self.made = values

    def hop(self):
        count = lax.axis_size("tensor")
        sends = [self.made[self.left], self.made[count - self.left]]
        if self.came:
            sends = [s + c.astype(F32) for s, c in zip(sends, self.came)]
        sends = [s.astype(LOW) for s in sends]
        self.came = [
            lax.ppermute(sends[0], "tensor", [(k, k + 1) for k in range(0, count - self.left)]),
            lax.ppermute(sends[1], "tensor", [(k, k - 1) for k in range(self.left, count)]),
        ]
        self.left -= 1
        self.prepare()

    def result(self):
        return self.made[0] + self.came[0].astype(F32) + self.came[1].astype(F32)


def copy_body(turn, in_ref, out_ref):
    out_ref[...] = in_ref[...]


def straighten(array):
    count = lax.axis_size("tensor")
    turn = (jnp.arange(count, dtype=jnp.int32) - lax.axis_index("tensor")) % count
    size = (array.shape[0], array.shape[1] // count)
    return pl.pallas_call(
        copy_body,
        grid_spec=pltpu.PrefetchScalarGridSpec(
            num_scalar_prefetch=1,
            grid=(count,),
            in_specs=[pl.BlockSpec(size, lambda n, t: (0, t[n]))],
            out_specs=pl.BlockSpec(size, lambda n, t: (0, n)),
        ),
        out_shape=shape(array.shape, array.dtype),
        name="straighten",
        compiler_params=BIG,
        cost_estimate=cost(4),
    )(turn, array)


def widen(part):
    return lax.all_gather(part, "tensor", axis=1, tiled=True)


def narrow(part):
    return lax.psum_scatter(part, "tensor", scatter_dimension=1, tiled=True)


def project(left, right):
    return jnp.dot(left, right, preferred_element_type=F32)


def project_back(left, right):
    return jnp.einsum("ti,ji->tj", left, right, preferred_element_type=F32)


def across(left, right):
    return jnp.einsum("it,ij->tj", left, right, preferred_element_type=F32)


def row_sum(values):
    return jnp.sum(values, axis=1, keepdims=True)


def local(
    tokens, doc_lengths, norm1_gain, w_query, w_key, w_value, w_out, norm2_gain, w_gate, w_up, w_down, cotangent,
):
    count, slice_width = tokens.shape
    heads = w_value.shape[1] // HV
    lanes = heads * FEAT
    width = w_query.shape[0]
    begin_here = lax.axis_index("batch") * count
    position = begin_here + jnp.arange(count, dtype=jnp.int32)
    doc_index = jnp.arange(doc_lengths.shape[0], dtype=jnp.int32)
    doc_begins = jnp.sum(jnp.where(doc_index[None, :] < doc_index[:, None], doc_lengths[None, :], 0), axis=1)
    segment = jnp.sum((position[:, None] >= doc_begins[None, :]).astype(jnp.int32), axis=1) - 1
    head_seg, tail_seg = segment[0], segment[-1]
    first_begin = jnp.sum(jnp.where(doc_index == head_seg, doc_begins, 0))
    opened = ((segment == head_seg) & (first_begin < begin_here)).astype(F32)[:, None]
    tail = (segment == tail_seg).astype(F32)[:, None]
    segc, segr = segment[:, None], segment[None, :]
    table = jnp.asarray(feature_table())
    mixer = Mixer(count, heads)

    size, place = lax.axis_size("tensor"), lax.axis_index("tensor")
    half = count // 2
    cut = lambda a: (a[:half], a[half:])
    join = lambda *parts: jnp.concatenate(parts, axis=0)
    c_a, c_b = cut(cotangent)
    w_gate, w_up = w_gate.T, w_up.T
    units = w_gate.shape[0]

    x_full = widen(tokens)
    gains = lax.all_gather(jnp.stack([norm1_gain, norm2_gain]), "tensor", axis=1, tiled=True)
    thin = thin_width(heads)
    w_mix = [w_query, w_key, jnp.zeros((width, thin - 2 * lanes), LOW), w_value]
    w_mix = jnp.concatenate([w for w in w_mix if w.shape[1]], axis=1)
    gather_c = Gather(cotangent)
    x_full, gains, w_mix = lock(x_full, gains, w_mix, gather_c)

    gather_c.hop()
    x_wide = x_full.astype(F32)
    scale_one = lax.rsqrt(row_sum(x_wide * x_wide) / width + EPSILON)
    normed_one = (x_wide * scale_one * gains[0:1]).astype(LOW)
    pair = project(normed_one, w_mix[:, :thin]).astype(LOW)
    q, k, v = pair[:, :lanes], pair[:, lanes : 2 * lanes], project(normed_one, w_value).astype(LOW)
    carry = mixer.state(k, v, tail, table)
    prior = outside(carry, False)
    numer, denom = mixer.inner(q, k, v, segc, segr)
    y, total = mixer.merge(q, numer, denom, *prior, opened, table)
    columns = lambda w, r: lax.dynamic_slice_in_dim(w, ((place + r) % size) * slice_width, slice_width, 1)
    scatter = Scatter(lambda r: project(y, columns(w_out, r)))
    y, total = lock(y, total, gather_c, scatter)
    while scatter.left:
        scatter.hop()
        if gather_c.hops < gather_c.least:
            gather_c.hop()
        lock(scatter, gather_c)
    hidden = tokens.astype(F32) + scatter.result()
    hidden_a, hidden_b = cut(hidden)
    low_a, low_b = cut(hidden.astype(LOW))
    hidden_a, hidden_b, low_a, low_b = lock(hidden_a, hidden_b, low_a, low_b)

    wide_a = widen(low_a)
    c_full = straighten(jnp.concatenate(gather_c.pieces(), axis=1))
    ca_full, cb_full = cut(c_full)
    dinner_a = project_back(w_down, ca_full)
    dinner_b = project_back(w_down, cb_full)
    wide_a, c_full, dinner_a, dinner_b = lock(wide_a, c_full, dinner_a, dinner_b)
    ca_full, cb_full = cut(c_full)

    def feed(wide, dinner):
        wide32 = wide.astype(F32)
        scale = lax.rsqrt(row_sum(wide32 * wide32) / width + EPSILON)
        normed = (wide32 * scale * gains[1:2]).astype(LOW)
        gate = project_back(w_gate, normed)
        up = project_back(w_up, normed)
        sig = jax.nn.sigmoid(gate)
        silu = gate * sig
        inner = (silu * up).astype(LOW)
        dgate = (dinner * up * sig * (1.0 + gate * (1.0 - sig))).astype(LOW)
        dup = (dinner * silu).astype(LOW)
        pulled = (across(dgate, w_gate) + across(dup, w_up)).astype(LOW)
        return scale, normed, inner, dgate, dup, pulled

    wide_b = widen(low_b)
    wide_b, (scale_a, normed_a, inner_a, dgate_a, dup_a, part) = lock(wide_b, feed(wide_a, dinner_a))

    back_a = narrow(part)
    scale_b, normed_b, inner_b, dgate_b, dup_b, part = feed(wide_b, dinner_b)
    groups = [
        [(normed_a, dgate_a), (normed_b, dgate_b)],
        [(normed_a, dup_a), (normed_b, dup_b)],
        [(ca_full, inner_a), (cb_full, inner_b)],
    ]
    ffn = Exchange(grad_blocks("grad_ffn_far", groups, True, None, 16))
    back_a, scale_b, normed_b, inner_b, dgate_b, dup_b, part = lock(
        back_a, scale_b, normed_b, inner_b, dgate_b, dup_b, part, ffn
    )

    def turned(c, scale, back, hidden):
        scaled = scale * back.astype(F32)
        return c.astype(F32) + norm2_gain[None, :] * scaled, jnp.sum(scaled * hidden, axis=0)

    def spread(u, c, wide, scale, local_u, hidden):
        u, wide = u.astype(F32), wide.astype(F32)
        dot = row_sum((u - c.astype(F32)) * wide) * scale * scale / width
        dh = (u - wide * dot).astype(LOW)
        return dh, local_u - hidden * dot, project_back(dh, w_out)

    back_b = narrow(part)
    u_a, gain_a = turned(c_a, scale_a, back_a, hidden_a)
    low_a = u_a.astype(LOW)
    groups = [
        [(normed_a, dgate_a), (normed_b, dgate_b)],
        [(normed_a, dup_a), (normed_b, dup_b)],
        [(ca_full, inner_a), (cb_full, inner_b)],
    ]
    ffn.send()
    ffn.near = grad_blocks("grad_ffn_near", groups, False, None, 16)
    ffn.take()
    ffn.send()
    back_b, u_a, gain_a, low_a, ffn.away, ffn.near = lock(back_b, u_a, gain_a, low_a, ffn.away, ffn.near)

    wide_u = widen(low_a)
    u_b, gain_b = turned(c_b, scale_b, back_b, hidden_b)
    low_b = u_b.astype(LOW)
    parts = [across(m, w_down).astype(LOW) for m in (inner_a, inner_b)]
    y_turned = [p.T for p in cut(y)]
    wide_u, u_b, gain_b, low_b, parts, y_turned = lock(wide_u, u_b, gain_b, low_b, parts, y_turned, ffn)

    wide_v = widen(low_b)
    ffn.take()
    ffn.send()
    dh_a, grad_hidden_a, dy_a = spread(wide_u, ca_full, wide_a, scale_a, u_a, hidden_a)
    ffn.take()
    ffn.send()
    wide_v, dh_a, grad_hidden_a, dy_a, ffn.away, ffn.near = lock(
        wide_v, dh_a, grad_hidden_a, dy_a, ffn.away, ffn.near
    )

    down = narrow(join(*parts))
    dh_b, grad_hidden_b, dy_b = spread(wide_v, cb_full, wide_b, scale_b, u_b, hidden_b)
    wide, dsum, dnorm = mixer.pull_state(q, [dy_a, dy_b], y, total, opened, table)
    ffn.take()
    ffn.send(1)
    wide, dsum, dnorm = lock(wide, dsum, dnorm, ffn)
    following = outside([dsum, dnorm], True)
    dq, dk, dv = mixer.pull_inner(q, k, v, segc, segr, wide, *prior, opened, table)
    following, dq, dk, dv = lock(following, dq, dk, dv, ffn)
    ffn.send()
    dmix = mixer.pull_carry(k, v, tail, *following, dq, dk, dv, table)
    part = project_back(dmix, w_mix).astype(LOW)
    dot = row_sum(dmix[:, :thin].astype(F32) * pair.astype(F32))
    dot = dot + row_sum(dmix[:, thin:].astype(F32) * v.astype(F32))
    dots = line_sum(dot.reshape(count // 128, 128))
    down, part, dmix, dh_b, grad_hidden_b, dots = lock(down, part, dmix, dh_b, grad_hidden_b, dots, ffn)

    back = narrow(part)
    groups = [[(normed_one, dmix.T)], [(dh_a, y_turned[0]), (dh_b, y_turned[1])]]
    ffn.take()
    ffn.send()
    mix = Exchange(grad_blocks("grad_mix_far", groups, True, None, 5))
    mix.send()
    mix.begin("grad_mix_near", groups, 5)
    lock(mix, ffn)
    mix.send()
    ffn.take()
    final = ffn.run()

    def ffn_weight(n):
        return place_blocks(f"place_ffn_{n}", final, [(units, [(0, units, False)])], width, 7, n)[0]

    grad_w_gate = lock(mix, ffn_weight(0))[0]
    mix.take()
    mix.send()
    grad_w_up = lock(mix, ffn_weight(1))[0]
    mix.take()
    mix.send()
    output = (join(hidden_a, hidden_b) + down.astype(F32)).astype(LOW)
    output = lock(mix, output)[0]
    mix.take()
    mix.send()
    grad_w_down = lock(mix, ffn_weight(2))[0]
    mix.take()
    mix.send()
    back = lock(back, mix)[0]
    inputs, back = tokens.astype(F32), back.astype(F32)
    gain_one = jnp.sum(back * inputs * scale_one, axis=0)
    gain_grads = batch_sum(jnp.stack([gain_one, gain_a + gain_b]))
    grad_tokens = (
        join(grad_hidden_a, grad_hidden_b)
        + scale_one * norm1_gain[None, :] * back
        - inputs * (scale_one * scale_one * sum(dots).reshape(count, 1) / width)
    )
    values = heads * HV
    grad_w_query, grad_w_key, grad_w_value, grad_w_out = place_blocks(
        "place_mix",
        mix.run(),
        [
            (thin + values, [(0, lanes, False), (lanes, lanes, False), (thin, values, True)]),
            (values, [(0, values, False)]),
        ],
        width,
        5,
    )
    return (
        output,
        grad_tokens,
        gain_grads[0],
        grad_w_query.T,
        grad_w_key.T,
        grad_w_value,
        grad_w_out,
        gain_grads[1],
        grad_w_gate.T,
        grad_w_up.T,
        grad_w_down,
    )


def solution(mesh):
    rows, cols = P("tensor", None), P(None, "tensor")
    both, one = P("batch", "tensor"), P("tensor")
    in_specs = (both, P(), one, cols, cols, cols, rows, one, cols, cols, rows, both)
    out_specs = (both, both, one, cols, cols, cols, rows, one, cols, cols, rows)
    return jax.shard_map(local, mesh=mesh, in_specs=in_specs, out_specs=out_specs, check_vma=False)
```

```python
import functools
import math

import jax
import jax.numpy as jnp
import numpy as np
from jax import lax
from jax.experimental import pallas as pl
from jax.experimental.pallas import tpu as pltpu
from jax.sharding import PartitionSpec as P

FEAT = 16
HV = 128
EPSILON = 1e-05
WIDE = 256
ROWS = 160
STRIP = 256
CHUNKS = 2
LOW = jnp.bfloat16
F32 = jnp.float32


def feature_table():
    table = np.zeros((8, WIDE), np.float32)
    table[0:2] = -1.0
    at = 0
    for i in range(FEAT + 1):
        for j in range(i, FEAT + 1):
            table[0, at] = i if i < FEAT else -1
            table[1, at] = j if j < FEAT else -1
            table[2, at] = float(i == FEAT)
            table[3, at] = float(j == FEAT)
            table[4, at] = 0.5 if i == j and i < FEAT else 1.0
            at += 1
    return table


def nt(a, b):
    return lax.dot_general(a, b, (((1,), (1,)), ((), ())), preferred_element_type=F32)


def tn(a, b):
    return lax.dot_general(a, b, (((0,), (0,)), ((), ())), preferred_element_type=F32)


def nn(a, b):
    return lax.dot_general(a, b, (((1,), (0,)), ((), ())), preferred_element_type=F32)


def pickers(table, head, lanes):
    lane = lax.broadcasted_iota(jnp.int32, (lanes, WIDE), 0).astype(F32)
    base = (head * FEAT).astype(F32)
    first, second = table[0:1, :], table[1:2, :]
    one = jnp.where((lane == base + first) & (first >= 0), 0.5, 0.0).astype(LOW)
    two = jnp.where((lane == base + second) & (second >= 0), 0.5, 0.0).astype(LOW)
    return one, two


def head_lanes(head, lanes):
    lane = lax.broadcasted_iota(jnp.int32, (1, lanes), 1)
    return (lane >= head * FEAT) & (lane < (head + 1) * FEAT)


def factors(z, table, one, two):
    return nn(z, one) + table[2:3, :], nn(z, two) + table[3:4, :]


def pad_state(state):
    return jnp.concatenate([state, jnp.zeros((WIDE - ROWS, HV), state.dtype)], axis=0)


def state_body(k_ref, v_ref, tail_ref, table_ref, sum_ref, norm_ref):
    head = pl.program_id(0)
    table = table_ref[...]
    one, two = pickers(table, head, k_ref.shape[1])
    left, right = factors(k_ref[...], table, one, two)
    feats = (left * right * table[4:5, :] * tail_ref[...]).astype(LOW)
    sum_ref[0] = tn(feats, v_ref[...])[:ROWS].astype(sum_ref.dtype)
    norm_ref[0] = nn(jnp.ones((8, feats.shape[0]), LOW), feats)


def masked_weights(scores, segc, segr, row0, width):
    rows = scores.shape[0]
    row = row0 + lax.broadcasted_iota(jnp.int32, (rows, width), 0)
    col = lax.broadcasted_iota(jnp.int32, (rows, width), 1)
    return (row >= col) & (segc == segr)


def inner_body(q_ref, k_ref, v_ref, segc_ref, segr_ref, numer_ref, denom_ref):
    head = pl.program_id(0)
    tokens, lanes = q_ref.shape
    mine = head_lanes(head, lanes)
    for row0 in range(0, tokens, STRIP):
        width = row0 + STRIP
        query = jnp.where(mine, q_ref[pl.ds(row0, STRIP), :] * LOW(0.25), LOW(0.0))
        scores = nt(query, k_ref[pl.ds(0, width), :])
        keep = masked_weights(scores, segc_ref[pl.ds(row0, STRIP), :], segr_ref[:, pl.ds(0, width)], row0, width)
        weights = jnp.where(keep, 1.0 + scores * (1.0 + 0.5 * scores), 0.0).astype(LOW)
        wide = jnp.concatenate([v_ref[pl.ds(0, width), :], jnp.ones((width, HV), LOW)], axis=1)
        both = nn(weights, wide)
        numer_ref[pl.ds(row0, STRIP), :] = both[:, :HV]
        denom_ref[pl.ds(row0, STRIP), :] = both[:, HV:]


def merge_body(q_ref, numer_ref, denom_ref, sum_ref, norm_ref, open_ref, table_ref, y_ref, total_ref):
    head = pl.program_id(0)
    table = table_ref[...]
    one, two = pickers(table, head, q_ref.shape[1])
    left, right = factors(q_ref[...], table, one, two)
    feats = (left * right * open_ref[...]).astype(LOW)
    norm = jnp.broadcast_to(norm_ref[0][0:1, :], (HV, WIDE))
    norm_high = norm.astype(LOW)
    norm_rest = (norm - norm_high.astype(F32)).astype(LOW)
    total = denom_ref[...] + nt(feats, norm_high) + nt(feats, norm_rest)
    numer = numer_ref[...] + nn(feats, pad_state(sum_ref[0].astype(LOW)))
    total_ref[...] = total
    y_ref[...] = (numer / total).astype(LOW)


def pull_state_body(q_ref, y_ref, total_ref, open_ref, table_ref, *refs):
    *dy_refs, wide_ref, sum_ref, norm_ref = refs
    head = pl.program_id(0)
    table = table_ref[...]
    one, two = pickers(table, head, q_ref.shape[1])
    left, right = factors(q_ref[...], table, one, two)
    feats = (left * right * open_ref[...]).astype(LOW)
    inverse = 1.0 / total_ref[...]
    dy = jnp.concatenate([r[...] for r in dy_refs], axis=0)
    dnumer = (dy * inverse).astype(LOW)
    ddenom = -jnp.sum(dy * y_ref[...].astype(F32), axis=1, keepdims=True) * inverse
    ddenom = jnp.where(lax.broadcasted_iota(jnp.int32, ddenom.shape, 1) < 8, ddenom, 0.0).astype(LOW)
    wide_ref[...] = jnp.concatenate([dnumer, ddenom], axis=1)
    sum_ref[0] = tn(feats, dnumer)[:ROWS].astype(sum_ref.dtype)
    norm_ref[0] = tn(ddenom, feats)[:8]


def pull_inner_body(
    q_ref, k_ref, v_ref, segc_ref, segr_ref, wide_ref, sum_ref, norm_ref, open_ref, table_ref,
    dq_ref, dk_ref, dv_ref, dq_acc, dk_acc,
):
    head = pl.program_id(0)
    last = pl.num_programs(0) - 1
    tokens, lanes = q_ref.shape
    mine = head_lanes(head, lanes)

    @pl.when(head == 0)
    def _():
        dq_acc[...] = jnp.zeros_like(dq_acc)
        dk_acc[...] = jnp.zeros_like(dk_acc)

    dv_ref[...] = jnp.zeros_like(dv_ref)
    table = table_ref[...]
    one, two = pickers(table, head, lanes)
    state = pad_state(sum_ref[0].astype(LOW))
    norm = norm_ref[0][0:1, :]
    single = (lax.broadcasted_iota(jnp.int32, (1, HV), 1) < 1).astype(LOW)
    for row0 in range(0, tokens, STRIP):
        width = row0 + STRIP
        rows = pl.ds(row0, STRIP)
        query = jnp.where(mine, q_ref[rows, :] * LOW(0.25), LOW(0.0))
        keys = jnp.where(mine, k_ref[pl.ds(0, width), :] * LOW(0.25), LOW(0.0))
        scores = nt(query, k_ref[pl.ds(0, width), :])
        keep = masked_weights(scores, segc_ref[rows, :], segr_ref[:, pl.ds(0, width)], row0, width)
        weights = jnp.where(keep, 1.0 + scores * (1.0 + 0.5 * scores), 0.0).astype(LOW)
        dwide = wide_ref[rows, :]
        ones = jnp.broadcast_to(single, (width, HV))
        wide = jnp.concatenate([v_ref[pl.ds(0, width), :], ones], axis=1)
        dscores = jnp.where(keep, nt(dwide, wide) * (1.0 + scores), 0.0).astype(LOW)
        dv_ref[pl.ds(0, width), :] += tn(weights, dwide[:, :HV])
        dk_acc[pl.ds(0, width), :] += tn(dscores, query)
        left, right = factors(q_ref[rows, :], table, one, two)
        pulled = nt(dwide[:, :HV], state) + dwide[:, HV : HV + 1].astype(F32) * norm
        pulled = pulled * open_ref[rows, :]
        dq_acc[rows, :] += nn(dscores, keys) + nt((pulled * right).astype(LOW), one) + nt((pulled * left).astype(LOW), two)

    @pl.when(head == last)
    def _():
        dq_ref[...] = dq_acc[...].astype(dq_ref.dtype)
        dk_ref[...] = dk_acc[...]


def thin_width(heads):
    return -(-2 * heads * FEAT // HV) * HV


def pull_carry_body(k_ref, v_ref, tail_ref, sum_ref, norm_ref, dq_ref, dk_ref, dv_ref, table_ref, out_ref, dk_acc):
    head = pl.program_id(0)
    tokens, lanes = k_ref.shape
    start = 2 * lanes + -2 * lanes % HV

    @pl.when(head == 0)
    def _():
        dk_acc[...] = dk_ref[...]

    table = table_ref[...]
    one, two = pickers(table, head, lanes)
    left, right = factors(k_ref[...], table, one, two)
    scale = table[4:5, :] * tail_ref[...]
    state = pad_state(sum_ref[0].astype(LOW))
    dv = dv_ref[...] + nn((left * right * scale).astype(LOW), state)
    out_ref[:, pl.ds(pl.multiple_of(start + head * HV, HV), HV)] = dv.astype(out_ref.dtype)
    pulled = (nt(v_ref[...], state) + norm_ref[0][0:1, :]) * scale
    dk_acc[...] += nt((pulled * right).astype(LOW), one) + nt((pulled * left).astype(LOW), two)

    @pl.when(head == pl.num_programs(0) - 1)
    def _():
        thin = [dq_ref[...], dk_acc[...].astype(out_ref.dtype)]
        if start > 2 * lanes:
            thin.append(jnp.zeros((tokens, start - 2 * lanes), out_ref.dtype))
        out_ref[:, :start] = jnp.concatenate(thin, axis=1)


def shape(dims, kind):
    return jax.ShapeDtypeStruct(dims, kind)


class Mixer:
    def __init__(self, tokens, heads):
        self.tokens, self.heads = tokens, heads
        lanes = heads * FEAT
        self.full = lambda a, b: pl.BlockSpec((a, b), lambda h: (0, 0))
        self.thin = self.full(tokens, lanes)
        self.column = self.full(tokens, 1)
        self.row = self.full(1, tokens)
        self.table = self.full(8, WIDE)
        self.head = pl.BlockSpec((tokens, HV), lambda h: (0, h))
        self.pair = pl.BlockSpec((tokens, 2 * HV), lambda h: (0, h))
        self.sum = pl.BlockSpec((1, ROWS, HV), lambda h: (h, 0, 0))
        self.norm = pl.BlockSpec((1, 8, WIDE), lambda h: (h, 0, 0))
        self.thin_shape = lambda kind: shape((tokens, lanes), kind)
        self.head_shape = lambda kind: shape((tokens, heads * HV), kind)
        self.state_shapes = [shape((heads, ROWS, HV), F32), shape((heads, 8, WIDE), F32)]
        self.acc = pltpu.VMEM((tokens, lanes), F32)

    def call(self, body, name, in_specs, out_specs, out_shape, scratch, micros, *args):
        return pl.pallas_call(
            body,
            grid=(self.heads,),
            in_specs=in_specs,
            out_specs=out_specs,
            out_shape=out_shape,
            scratch_shapes=scratch,
            name=name,
            compiler_params=pltpu.CompilerParams(
                dimension_semantics=("arbitrary",), vmem_limit_bytes=48 * 1024 * 1024
            ),
            cost_estimate=pl.CostEstimate(
                flops=int(micros * 1e-6 * 1e15), bytes_accessed=1 << 20, transcendentals=0
            ),
        )(*args)

    def state(self, k, v, tail, table):
        return self.call(
            state_body, "mix_state", [self.thin, self.head, self.column, self.table],
            [self.sum, self.norm], self.state_shapes, [], 4, k, v, tail, table,
        )

    def inner(self, q, k, v, segc, segr):
        return self.call(
            inner_body, "mix_inner", [self.thin, self.thin, self.head, self.column, self.row],
            [self.head, self.head], [self.head_shape(F32)] * 2, [], 10, q, k, v, segc, segr,
        )

    def merge(self, q, numer, denom, total, norm, opened, table):
        return self.call(
            merge_body, "mix_merge",
            [self.thin, self.head, self.head, self.sum, self.norm, self.column, self.table],
            [self.head, self.head], [self.head_shape(LOW), self.head_shape(F32)], [], 5,
            q, numer, denom, total, norm, opened, table,
        )

    def pull_state(self, q, dy, y, total, opened, table):
        return self.call(
            pull_state_body, "mix_pull_state",
            [self.thin, self.head, self.head, self.column, self.table]
            + [pl.BlockSpec((d.shape[0], HV), lambda h: (0, h)) for d in dy],
            [self.pair, self.sum, self.norm],
            [shape((self.tokens, self.heads * 2 * HV), LOW)] + self.state_shapes, [], 5,
            q, y, total, opened, table, *dy,
        )

    def pull_inner(self, q, k, v, segc, segr, wide, total, norm, opened, table):
        return self.call(
            pull_inner_body, "mix_pull_inner",
            [self.thin, self.thin, self.head, self.column, self.row, self.pair, self.sum, self.norm, self.column, self.table],
            [self.thin, self.thin, self.head],
            [self.thin_shape(LOW), self.thin_shape(F32), self.head_shape(F32)],
            [self.acc, self.acc], 20, q, k, v, segc, segr, wide, total, norm, opened, table,
        )

    def pull_carry(self, k, v, tail, total, norm, dq, dk, dv, table):
        width = thin_width(self.heads) + self.heads * HV
        return self.call(
            pull_carry_body, "mix_pull_carry",
            [self.thin, self.head, self.column, self.sum, self.norm, self.thin, self.thin, self.head, self.table],
            self.full(self.tokens, width), shape((self.tokens, width), LOW), [self.acc], 6,
            k, v, tail, total, norm, dq, dk, dv, table,
        )


def outside(part, reverse):
    count, place = lax.axis_size("batch"), lax.axis_index("batch")
    total = list(part)
    before = [jnp.zeros_like(a) for a in part]
    bit = 1
    while bit < count:
        pairs = [(i, i ^ bit) for i in range(count)]
        low = total[0].astype(LOW)
        other = [lax.ppermute(low, "batch", pairs).astype(F32), lax.ppermute(total[1], "batch", pairs)]
        upper = (place & bit) != 0
        take = jnp.logical_not(upper) if reverse else upper
        before = [a + jnp.where(take, b, 0.0) for a, b in zip(before, other)]
        total = [a + b for a, b in zip(total, other)]
        bit *= 2
    return before


def padded(width):
    return -(-width // 16) * 16


def batch_orders():
    count = lax.axis_size("batch")
    bits = [1 << b for b in range(count.bit_length() - 1)]
    return bits[:1] + bits[1:], bits[:1] + bits[:0:-1]


def block_order():
    count = lax.axis_size("batch")
    first, second = batch_orders()
    relative, places = [], []
    for step in range(count):
        at = sum(bit for n, bit in enumerate(first) if step >> (len(first) - 1 - n) & 1)
        relative.append(at)
        places.append(sum(1 << (len(second) - 1 - n) for n, bit in enumerate(second) if at & bit))
    blocks = jnp.asarray(np.array(relative, np.int32)) ^ lax.axis_index("batch").astype(jnp.int32)
    return blocks, places


def cost(micros):
    return pl.CostEstimate(flops=int(micros * 1e9), bytes_accessed=1 << 20, transcendentals=0)


BIG = pltpu.CompilerParams(dimension_semantics=("arbitrary",), vmem_limit_bytes=56 * 1024 * 1024)


def grad_values(refs, groups):
    values = []
    for rows, parts in groups:
        value = None
        for _ in range(parts):
            term = nn(refs[1][...], refs[0][...])
            refs = refs[2:]
            value = term if value is None else value + term
        values.append(value)
    return values


def grad_body(blocks, swap, *refs, groups, summed):
    step = pl.program_id(0)
    places = (step, swap[0, step])
    middle = pl.num_programs(0) // 2
    sources = 2 * sum(parts for _, parts in groups)
    values = grad_values(list(refs[:sources]), groups)
    outs = refs[-4:]
    came = refs[sources:-4]
    at = 0
    for (rows, _), value in zip(groups, values):
        size = padded(rows // 2)
        for n in range(2):
            half = value[n * rows // 2 : (n + 1) * rows // 2]
            if size > rows // 2:
                half = jnp.concatenate([half, jnp.zeros((size - rows // 2, half.shape[1]), F32)], axis=0)
            span = slice(at, at + size)
            if summed:
                other = jnp.where(places[n] < middle, came[n][0, span, :], came[2 + n][0, span, :])
                half = half + other.astype(F32)
            half = half.astype(LOW)

            @pl.when(places[n] < middle)
            def _():
                outs[n][0, span, :] = half

            @pl.when(places[n] >= middle)
            def _():
                outs[2 + n][0, span, :] = half

        at += size


def grad_blocks(name, groups, far, came, micros):
    count = lax.axis_size("batch")
    split = count // 2
    width = groups[0][0][0].shape[1]
    columns = width // count
    blocks, places = block_order()
    base = split if far else 0
    in_specs, operands, kinds, rows = [], [], [], 0
    for parts in groups:
        for left, right in parts:
            in_specs.append(pl.BlockSpec((left.shape[0], columns), lambda s, b, w: (0, b[s])))
            in_specs.append(pl.BlockSpec(right.shape, lambda s, b, w: (0, 0)))
            operands += [left, right]
        kinds.append((parts[0][1].shape[0], len(parts)))
        rows += padded(parts[0][1].shape[0] // 2)
    size = (1, rows, columns)
    places = [p - base for p in places[base : base + split]]
    table, specs = [places], []
    for low in (0, split // 2):
        for order in (list(range(split)), places):
            uses = [(s, p - low) for s, p in enumerate(order) if low <= p < low + split // 2]
            table.append([([at for when, at in uses if when <= s] or [uses[0][1]])[-1] for s in range(split)])
            specs.append(pl.BlockSpec(size, lambda s, b, w, n=len(table) - 1: (w[n, s], 0, 0)))
    if came:
        in_specs += specs
        operands += came
    outs = pl.pallas_call(
        functools.partial(grad_body, groups=tuple(kinds), summed=bool(came)),
        grid_spec=pltpu.PrefetchScalarGridSpec(
            num_scalar_prefetch=2, grid=(split,), in_specs=in_specs, out_specs=specs
        ),
        out_shape=[shape((split // 2, rows, columns), LOW)] * 4,
        name=name,
        compiler_params=BIG,
        cost_estimate=cost(micros),
    )(blocks[base : base + split], jnp.asarray(np.array(table, np.int32)), *operands)
    return outs[:2], outs[2:]


def flip(value, bit):
    return lax.ppermute(value, "batch", [(i, i ^ bit) for i in range(lax.axis_size("batch"))])


def added(one, other):
    return (one.astype(F32) + other.astype(F32)).astype(LOW)


class Exchange:
    def __init__(self, far):
        self.orders = batch_orders()
        self.steps = len(self.orders[0])
        self.away, self.near, self.came = [list(f) for f in zip(*far)], None, [[], []]
        self.step = 0

    def get(self):
        return [self.away, self.near, self.came]

    def put(self, values):
        self.away, self.near, self.came = values

    def send(self, limit=None):
        n = self.step
        if n == 2 * self.steps:
            return
        for half, order in enumerate(self.orders):
            bit = order[n if n < self.steps else 2 * self.steps - 1 - n]
            first = len(self.came[half])
            last = len(self.away[half]) if limit is None else first + limit
            self.came[half] += [flip(a, bit) for a in self.away[half][first:last]]

    def begin(self, name, groups, micros):
        self.near, away = grad_blocks(name, groups, False, [c[n] for n in range(2) for c in self.came], micros)
        self.away, self.came, self.step = [[a] for a in away], [[], []], 1

    def take(self):
        n = self.step
        if n == 2 * self.steps:
            return
        self.step += 1
        if n == 0:
            self.near, away = [[added(b, c[m]) for b, c in zip(half, self.came)] for m, half in enumerate(self.near)]
            self.away = [[a] for a in away]
        elif n < self.steps:
            half = self.near[0].shape[0] // 2
            pairs = [(k, c[0]) for k, c in zip(self.near, self.came)]
            if half:
                self.away = [[added(k[half:], c[half:])] for k, c in pairs]
                self.near = [added(k[:half], c[:half]) for k, c in pairs]
            else:
                self.near = [added(k, c) for k, c in pairs]
                self.away = [[k] for k in self.near]
        else:
            self.away = [a + c for a, c in zip(self.away, self.came)]
        self.came = [[], []]

    def run(self):
        while self.step < 2 * self.steps:
            self.send()
            self.take()
        return self.away


def place_body(blocks, table, *refs, outs, count):
    step = pl.program_id(0)
    pieces = count
    if len(outs) == 1 and len(outs[0][2]) == 1 and not outs[0][2][0][3]:
        used = outs[0][1] // 2
        for n in range(2):
            for m in range(pieces):

                @pl.when(table[n, step] == m)
                def _():
                    refs[-1][n * used : (n + 1) * used, :] = refs[n * pieces + m][0, :used, :].astype(F32)

        return
    chosen = []
    for n in range(2):
        which = table[n, step]
        group = refs[n * pieces : (n + 1) * pieces]
        value = group[0][0]
        for m in range(1, pieces):
            value = jnp.where(which == m, group[m][0], value)
        chosen.append(value)
    results = refs[2 * pieces :]
    for start, rows, targets in outs:
        both = jnp.concatenate([c[start : start + rows // 2].astype(F32) for c in chosen], axis=0)
        for index, first, size, turned in targets:
            part = both[first : first + size]
            results[index][...] = part.T if turned else part


def place_blocks(name, pieces, outs, width, micros, part=None):
    count = lax.axis_size("batch")
    columns = width // count
    blocks, places = block_order()
    table = np.array([list(range(count)), places], np.int32)
    size = pieces[0][0].shape[1:]
    if part is not None:
        size = (padded(outs[0][0] // 2), size[1])
    piece = pl.BlockSpec((1,) + size, lambda s, b, t: (0, part or 0, 0), pipeline_mode=pl.Buffered(1))
    out_specs, out_shape, layout, start = [], [], [], 0
    for rows, targets in outs:
        listed = []
        for first, used, turned in targets:
            listed.append((len(out_shape), first, used, turned))
            if turned:
                out_specs.append(pl.BlockSpec((columns, used), lambda s, b, t: (b[s], 0)))
                out_shape.append(shape((width, used), F32))
            else:
                out_specs.append(pl.BlockSpec((used, columns), lambda s, b, t: (0, b[s])))
                out_shape.append(shape((used, width), F32))
        layout.append((start, rows, tuple(listed)))
        start += padded(rows // 2)
    return pl.pallas_call(
        functools.partial(place_body, outs=tuple(layout), count=count),
        grid_spec=pltpu.PrefetchScalarGridSpec(
            num_scalar_prefetch=2,
            grid=(count,),
            in_specs=[piece] * (2 * count),
            out_specs=out_specs,
        ),
        out_shape=out_shape,
        name=name,
        compiler_params=BIG,
        cost_estimate=cost(micros),
    )(blocks, jnp.asarray(table), *pieces[0], *pieces[1])


def line_sum(value):
    count = lax.axis_size("tensor")
    turned = [lax.ppermute(value, "tensor", [(i, (i + n) % count) for i in range(count)]) for n in range(1, count)]
    return [value] + turned


def batch_sum(value):
    value = value + flip(value, 1)
    return value + sum(flip(value, mask) for mask in range(2, lax.axis_size("batch"), 2))


def after(values, *others):
    return lax.optimization_barrier((values, others))[0]


def lock(*items):
    values = lax.optimization_barrier([i.get() if hasattr(i, "get") else i for i in items])
    for item, value in zip(items, values):
        if hasattr(item, "put"):
            item.put(value)
    return [v for i, v in zip(items, values) if not hasattr(i, "get")]


class Gather:
    def __init__(self, *parts):
        self.right, self.left = [list(parts)], [list(parts)]
        self.hops = 0
        self.least = lax.axis_size("tensor") - 1

    def get(self):
        return [self.right, self.left]

    def put(self, values):
        self.right, self.left = values

    def hop(self):
        count = lax.axis_size("tensor")
        self.hops += 1
        to_right = [(k, k + 1) for k in range(self.hops - 1, count - 1)]
        to_left = [(k, k - 1) for k in range(1, count - self.hops + 1)]
        self.right.append([lax.ppermute(a, "tensor", to_right) for a in self.right[-1]])
        self.left.append([lax.ppermute(a, "tensor", to_left) for a in self.left[-1]])

    def run(self):
        while self.hops < self.least:
            self.hop()
        return self

    def pieces(self, n=0):
        count, place = lax.axis_size("tensor"), lax.axis_index("tensor")
        return [self.right[0][n]] + [
            jnp.where(place + r < count, self.left[r][n], self.right[count - r][n]) for r in range(1, count)
        ]

    def total(self, n=0):
        return sum(a[n] for a in self.right) + sum(a[n] for a in self.left[1:])


class Scatter:
    def __init__(self, make):
        self.make, self.came, self.made = make, [], {}
        self.left = lax.axis_size("tensor") - 1
        self.prepare()

    def prepare(self):
        count = lax.axis_size("tensor")
        for r in (self.left, (count - self.left) % count):
            if r not in self.made:
                self.made[r] = self.make(r)

    def get(self):
        return [self.came, self.made]

    def put(self, values):
        self.came, self.made = values

    def hop(self):
        count = lax.axis_size("tensor")
        sends = [self.made[self.left], self.made[count - self.left]]
        if self.came:
            sends = [s + c.astype(F32) for s, c in zip(sends, self.came)]
        sends = [s.astype(LOW) for s in sends]
        self.came = [
            lax.ppermute(sends[0], "tensor", [(k, k + 1) for k in range(0, count - self.left)]),
            lax.ppermute(sends[1], "tensor", [(k, k - 1) for k in range(self.left, count)]),
        ]
        self.left -= 1
        self.prepare()

    def result(self):
        return self.made[0] + self.came[0].astype(F32) + self.came[1].astype(F32)


def copy_body(turn, in_ref, out_ref):
    out_ref[...] = in_ref[...]


def straighten(array):
    count = lax.axis_size("tensor")
    turn = (jnp.arange(count, dtype=jnp.int32) - lax.axis_index("tensor")) % count
    size = (array.shape[0], array.shape[1] // count)
    return pl.pallas_call(
        copy_body,
        grid_spec=pltpu.PrefetchScalarGridSpec(
            num_scalar_prefetch=1,
            grid=(count,),
            in_specs=[pl.BlockSpec(size, lambda n, t: (0, t[n]))],
            out_specs=pl.BlockSpec(size, lambda n, t: (0, n)),
        ),
        out_shape=shape(array.shape, array.dtype),
        name="straighten",
        compiler_params=BIG,
        cost_estimate=cost(4),
    )(turn, array)


def widen(part):
    return lax.all_gather(part, "tensor", axis=1, tiled=True)


def narrow(part):
    return lax.psum_scatter(part, "tensor", scatter_dimension=1, tiled=True)


def project(left, right):
    return jnp.dot(left, right, preferred_element_type=F32)


def project_back(left, right):
    return jnp.einsum("ti,ji->tj", left, right, preferred_element_type=F32)


def across(left, right):
    return jnp.einsum("it,ij->tj", left, right, preferred_element_type=F32)


def row_sum(values):
    return jnp.sum(values, axis=1, keepdims=True)


def local(
    tokens, doc_lengths, norm1_gain, w_query, w_key, w_value, w_out, norm2_gain, w_gate, w_up, w_down, cotangent,
):
    count, slice_width = tokens.shape
    heads = w_value.shape[1] // HV
    lanes = heads * FEAT
    width = w_query.shape[0]
    begin_here = lax.axis_index("batch") * count
    position = begin_here + jnp.arange(count, dtype=jnp.int32)
    doc_index = jnp.arange(doc_lengths.shape[0], dtype=jnp.int32)
    doc_begins = jnp.sum(jnp.where(doc_index[None, :] < doc_index[:, None], doc_lengths[None, :], 0), axis=1)
    segment = jnp.sum((position[:, None] >= doc_begins[None, :]).astype(jnp.int32), axis=1) - 1
    head_seg, tail_seg = segment[0], segment[-1]
    first_begin = jnp.sum(jnp.where(doc_index == head_seg, doc_begins, 0))
    opened = ((segment == head_seg) & (first_begin < begin_here)).astype(F32)[:, None]
    tail = (segment == tail_seg).astype(F32)[:, None]
    segc, segr = segment[:, None], segment[None, :]
    table = jnp.asarray(feature_table())
    mixer = Mixer(count, heads)

    size, place = lax.axis_size("tensor"), lax.axis_index("tensor")
    half = count // 2
    cut = lambda a: (a[:half], a[half:])
    join = lambda *parts: jnp.concatenate(parts, axis=0)
    c_a, c_b = cut(cotangent)
    w_gate, w_up = w_gate.T, w_up.T
    units = w_gate.shape[0]

    x_full = widen(tokens)
    gains = lax.all_gather(jnp.stack([norm1_gain, norm2_gain]), "tensor", axis=1, tiled=True)
    thin = thin_width(heads)
    w_mix = [w_query, w_key, jnp.zeros((width, thin - 2 * lanes), LOW), w_value]
    w_mix = jnp.concatenate([w for w in w_mix if w.shape[1]], axis=1)
    gather_c = Gather(cotangent)
    x_full, gains, w_mix = lock(x_full, gains, w_mix, gather_c)

    gather_c.hop()
    x_wide = x_full.astype(F32)
    scale_one = lax.rsqrt(row_sum(x_wide * x_wide) / width + EPSILON)
    normed_one = (x_wide * scale_one * gains[0:1]).astype(LOW)
    pair = project(normed_one, w_mix[:, :thin]).astype(LOW)
    q, k, v = pair[:, :lanes], pair[:, lanes : 2 * lanes], project(normed_one, w_value).astype(LOW)
    carry = mixer.state(k, v, tail, table)
    prior = outside(carry, False)
    numer, denom = mixer.inner(q, k, v, segc, segr)
    y, total = mixer.merge(q, numer, denom, *prior, opened, table)
    columns = lambda w, r: lax.dynamic_slice_in_dim(w, ((place + r) % size) * slice_width, slice_width, 1)
    scatter = Scatter(lambda r: project(y, columns(w_out, r)))
    y, total = lock(y, total, gather_c, scatter)
    while scatter.left:
        scatter.hop()
        if gather_c.hops < gather_c.least:
            gather_c.hop()
        lock(scatter, gather_c)
    hidden = tokens.astype(F32) + scatter.result()
    hidden_a, hidden_b = cut(hidden)
    low_a, low_b = cut(hidden.astype(LOW))
    hidden_a, hidden_b, low_a, low_b = lock(hidden_a, hidden_b, low_a, low_b)

    wide_a = widen(low_a)
    c_full = straighten(jnp.concatenate(gather_c.pieces(), axis=1))
    ca_full, cb_full = cut(c_full)
    dinner_a = project_back(w_down, ca_full)
    dinner_b = project_back(w_down, cb_full)
    wide_a, c_full, dinner_a, dinner_b = lock(wide_a, c_full, dinner_a, dinner_b)
    ca_full, cb_full = cut(c_full)

    def feed(wide, dinner):
        wide32 = wide.astype(F32)
        scale = lax.rsqrt(row_sum(wide32 * wide32) / width + EPSILON)
        normed = (wide32 * scale * gains[1:2]).astype(LOW)
        gate = project_back(w_gate, normed)
        up = project_back(w_up, normed)
        sig = jax.nn.sigmoid(gate)
        silu = gate * sig
        inner = (silu * up).astype(LOW)
        dgate = (dinner * up * sig * (1.0 + gate * (1.0 - sig))).astype(LOW)
        dup = (dinner * silu).astype(LOW)
        pulled = (across(dgate, w_gate) + across(dup, w_up)).astype(LOW)
        return scale, normed, inner, dgate, dup, pulled

    wide_b = widen(low_b)
    wide_b, (scale_a, normed_a, inner_a, dgate_a, dup_a, part) = lock(wide_b, feed(wide_a, dinner_a))

    back_a = narrow(part)
    scale_b, normed_b, inner_b, dgate_b, dup_b, part = feed(wide_b, dinner_b)
    groups = [
        [(normed_a, dgate_a), (normed_b, dgate_b)],
        [(normed_a, dup_a), (normed_b, dup_b)],
        [(ca_full, inner_a), (cb_full, inner_b)],
    ]
    ffn = Exchange(grad_blocks("grad_ffn_far", groups, True, None, 16))
    back_a, scale_b, normed_b, inner_b, dgate_b, dup_b, part = lock(
        back_a, scale_b, normed_b, inner_b, dgate_b, dup_b, part, ffn
    )

    def turned(c, scale, back, hidden):
        scaled = scale * back.astype(F32)
        return c.astype(F32) + norm2_gain[None, :] * scaled, jnp.sum(scaled * hidden, axis=0)

    def spread(u, c, wide, scale, local_u, hidden):
        u, wide = u.astype(F32), wide.astype(F32)
        dot = row_sum((u - c.astype(F32)) * wide) * scale * scale / width
        dh = (u - wide * dot).astype(LOW)
        return dh, local_u - hidden * dot, project_back(dh, w_out)

    back_b = narrow(part)
    u_a, gain_a = turned(c_a, scale_a, back_a, hidden_a)
    low_a = u_a.astype(LOW)
    groups = [
        [(normed_a, dgate_a), (normed_b, dgate_b)],
        [(normed_a, dup_a), (normed_b, dup_b)],
        [(ca_full, inner_a), (cb_full, inner_b)],
    ]
    ffn.send()
    ffn.near = grad_blocks("grad_ffn_near", groups, False, None, 16)
    ffn.take()
    ffn.send()
    back_b, u_a, gain_a, low_a, ffn.away, ffn.near = lock(back_b, u_a, gain_a, low_a, ffn.away, ffn.near)

    wide_u = widen(low_a)
    u_b, gain_b = turned(c_b, scale_b, back_b, hidden_b)
    low_b = u_b.astype(LOW)
    parts = [across(m, w_down).astype(LOW) for m in (inner_a, inner_b)]
    y_turned = [p.T for p in cut(y)]
    wide_u, u_b, gain_b, low_b, parts, y_turned = lock(wide_u, u_b, gain_b, low_b, parts, y_turned, ffn)

    wide_v = widen(low_b)
    ffn.take()
    ffn.send()
    dh_a, grad_hidden_a, dy_a = spread(wide_u, ca_full, wide_a, scale_a, u_a, hidden_a)
    ffn.take()
    ffn.send()
    wide_v, dh_a, grad_hidden_a, dy_a, ffn.away, ffn.near = lock(
        wide_v, dh_a, grad_hidden_a, dy_a, ffn.away, ffn.near
    )

    down = narrow(join(*parts))
    dh_b, grad_hidden_b, dy_b = spread(wide_v, cb_full, wide_b, scale_b, u_b, hidden_b)
    wide, dsum, dnorm = mixer.pull_state(q, [dy_a, dy_b], y, total, opened, table)
    ffn.take()
    ffn.send(1)
    wide, dsum, dnorm = lock(wide, dsum, dnorm, ffn)
    following = outside([dsum, dnorm], True)
    dq, dk, dv = mixer.pull_inner(q, k, v, segc, segr, wide, *prior, opened, table)
    following, dq, dk, dv = lock(following, dq, dk, dv, ffn)
    ffn.send()
    dmix = mixer.pull_carry(k, v, tail, *following, dq, dk, dv, table)
    part = project_back(dmix, w_mix).astype(LOW)
    dot = row_sum(dmix[:, :thin].astype(F32) * pair.astype(F32))
    dot = dot + row_sum(dmix[:, thin:].astype(F32) * v.astype(F32))
    dots = line_sum(dot.reshape(count // 128, 128))
    down, part, dmix, dh_b, grad_hidden_b, dots = lock(down, part, dmix, dh_b, grad_hidden_b, dots, ffn)

    back = narrow(part)
    groups = [[(normed_one, dmix.T)], [(dh_a, y_turned[0]), (dh_b, y_turned[1])]]
    ffn.take()
    ffn.send()
    mix = Exchange(grad_blocks("grad_mix_far", groups, True, None, 5))
    mix.send()
    mix.begin("grad_mix_near", groups, 5)
    lock(mix, ffn)
    mix.send()
    ffn.take()
    final = ffn.run()

    def ffn_weight(n):
        return place_blocks(f"place_ffn_{n}", final, [(units, [(0, units, False)])], width, 7, n)[0]

    grad_w_gate = lock(mix, ffn_weight(0))[0]
    mix.take()
    mix.send()
    grad_w_up = lock(mix, ffn_weight(1))[0]
    mix.take()
    mix.send()
    output = (join(hidden_a, hidden_b) + down.astype(F32)).astype(LOW)
    output = lock(mix, output)[0]
    mix.take()
    mix.send()
    grad_w_down = lock(mix, ffn_weight(2))[0]
    mix.take()
    mix.send()
    back = lock(back, mix)[0]
    inputs, back = tokens.astype(F32), back.astype(F32)
    gain_one = jnp.sum(back * inputs * scale_one, axis=0)
    gain_grads = batch_sum(jnp.stack([gain_one, gain_a + gain_b]))
    grad_tokens = (
        join(grad_hidden_a, grad_hidden_b)
        + scale_one * norm1_gain[None, :] * back
        - inputs * (scale_one * scale_one * sum(dots).reshape(count, 1) / width)
    )
    values = heads * HV
    grad_w_query, grad_w_key, grad_w_value, grad_w_out = place_blocks(
        "place_mix",
        mix.run(),
        [
            (thin + values, [(0, lanes, False), (lanes, lanes, False), (thin, values, True)]),
            (values, [(0, values, False)]),
        ],
        width,
        5,
    )
    return (
        output,
        grad_tokens,
        gain_grads[0],
        grad_w_query.T,
        grad_w_key.T,
        grad_w_value,
        grad_w_out,
        gain_grads[1],
        grad_w_gate.T,
        grad_w_up.T,
        grad_w_down,
    )


def solution(mesh):
    rows, cols = P("tensor", None), P(None, "tensor")
    both, one = P("batch", "tensor"), P("tensor")
    in_specs = (both, P(), one, cols, cols, cols, rows, one, cols, cols, rows, both)
    out_specs = (both, both, one, cols, cols, cols, rows, one, cols, cols, rows)
    return jax.shard_map(local, mesh=mesh, in_specs=in_specs, out_specs=out_specs, check_vma=False)
```
